256 devices in a mesh: pipe: 4 (over y), expert: 16 (over z, core), dp: 4 (over x).
Axes of the slice: x: 4, y: 4, z: 8, core: 2. Of those that a mesh axis runs over, the one named last changes fastest.
Arguments:
- normed: bfloat16 [4, 4, 3072, 4096], P('pipe', None, ('expert', 'dp')), may hold values from -1.5 to 1.5
- saved_out: bfloat16 [4, 4, 3072, 2, 4096], P('pipe', None, ('expert', 'dp')), may hold values from -0.59765625 to 0.59765625
- expert_grads: bfloat16 [4, 4, 4, 16, 16, 9, 4096], P('pipe', None, 'dp', 'expert'), may hold values from -24 to 24
- routes: int32 [4, 4, 3072, 2], P('pipe', None, ('expert', 'dp')), may hold values from 0 to 15, all different within a row; in each aligned block of 48 rows (0 to 47, 48 to 95, ..., all dimensions but the last counted through in order) at most 9 rows name the same one
- router_weight: bfloat16 [4, 4096, 16], P('pipe'), may hold values from -0.375 to 0.375
- upstream: bfloat16 [4, 3072, 4096], P(None, ('expert', 'dp')), may hold values from -6 to 6
Outputs:
- grad_input: bfloat16 [4, 4, 3072, 4096], P('pipe', None, ('expert', 'dp'))
- router_grad: float32 [4, 4096, 16], P('pipe')
The draws below stay inside these ranges and needn't reach their ends.
Inputs may be any that keep to these rules, and one draw needn't show every extreme that they name: `routes`: the two experts of a row differ. Within the 48 rows of one device for one section and micro-batch no expert is named more than 9 times, a bound that some expert reaches in some of these blocks.
All inputs are finite; a program needn't handle non-finite values.
Results may differ from the reference program's by a relative error of at most 0.007.
Values may be sent and summed in bfloat16 or wider, within the bound.
No kernel may reach another device: no remote copies, remote signals or barrier semaphores. Data moves between devices by JAX's collectives and lax.ppermute only.
A program may use at most 128 MiB of HBM per device.

```python
import math
import jax
import jax.numpy as jnp
import numpy as np

D = 4096
TOP = 2
MICRO = 4
ROWS = 48
EXPERTS = 16
CAP = 9
TOK_MB = 3072
N_PIPE = 4
N_EXPERT = 16
N_DP = 4


def level_of(key, shape, split, least, high):
    def one(dim, blocks):
        steps = jax.random.uniform(jax.random.fold_in(jax.random.fold_in(key, 6), dim), (blocks,), jnp.float32, least / len(split), high / len(split))
        return jnp.repeat(jnp.exp(steps), shape[dim] // blocks).reshape((-1,) + (1,) * (len(shape) - dim - 1))

    gain = one(*split[0])
    for cut in split[1:]:
        gain = gain * one(*cut)
    return gain


def shared_out(stream_key, own, number, rows, count, top, reach, skew):
    order = jax.random.permutation(stream_key, count)
    heavy_load, ordinary = shares(count, rows * top, reach, skew, True), shares(count, rows * top, reach, skew, False)
    places = jnp.arange(count)

    def named(tallies, turn):
        used = int((tallies > 0).sum())
        fixed = max(1, used // 4)
        shifted = fixed + (places - fixed + turn * (used - fixed)) % max(1, count - fixed)
        return jnp.zeros((count,), jnp.int32).at[order[jnp.where(places < fixed, places, shifted)]].set(jnp.asarray(tallies, jnp.int32))

    tallies = jnp.where(number % 4 == 0, named(heavy_load, number // 4), named(ordinary, number - number // 4 - 1))
    mixed = jax.random.permutation(jax.random.fold_in(own, 3), count)
    source_of, sink = mixed[0:count // 2 * 2:2], mixed[1:count // 2 * 2:2]
    margin = jnp.minimum(tallies[source_of] - 1, reach - tallies[sink]) // 2
    margin = jnp.where((source_of == order[0]) | (sink == order[0]) | (tallies[sink] == 0), 0, jnp.maximum(margin, 0))
    shifted = jax.random.randint(jax.random.fold_in(own, 4), (count // 2,), 0, 1 << 20) % (margin + 1)
    tallies = tallies.at[source_of].add(-shifted).at[sink].add(shifted)
    labels = jnp.searchsorted(jnp.cumsum(tallies), jnp.arange(rows * top), side="right").astype(jnp.int32)
    listing = labels.reshape(top, rows).T
    listing = listing[jax.random.permutation(jax.random.fold_in(own, 1), rows)]
    turn = jax.random.randint(jax.random.fold_in(own, 2), (rows, 1), 0, top)
    return jnp.take_along_axis(listing, (jnp.arange(top)[None, :] + turn) % top, axis=1)


def shares(count, total, limit, slope, full):
    portions = [(1 << 20) // math.isqrt(rank ** slope) + 1 for rank in range(1, count + 1)]
    largest = limit if full else min(limit, max(-(-total // count), total * portions[0] // sum(portions)))
    least = 1 if total - largest >= count - 1 else 0
    counts, surplus = [largest] + [least] * (count - 1), total - largest - least * (count - 1)
    while surplus > 0:
        free = [i for i in range(1, count) if counts[i] < largest] or [i for i in range(1, count) if counts[i] < limit]
        whole, budget = sum([portions[i] for i in free]), surplus
        for i in free:
            more = min(limit - counts[i], max(1, budget * portions[i] // whole), surplus)
            counts[i] = counts[i] + more
            surplus = surplus - more
    return np.array(counts)


def gaussian(rng, shape, deviation, reach, split=(), kind=jnp.bfloat16):
    array = jax.random.normal(rng, shape, jnp.float32) * deviation
    if len(split) > 0:
        array = level_of(rng, shape, split, -0.22, 0.18) * array
    return jnp.clip(array, min=-reach, max=reach).astype(kind)


def setup_inputs(seed: int = 0) -> dict:
    keys = jax.random.split(jax.random.key(seed), 7)
    normed = gaussian(keys[0], (N_PIPE, MICRO, TOK_MB, D), 0.25, 1.5, ((0, 4), (2, 64)))
    saved_out = gaussian(keys[1], (N_PIPE, MICRO, TOK_MB, TOP, D), 0.1, 0.59765625, ((0, 4), (2, 64)))
    expert_grads = gaussian(keys[2], (N_PIPE, MICRO, N_DP, EXPERTS, N_EXPERT, CAP, D), 4.0, 24.0, ((0, 4), (2, 4), (3, 16)))
    routes_keys = jax.random.split(jax.random.fold_in(keys[3], 1), N_PIPE * MICRO * TOK_MB // ROWS)
    routes_turns = jax.random.permutation(jax.random.fold_in(keys[3], 3), N_PIPE * MICRO * TOK_MB // ROWS)
    routes = jax.vmap(lambda own, number: shared_out(jax.random.fold_in(keys[3], 2), own, number, ROWS, EXPERTS, TOP, CAP, 2))(routes_keys, routes_turns).reshape((N_PIPE, MICRO, TOK_MB, TOP))
    router_weight = gaussian(keys[4], (N_PIPE, D, EXPERTS), (D // 16) ** -0.5, 0.375, ((0, 4),))
    upstream = gaussian(keys[5], (MICRO, TOK_MB, D), 1.0, 6.0, ((1, 64),))
    return {"normed": normed, "saved_out": saved_out, "expert_grads": expert_grads, "routes": routes, "router_weight": router_weight, "upstream": upstream}


def slot_index(flat, experts, capacity):
    onehot = (flat[..., None] == jnp.arange(experts, dtype=jnp.int32)).astype(jnp.int32)
    before = jnp.cumsum(onehot, axis=-2) - onehot
    position = jnp.sum(before * onehot, axis=-1).astype(jnp.int32)
    return (flat * capacity + position).astype(jnp.int32)


def take_rows(buffer, index):
    return buffer[index]


def reference(normed, saved_out, expert_grads, routes, router_weight, upstream):
    groups = N_EXPERT * N_DP
    grads = [None] * N_PIPE
    weight_grads = [None] * N_PIPE
    incoming = upstream
    for section_num in reversed(range(N_PIPE)):
        buffer = jnp.transpose(expert_grads[section_num], (0, 3, 1, 2, 4, 5)).reshape(MICRO, groups, EXPERTS * CAP, D)
        flat = routes[section_num].reshape(MICRO, groups, ROWS * TOP)
        index = slot_index(flat, EXPERTS, CAP)
        back = jax.vmap(jax.vmap(take_rows))(buffer, index).reshape(MICRO, TOK_MB, TOP, D).astype(jnp.float32)
        router_w = router_weight[section_num]
        rows_2d = normed[section_num].reshape(MICRO * TOK_MB, D)
        logits = jnp.dot(rows_2d, router_w, preferred_element_type=jnp.float32).reshape(MICRO, TOK_MB, EXPERTS)
        expl = jnp.exp(logits)
        probs = expl / jnp.sum(expl, axis=-1, keepdims=True)
        chosen = (routes[section_num][..., None] == jnp.arange(EXPERTS, dtype=jnp.int32)).astype(jnp.float32)
        gates = jnp.einsum("mtke,mte->mtk", chosen, probs)
        dot_grads = jnp.einsum("mtd,mtkd->mtk", incoming.astype(jnp.float32), saved_out[section_num].astype(jnp.float32))
        weighted = dot_grads * gates
        dense_f = jnp.einsum("mtke,mtk->mte", chosen, weighted) - probs * jnp.sum(weighted, axis=-1)[..., None]
        dense = dense_f.astype(jnp.bfloat16)
        dense_2d = dense.reshape(MICRO * TOK_MB, EXPERTS)
        router_term = jnp.dot(dense_2d, router_w.T, preferred_element_type=jnp.float32).reshape(MICRO, TOK_MB, D)
        total = incoming.astype(jnp.float32) + gates[..., 0, None] * back[:, :, 0] + gates[..., 1, None] * back[:, :, 1] + router_term
        new_grad = total.astype(jnp.bfloat16)
        weight_grads[section_num] = jnp.dot(rows_2d.T, dense_2d, preferred_element_type=jnp.float32) / MICRO
        grads[section_num] = new_grad
        incoming = new_grad
    return jnp.stack(grads), jnp.stack(weight_grads)
```

```python
import jax
import jax.numpy as jnp
from jax import lax
from jax.experimental import pallas as pl
from jax.experimental.pallas import tpu as pltpu
from jax.sharding import PartitionSpec as P

F32 = jnp.float32
BF16 = jnp.bfloat16
NT = (((1,), (1,)), ((), ()))
TN = (((0,), (0,)), ((), ()))


def params(mib):
    return pltpu.CompilerParams(vmem_limit_bytes=mib << 20)


def pack_kernel(main_ref, last_ref, out_ref):
    unit = pl.program_id(0)
    units = pl.num_programs(0)
    micro, _, dests, width = last_ref.shape
    half = width // 2

    @pl.when(unit < units - 1)
    def _():
        slots = main_ref.shape[1]
        n = slots * dests
        out_row = lax.broadcasted_iota(jnp.int32, (n, n), 0)
        in_row = lax.broadcasted_iota(jnp.int32, (n, n), 1)
        swap = (in_row == (out_row % slots) * dests + out_row // slots).astype(BF16)
        rows = main_ref[0].reshape(n, half)
        moved = jnp.dot(swap, rows, preferred_element_type=F32)
        out_ref[...] = moved.reshape(dests, slots, half).astype(BF16)

    @pl.when(unit == units - 1)
    def _():
        n_in = micro * dests
        n_out = 2 * micro * dests
        out_row = lax.broadcasted_iota(jnp.int32, (n_out, n_in), 0)
        in_row = lax.broadcasted_iota(jnp.int32, (n_out, n_in), 1)
        within = out_row % (2 * micro)
        source = (within % micro) * dests + out_row // (2 * micro)
        total = jnp.zeros((n_out, half), F32)
        for h in range(2):
            pick = ((in_row == source) & (within // micro == h)).astype(BF16)
            rows = last_ref[:, 0, :, h * half : (h + 1) * half].reshape(n_in, half)
            total = total + jnp.dot(pick, rows, preferred_element_type=F32)
        out_ref[...] = total.reshape(dests, 2 * micro, half).astype(BF16)


def pack(grads):
    micro, cap, dests, width = grads.shape
    half = width // 2
    units = 2 * micro + 1
    last_unit = 2 * micro - 1
    return pl.pallas_call(
        pack_kernel,
        grid=(units,),
        in_specs=[
            pl.BlockSpec(
                (1, cap - 1, dests, half),
                lambda u: (jnp.minimum(u, last_unit) // 2, 0, 0, jnp.minimum(u, last_unit) % 2),
            ),
            pl.BlockSpec((micro, 1, dests, width), lambda u: (0, cap - 1, 0, 0)),
        ],
        out_specs=pl.BlockSpec((dests, 8, half), lambda u: (0, u, 0)),
        out_shape=jax.ShapeDtypeStruct((dests, units * 8, half), BF16),
        compiler_params=params(40),
        name="pack_slots",
    )(grads, grads)


def gate_kernel(normed_ref, w_ref, routes_ref, v_ref, gate_ref, place_ref):
    m = pl.program_id(0)
    logits = lax.dot_general(w_ref[...], normed_ref[0], NT, preferred_element_type=F32)
    experts, rows = logits.shape
    expl = jnp.exp(logits)
    probs = expl / jnp.sum(expl, axis=0, keepdims=True)
    ids = lax.broadcasted_iota(jnp.int32, (experts, rows), 0)
    first = lax.broadcasted_iota(jnp.int32, (rows, rows), 0)
    second = lax.broadcasted_iota(jnp.int32, (rows, rows), 1)
    earlier = (first < second).astype(BF16)
    named = [ids == routes_ref[0, k : k + 1, :] for k in range(2)]
    both = jnp.where(named[0] | named[1], 1.0, 0.0).astype(BF16)
    before = jnp.dot(both, earlier, preferred_element_type=F32)
    for k in range(2):
        gate = jnp.sum(jnp.where(named[k], probs, 0.0), axis=0, keepdims=True)
        v_ref[0, k * experts : (k + 1) * experts, :] = gate * (jnp.where(named[k], 1.0, 0.0) - probs)
        gate_ref[0, k : k + 1, :] = gate
        slot = jnp.sum(jnp.where(named[k], before, 0.0), axis=0, keepdims=True).astype(jnp.int32)
        start = routes_ref[0, k : k + 1, :] * 8
        place_ref[0, k : k + 1, :] = jnp.where(slot < 8, start + slot, experts * 8 + start + m)


def gates_of(normed, w, routes):
    micro, rows, width = normed.shape
    experts = w.shape[0]
    return pl.pallas_call(
        gate_kernel,
        grid=(micro,),
        in_specs=[
            pl.BlockSpec((1, rows, width), lambda m: (m, 0, 0)),
            pl.BlockSpec((experts, width), lambda m: (0, 0)),
            pl.BlockSpec((1, 2, rows), lambda m: (m, 0, 0)),
        ],
        out_specs=[
            pl.BlockSpec((1, 2 * experts, rows), lambda m: (m, 0, 0)),
            pl.BlockSpec((1, 2, rows), lambda m: (m, 0, 0)),
            pl.BlockSpec((1, 2, rows), lambda m: (m, 0, 0)),
        ],
        out_shape=[
            jax.ShapeDtypeStruct((micro, 2 * experts, rows), F32),
            jax.ShapeDtypeStruct((micro, 2, rows), F32),
            jax.ShapeDtypeStruct((micro, 2, rows), jnp.int32),
        ],
        compiler_params=params(32),
        name="gates",
    )(normed, w, routes)


def pairs(sections):
    found = []
    for s in range(sections - 1):
        for k in range(2):
            for upper in range(s + 1, sections):
                for k2 in range(2):
                    found.append((s, k, upper, k2))
    return {key: row for row, key in enumerate(found)}


def couple_kernel(p_ref, saved_ref, w_ref, v_ref, out_ref):
    p = p_ref[0]
    sections, experts, _ = w_ref.shape
    for s in range(sections - 1):
        j = (s - p) & (sections - 1)
        for k in range(2):
            saved = saved_ref[j, k, 0]
            for upper in range(s + 1, sections):
                j2 = (upper - p) & (sections - 1)
                part = lax.dot_general(w_ref[j2], saved, NT, preferred_element_type=F32)
                for k2 in range(2):
                    row = pairs(sections)[(s, k, upper, k2)]
                    v = v_ref[j2, 0, k2 * experts : (k2 + 1) * experts, :]
                    out_ref[0, row : row + 1, :] = jnp.sum(part * v, axis=0, keepdims=True)


def coupling(p, saved, w, v):
    sections, _, micro, rows, quarter = saved.shape
    experts = w.shape[1]
    n = len(pairs(sections))
    return pl.pallas_call(
        couple_kernel,
        grid_spec=pltpu.PrefetchScalarGridSpec(
            num_scalar_prefetch=1,
            grid=(micro,),
            in_specs=[
                pl.BlockSpec((sections, 2, 1, rows, quarter), lambda m, p: (0, 0, m, 0, 0)),
                pl.BlockSpec((sections, experts, quarter), lambda m, p: (0, 0, 0)),
                pl.BlockSpec((sections, 1, 2 * experts, rows), lambda m, p: (0, m, 0, 0)),
            ],
            out_specs=pl.BlockSpec((1, n, rows), lambda m, p: (m, 0, 0)),
        ),
        out_shape=jax.ShapeDtypeStruct((micro, n, rows), F32),
        compiler_params=params(32),
        name="coupling",
    )(p, saved, w, v)


def combine_kernel(main_ref, last_ref, gate_ref, place_ref, out_ref):
    h = pl.program_id(0)
    experts, _, half = main_ref.shape
    lanes = gate_ref.shape[2]
    rows = lanes // 2
    n = experts * 8
    micro = pl.num_programs(1)
    index = lax.broadcasted_iota(jnp.int32, (2 * n, lanes), 0)
    pick = jnp.zeros((2 * n, lanes), F32)
    for k in range(2):
        place = place_ref[0, k : k + 1, :]
        place = place + jnp.where(place >= n, h * micro, 0)
        pick = pick + jnp.where(index == place, gate_ref[0, k : k + 1, :], 0.0)
    high = pick.astype(BF16)
    low = (pick - high.astype(F32)).astype(BF16)
    is_low = lax.broadcasted_iota(jnp.int32, (2 * n, lanes), 1) >= rows
    pick = jnp.where(is_low, low.astype(F32), high.astype(F32)).astype(BF16)
    both = lax.dot_general(
        pick[:n], main_ref[...].reshape(n, half), TN, preferred_element_type=F32
    ) + lax.dot_general(pick[n:], last_ref[...].reshape(n, half), TN, preferred_element_type=F32)
    total = (both[:rows] + both[rows:]).astype(BF16)
    out_ref[0, 0] = total[:, : half // 2]
    out_ref[1, 0] = total[:, half // 2 :]


def combine(received, gates, places):
    experts, packed, half = received.shape
    units = packed // 8
    micro = (units - 1) // 2
    lanes = gates.shape[2]
    rows = lanes // 2
    return pl.pallas_call(
        combine_kernel,
        grid=(2, micro),
        in_specs=[
            pl.BlockSpec((experts, 8, half), lambda h, m: (0, 2 * m + h, 0)),
            pl.BlockSpec((experts, 8, half), lambda h, m: (0, units - 1, 0)),
            pl.BlockSpec((1, 2, lanes), lambda h, m: (m, 0, 0)),
            pl.BlockSpec((1, 2, lanes), lambda h, m: (m, 0, 0)),
        ],
        out_specs=pl.BlockSpec((2, 1, rows, half // 2), lambda h, m: (h, m, 0, 0)),
        out_shape=jax.ShapeDtypeStruct((4, micro, rows, half // 2), BF16),
        compiler_params=params(40),
        name="combine",
    )(received, received, gates, places)


def dots_kernel(p_ref, up_ref, back_ref, saved_ref, out_ref):
    p = p_ref[0]
    sections, _, rows, quarter = back_ref.shape
    base = up_ref[0].astype(F32)
    ones = jnp.ones((8, 128), F32)
    for s in reversed(range(sections)):
        j = (s - p) & (sections - 1)
        for k in range(2):
            product = base * saved_ref[j, k, 0].astype(F32)
            lane = product[:, :128]
            for c in range(1, quarter // 128):
                lane = lane + product[:, c * 128 : (c + 1) * 128]
            row = lax.dot_general(
                ones, lane, NT, precision=lax.Precision.HIGHEST, preferred_element_type=F32
            )
            out_ref[0, 2 * s + k : 2 * s + k + 1, :] = row[:1]
        if s > 0:
            base = base + back_ref[s, 0].astype(F32)


def partial_dots(p, upstream, back, saved):
    sections, micro, rows, quarter = back.shape
    return pl.pallas_call(
        dots_kernel,
        grid_spec=pltpu.PrefetchScalarGridSpec(
            num_scalar_prefetch=1,
            grid=(micro,),
            in_specs=[
                pl.BlockSpec((1, rows, quarter), lambda m, p: (m, 0, p[0])),
                pl.BlockSpec((sections, 1, rows, quarter), lambda m, p: (0, m, 0, 0)),
                pl.BlockSpec((sections, 2, 1, rows, quarter), lambda m, p: (0, 0, m, 0, 0)),
            ],
            out_specs=pl.BlockSpec((1, 2 * sections, rows), lambda m, p: (m, 0, 0)),
        ),
        out_shape=jax.ShapeDtypeStruct((micro, 2 * sections, rows), F32),
        compiler_params=params(32),
        name="dots",
    )(p, upstream, back, saved)


def dense_kernel(p_ref, dots_ref, couple_ref, v_ref, normed_ref, dense_ref, part_ref):
    p = p_ref[0]
    sections, micro, _, rows = dots_ref.shape
    experts = v_ref.shape[2] // 2
    width = normed_ref.shape[2]
    table = pairs(sections)
    total = jnp.zeros((experts, width), F32)
    for m in range(micro):
        given = dots_ref[0, m]
        for source in range(1, sections):
            given = given + dots_ref[source, m]
        links = couple_ref[m]
        dots = {}
        own = jnp.zeros((experts, rows), F32)
        for s in reversed(range(sections)):
            j = (s - p) & (sections - 1)
            dense = jnp.zeros((experts, rows), F32)
            for k in range(2):
                value = given[2 * s + k : 2 * s + k + 1, :]
                for upper in range(s + 1, sections):
                    for k2 in range(2):
                        row = table[(s, k, upper, k2)]
                        value = value + links[row : row + 1, :] * dots[(upper, k2)]
                dots[(s, k)] = value
                dense = dense + value * v_ref[j, m, k * experts : (k + 1) * experts, :]
            dense_ref[m, s * experts : (s + 1) * experts, :] = dense.astype(BF16)
            own = jnp.where(p == s, dense, own)
        total = total + jnp.dot(own.astype(BF16), normed_ref[m], preferred_element_type=F32)
    total = total * (1.0 / micro)
    cols = width // 128
    for r in range(experts // 8):
        for c in range(cols):
            part_ref[r * cols + c] = total[r * 8 : (r + 1) * 8, c * 128 : (c + 1) * 128]


def dense_terms(p, dots, links, v, normed):
    sections, micro, _, rows = dots.shape
    experts = v.shape[2] // 2
    width = normed.shape[2]
    blocks = experts // 8 * (width // 128)
    whole = pl.BlockSpec(memory_space=pltpu.MemorySpace.VMEM)
    return pl.pallas_call(
        dense_kernel,
        in_specs=[pl.BlockSpec(memory_space=pltpu.MemorySpace.SMEM)] + [whole] * 4,
        out_specs=[whole] * 2,
        out_shape=[
            jax.ShapeDtypeStruct((micro, sections * experts, rows), BF16),
            jax.ShapeDtypeStruct((blocks, 8, 128), F32),
        ],
        compiler_params=params(32),
        name="dense",
    )(p, dots, links, v, normed)


def grads_kernel(p_ref, up_ref, back_ref, dense_ref, w_ref, out_ref):
    p = p_ref[0]
    sections = back_ref.shape[0]
    experts = w_ref.shape[1]
    total = up_ref[0].astype(F32)
    for s in reversed(range(sections)):
        j = (s - p) & (sections - 1)
        dense = dense_ref[0, s * experts : (s + 1) * experts, :]
        term = lax.dot_general(dense, w_ref[j], TN, preferred_element_type=F32)
        total = total + back_ref[s, 0].astype(F32) + term
        out_ref[s, 0] = total.astype(BF16)


def grads_of(p, upstream, back, dense, w):
    sections, micro, rows, quarter = back.shape
    experts = w.shape[1]
    return pl.pallas_call(
        grads_kernel,
        grid_spec=pltpu.PrefetchScalarGridSpec(
            num_scalar_prefetch=1,
            grid=(micro,),
            in_specs=[
                pl.BlockSpec((1, rows, quarter), lambda m, p: (m, 0, p[0])),
                pl.BlockSpec((sections, 1, rows, quarter), lambda m, p: (0, m, 0, 0)),
                pl.BlockSpec((1, sections * experts, rows), lambda m, p: (m, 0, 0)),
                pl.BlockSpec((sections, experts, quarter), lambda m, p: (0, 0, 0)),
            ],
            out_specs=pl.BlockSpec((sections, 1, rows, quarter), lambda m, p: (0, m, 0, 0)),
        ),
        out_shape=jax.ShapeDtypeStruct((sections, micro, rows, quarter), BF16),
        compiler_params=params(32),
        name="grads",
    )(p, upstream, back, dense, w)


def join_kernel(p_ref, *refs):
    step = pl.program_id(0)
    out_ref = refs[-1]
    for d in range(len(refs) - 1):

        @pl.when(step == d)
        def _():
            out_ref[...] = refs[d][...]


def join(p, blocks):
    n = len(blocks)
    micro, rows, quarter = blocks[0].shape
    return pl.pallas_call(
        join_kernel,
        grid_spec=pltpu.PrefetchScalarGridSpec(
            num_scalar_prefetch=1,
            grid=(n,),
            in_specs=[pl.BlockSpec((micro, rows, quarter), lambda d, p: (0, 0, 0))] * n,
            out_specs=pl.BlockSpec((micro, rows, quarter), lambda d, p: (0, 0, (p[0] - d) & (n - 1))),
        ),
        out_shape=jax.ShapeDtypeStruct((micro, rows, n * quarter), BF16),
        compiler_params=params(32),
        name="join",
    )(p, *blocks)


def turned(block, distance):
    n = lax.axis_size("pipe")
    return lax.ppermute(block, "pipe", [(i, (i + distance) % n) for i in range(n)])


def gathered(block):
    n = lax.axis_size("pipe")
    return [block] + [turned(block, n - j) for j in range(1, n)]


def on_device(normed, saved_out, expert_grads, routes, router_weight, upstream):
    sections = lax.axis_size("pipe")
    section = lax.axis_index("pipe")
    p = section.astype(jnp.int32).reshape(1)
    normed = normed[0]
    micro, rows, width = normed.shape
    quarter = width // sections
    w = router_weight[0].T
    experts = w.shape[0]

    send = pack(jnp.transpose(expert_grads[0, :, 0, 0], (0, 2, 1, 3)))
    received = lax.all_to_all(send, "expert", 0, 0, tiled=True)

    v, gates, places = gates_of(normed, w, jnp.transpose(routes[0], (0, 2, 1)))
    gates = jnp.concatenate([gates, gates], axis=-1)
    places = jnp.concatenate([places, places], axis=-1)

    def part_for(array, distance, axis):
        start = ((section + distance) % sections) * quarter
        return lax.dynamic_slice_in_dim(array, start, quarter, axis)

    def spread(array, axis):
        blocks = [part_for(array, 0, axis)]
        for j in range(1, sections):
            blocks.append(turned(part_for(array, sections - j, axis), sections - j))
        return jnp.stack(blocks)

    v_all = jnp.stack(gathered(v))
    w_all = spread(w, 1)
    saved_all = spread(jnp.transpose(saved_out[0], (2, 0, 1, 3)), 3)
    links = coupling(p, saved_all, w_all, v_all)
    links = sum(gathered(links))

    back = combine(received, gates, places)
    back = lax.all_to_all(back, "pipe", 0, 0, tiled=True)
    dots = partial_dots(p, upstream, back, saved_all)
    dots = jnp.broadcast_to(dots[None], (sections,) + dots.shape)
    dots = lax.all_to_all(dots, "pipe", 0, 0, tiled=True)
    dense, part = dense_terms(p, dots, links, v_all, normed)

    axes = ("expert", "dp")
    part = lax.all_to_all(part, axes, 0, 0, tiled=True)
    part = jnp.broadcast_to(jnp.sum(part, axis=0, keepdims=True), part.shape)
    part = lax.all_to_all(part, axes, 0, 0, tiled=True)
    cols = width // 128
    router_grad = part.reshape(experts // 8, cols, 8, 128).transpose(0, 2, 1, 3)
    router_grad = router_grad.reshape(experts, width).T

    outs = grads_of(p, upstream, back, dense, w_all)
    blocks = [lax.dynamic_index_in_dim(outs, section, 0, keepdims=False)]
    for d in range(1, sections):
        block = lax.dynamic_index_in_dim(outs, (section + d) % sections, 0, keepdims=False)
        blocks.append(turned(block, d))
    grad_input = join(p, blocks)
    return (grad_input[None], router_grad[None])


def solution(mesh):
    in_specs = (
        P("pipe", None, ("expert", "dp"), None),
        P("pipe", None, ("expert", "dp"), None, None),
        P("pipe", None, "dp", "expert", None, None, None),
        P("pipe", None, ("expert", "dp"), None),
        P("pipe", None, None),
        P(None, ("expert", "dp"), None),
    )
    out_specs = (P("pipe", None, ("expert", "dp"), None), P("pipe", None, None))
    return jax.shard_map(
        on_device, mesh=mesh, in_specs=in_specs, out_specs=out_specs, check_vma=False
    )
```

```python
import functools

import jax
import jax.numpy as jnp
from jax import lax
from jax.experimental import pallas as pl
from jax.experimental.pallas import tpu as pltpu
from jax.sharding import PartitionSpec as P

F32 = jnp.float32
BF16 = jnp.bfloat16
NT = (((1,), (1,)), ((), ()))
TN = (((0,), (0,)), ((), ()))


def params(mib):
    return pltpu.CompilerParams(vmem_limit_bytes=mib << 20)


def in_hbm(array):
    return pltpu.with_memory_space_constraint(array, pltpu.MemorySpace.HBM)


def pack_kernel(first, main_ref, last_ref, out_ref):
    unit = pl.program_id(0) + first
    micro, _, dests, width = last_ref.shape
    half = width // 2

    @pl.when(unit > 0)
    def _():
        slots = main_ref.shape[1]
        n = slots * dests
        out_row = lax.broadcasted_iota(jnp.int32, (n, n), 0)
        in_row = lax.broadcasted_iota(jnp.int32, (n, n), 1)
        swap = (in_row == (out_row % slots) * dests + out_row // slots).astype(BF16)
        rows = main_ref[0].reshape(n, half)
        moved = jnp.dot(swap, rows, preferred_element_type=F32)
        out_ref[...] = moved.reshape(dests, slots, half).astype(BF16)

    @pl.when(unit == 0)
    def _():
        n_in = micro * dests
        n_out = 2 * micro * dests
        out_row = lax.broadcasted_iota(jnp.int32, (n_out, n_in), 0)
        in_row = lax.broadcasted_iota(jnp.int32, (n_out, n_in), 1)
        within = out_row % (2 * micro)
        source = (within % micro) * dests + out_row // (2 * micro)
        total = jnp.zeros((n_out, half), F32)
        for h in range(2):
            pick = ((in_row == source) & (within // micro == h)).astype(BF16)
            rows = last_ref[:, 0, :, h * half : (h + 1) * half].reshape(n_in, half)
            total = total + jnp.dot(pick, rows, preferred_element_type=F32)
        out_ref[...] = total.reshape(dests, 2 * micro, half).astype(BF16)


def pack(grads, first, last):
    micro, cap, dests, width = grads.shape
    half = width // 2

    def main(u):
        return jnp.maximum(u + first - 1, 0)

    return pl.pallas_call(
        functools.partial(pack_kernel, first),
        grid=(last - first,),
        in_specs=[
            pl.BlockSpec((1, cap - 1, dests, half), lambda u: (main(u) // 2, 0, 0, main(u) % 2)),
            pl.BlockSpec((micro, 1, dests, width), lambda u: (0, cap - 1, 0, 0)),
        ],
        out_specs=pl.BlockSpec((dests, 8, half), lambda u: (0, u, 0)),
        out_shape=pltpu.HBM((dests, (last - first) * 8, half), BF16),
        compiler_params=params(40),
        name="pack_slots",
    )(grads, grads)


def gate_kernel(normed_ref, w_ref, routes_ref, v_ref, gate_ref, place_ref):
    m = pl.program_id(0)
    logits = lax.dot_general(w_ref[...], normed_ref[0], NT, preferred_element_type=F32)
    experts, rows = logits.shape
    expl = jnp.exp(logits)
    probs = expl / jnp.sum(expl, axis=0, keepdims=True)
    ids = lax.broadcasted_iota(jnp.int32, (experts, rows), 0)
    first = lax.broadcasted_iota(jnp.int32, (rows, rows), 0)
    second = lax.broadcasted_iota(jnp.int32, (rows, rows), 1)
    earlier = (first < second).astype(BF16)
    named = [ids == routes_ref[0, k : k + 1, :] for k in range(2)]
    both = jnp.where(named[0] | named[1], 1.0, 0.0).astype(BF16)
    before = jnp.dot(both, earlier, preferred_element_type=F32)
    for k in range(2):
        gate = jnp.sum(jnp.where(named[k], probs, 0.0), axis=0, keepdims=True)
        v_ref[0, k * experts : (k + 1) * experts, :] = gate * (jnp.where(named[k], 1.0, 0.0) - probs)
        gate_ref[0, k : k + 1, :] = gate
        slot = jnp.sum(jnp.where(named[k], before, 0.0), axis=0, keepdims=True).astype(jnp.int32)
        start = routes_ref[0, k : k + 1, :] * 8
        place_ref[0, k : k + 1, :] = jnp.where(slot < 8, start + slot, experts * 8 + start + m)


def gates_of(normed, w, routes):
    micro, rows, width = normed.shape
    experts = w.shape[0]
    return pl.pallas_call(
        gate_kernel,
        grid=(micro,),
        in_specs=[
            pl.BlockSpec((1, rows, width), lambda m: (m, 0, 0)),
            pl.BlockSpec((experts, width), lambda m: (0, 0)),
            pl.BlockSpec((1, 2, rows), lambda m: (m, 0, 0)),
        ],
        out_specs=[
            pl.BlockSpec((1, 2 * experts, rows), lambda m: (m, 0, 0)),
            pl.BlockSpec((1, 2, rows), lambda m: (m, 0, 0)),
            pl.BlockSpec((1, 2, rows), lambda m: (m, 0, 0)),
        ],
        out_shape=[
            jax.ShapeDtypeStruct((micro, 2 * experts, rows), F32),
            jax.ShapeDtypeStruct((micro, 2, rows), F32),
            jax.ShapeDtypeStruct((micro, 2, rows), jnp.int32),
        ],
        compiler_params=params(32),
        name="gates",
    )(normed, w, routes)


def pairs(sections):
    found = []
    for s in range(sections - 1):
        for k in range(2):
            for upper in range(s + 1, sections):
                for k2 in range(2):
                    found.append((s, k, upper, k2))
    return {key: row for row, key in enumerate(found)}


def couple_kernel(p_ref, saved_ref, w_ref, v_ref, out_ref):
    p = p_ref[0]
    sections, experts, _ = w_ref.shape
    for s in range(sections - 1):
        j = (s - p) & (sections - 1)
        for k in range(2):
            saved = saved_ref[j, k, 0]
            for upper in range(s + 1, sections):
                j2 = (upper - p) & (sections - 1)
                part = lax.dot_general(w_ref[j2], saved, NT, preferred_element_type=F32)
                for k2 in range(2):
                    row = pairs(sections)[(s, k, upper, k2)]
                    v = v_ref[j2, 0, k2 * experts : (k2 + 1) * experts, :]
                    out_ref[0, row : row + 1, :] = jnp.sum(part * v, axis=0, keepdims=True)


def coupling(p, saved, w, v):
    sections, _, micro, rows, quarter = saved.shape
    experts = w.shape[1]
    n = len(pairs(sections))
    return pl.pallas_call(
        couple_kernel,
        grid_spec=pltpu.PrefetchScalarGridSpec(
            num_scalar_prefetch=1,
            grid=(micro,),
            in_specs=[
                pl.BlockSpec((sections, 2, 1, rows, quarter), lambda m, p: (0, 0, m, 0, 0)),
                pl.BlockSpec((sections, experts, quarter), lambda m, p: (0, 0, 0)),
                pl.BlockSpec((sections, 1, 2 * experts, rows), lambda m, p: (0, m, 0, 0)),
            ],
            out_specs=pl.BlockSpec((1, n, rows), lambda m, p: (m, 0, 0)),
        ),
        out_shape=jax.ShapeDtypeStruct((micro, n, rows), F32),
        compiler_params=params(32),
        name="coupling",
    )(p, saved, w, v)


def combine_kernel(micro, main_ref, last_ref, gate_ref, place_ref, out_ref):
    h = pl.program_id(0)
    experts, _, half = main_ref.shape
    lanes = gate_ref.shape[2]
    rows = lanes // 2
    n = experts * 8
    index = lax.broadcasted_iota(jnp.int32, (2 * n, lanes), 0)
    pick = jnp.zeros((2 * n, lanes), F32)
    for k in range(2):
        place = place_ref[0, k : k + 1, :]
        place = place + jnp.where(place >= n, h * micro, 0)
        pick = pick + jnp.where(index == place, gate_ref[0, k : k + 1, :], 0.0)
    high = pick.astype(BF16)
    low = (pick - high.astype(F32)).astype(BF16)
    is_low = lax.broadcasted_iota(jnp.int32, (2 * n, lanes), 1) >= rows
    pick = jnp.where(is_low, low.astype(F32), high.astype(F32)).astype(BF16)
    both = lax.dot_general(
        pick[:n], main_ref[...].reshape(n, half), TN, preferred_element_type=F32
    ) + lax.dot_general(pick[n:], last_ref[...].reshape(n, half), TN, preferred_element_type=F32)
    total = (both[:rows] + both[rows:]).astype(BF16)
    out_ref[0, 0] = total[:, : half // 2]
    out_ref[1, 0] = total[:, half // 2 :]


def combine(main, last, gates, places, first_m, count, first_unit):
    experts, _, half = main.shape
    micro, _, lanes = gates.shape
    rows = lanes // 2
    return pl.pallas_call(
        functools.partial(combine_kernel, micro),
        grid=(2, count),
        in_specs=[
            pl.BlockSpec((experts, 8, half), lambda h, m: (0, first_unit + 2 * m + h, 0)),
            pl.BlockSpec((experts, 8, half), lambda h, m: (0, 0, 0)),
            pl.BlockSpec((1, 2, lanes), lambda h, m: (first_m + m, 0, 0)),
            pl.BlockSpec((1, 2, lanes), lambda h, m: (first_m + m, 0, 0)),
        ],
        out_specs=pl.BlockSpec((2, 1, rows, half // 2), lambda h, m: (h, m, 0, 0)),
        out_shape=jax.ShapeDtypeStruct((4, count, rows, half // 2), BF16),
        compiler_params=params(40),
        name="combine",
    )(main, last, gates, places)


def dots_kernel(turned_order, p_ref, up_ref, back_ref, saved_ref, out_ref):
    p = p_ref[0]
    sections, _, rows, quarter = back_ref.shape
    base = up_ref[0].astype(F32)
    ones = jnp.ones((8, 128), F32)
    for s in reversed(range(sections)):
        j = (s - p) & (sections - 1)
        for k in range(2):
            product = base * saved_ref[j, k, 0].astype(F32)
            lane = product[:, :128]
            for c in range(1, quarter // 128):
                lane = lane + product[:, c * 128 : (c + 1) * 128]
            row = lax.dot_general(
                ones, lane, NT, precision=lax.Precision.HIGHEST, preferred_element_type=F32
            )
            out_ref[0, 2 * s + k : 2 * s + k + 1, :] = row[:1]
        if s > 0:
            base = base + back_ref[j if turned_order else s, 0].astype(F32)


def partial_dots(p, upstream, back, saved, first_m, turned_order):
    sections, count, rows, quarter = back.shape
    return pl.pallas_call(
        functools.partial(dots_kernel, turned_order),
        grid_spec=pltpu.PrefetchScalarGridSpec(
            num_scalar_prefetch=1,
            grid=(count,),
            in_specs=[
                pl.BlockSpec((1, rows, quarter), lambda m, p: (first_m + m, 0, p[0])),
                pl.BlockSpec((sections, 1, rows, quarter), lambda m, p: (0, m, 0, 0)),
                pl.BlockSpec((sections, 2, 1, rows, quarter), lambda m, p: (0, 0, first_m + m, 0, 0)),
            ],
            out_specs=pl.BlockSpec((1, 2 * sections, rows), lambda m, p: (m, 0, 0)),
        ),
        out_shape=jax.ShapeDtypeStruct((count, 2 * sections, rows), F32),
        compiler_params=params(32),
        name="dots",
    )(p, upstream, back, saved)


def dense_kernel(p_ref, dots_ref, couple_ref, v_ref, normed_ref, dense_ref, part_ref):
    p = p_ref[0]
    sections, micro, _, rows = dots_ref.shape
    experts = v_ref.shape[2] // 2
    width = normed_ref.shape[2]
    table = pairs(sections)
    total = jnp.zeros((experts, width), F32)
    for m in range(micro):
        given = dots_ref[0, m]
        for source in range(1, sections):
            given = given + dots_ref[source, m]
        links = couple_ref[m]
        dots = {}
        own = jnp.zeros((experts, rows), F32)
        for s in reversed(range(sections)):
            j = (s - p) & (sections - 1)
            dense = jnp.zeros((experts, rows), F32)
            for k in range(2):
                value = given[2 * s + k : 2 * s + k + 1, :]
                for upper in range(s + 1, sections):
                    for k2 in range(2):
                        row = table[(s, k, upper, k2)]
                        value = value + links[row : row + 1, :] * dots[(upper, k2)]
                dots[(s, k)] = value
                dense = dense + value * v_ref[j, m, k * experts : (k + 1) * experts, :]
            dense_ref[m, s * experts : (s + 1) * experts, :] = dense.astype(BF16)
            own = jnp.where(p == s, dense, own)
        total = total + jnp.dot(own.astype(BF16), normed_ref[m], preferred_element_type=F32)
    total = total * (1.0 / micro)
    cols = width // 128
    for r in range(experts // 8):
        for c in range(cols):
            tile = total[r * 8 : (r + 1) * 8, c * 128 : (c + 1) * 128]
            part_ref[r * cols + c] = tile.astype(BF16)


def dense_terms(p, dots, links, v, normed):
    sections, micro, _, rows = dots.shape
    experts = v.shape[2] // 2
    width = normed.shape[2]
    blocks = experts // 8 * (width // 128)
    whole = pl.BlockSpec(memory_space=pltpu.MemorySpace.VMEM)
    return pl.pallas_call(
        dense_kernel,
        in_specs=[pl.BlockSpec(memory_space=pltpu.MemorySpace.SMEM)] + [whole] * 4,
        out_specs=[whole] * 2,
        out_shape=[
            jax.ShapeDtypeStruct((micro, sections * experts, rows), BF16),
            jax.ShapeDtypeStruct((blocks, 8, 128), BF16),
        ],
        compiler_params=params(32),
        name="dense",
    )(p, dots, links, v, normed)


def grads_kernel(turned_order, p_ref, up_ref, back_ref, dense_ref, w_ref, out_ref):
    p = p_ref[0]
    sections = back_ref.shape[0]
    experts = w_ref.shape[1]
    total = up_ref[0].astype(F32)
    for s in reversed(range(sections)):
        j = (s - p) & (sections - 1)
        dense = dense_ref[0, s * experts : (s + 1) * experts, :]
        term = lax.dot_general(dense, w_ref[j], TN, preferred_element_type=F32)
        total = total + back_ref[j if turned_order else s, 0].astype(F32) + term
        out_ref[j, 0] = total.astype(BF16)


def grads_of(p, upstream, back, dense, w, first_m, turned_order):
    sections, count, rows, quarter = back.shape
    experts = w.shape[1]
    return pl.pallas_call(
        functools.partial(grads_kernel, turned_order),
        grid_spec=pltpu.PrefetchScalarGridSpec(
            num_scalar_prefetch=1,
            grid=(count,),
            in_specs=[
                pl.BlockSpec((1, rows, quarter), lambda m, p: (first_m + m, 0, p[0])),
                pl.BlockSpec((sections, 1, rows, quarter), lambda m, p: (0, m, 0, 0)),
                pl.BlockSpec((1, sections * experts, rows), lambda m, p: (first_m + m, 0, 0)),
                pl.BlockSpec((sections, experts, quarter), lambda m, p: (0, 0, 0)),
            ],
            out_specs=pl.BlockSpec((sections, 1, rows, quarter), lambda m, p: (0, m, 0, 0)),
        ),
        out_shape=jax.ShapeDtypeStruct((sections, count, rows, quarter), BF16),
        compiler_params=params(32),
        name="grads",
    )(p, upstream, back, dense, w)


def join_kernel(p_ref, *refs):
    step = pl.program_id(0)
    out_ref = refs[-1]
    for d in range(len(refs) - 1):

        @pl.when(step == d)
        def _():
            out_ref[...] = refs[d][...]


def join(p, blocks):
    n = len(blocks)
    micro, rows, quarter = blocks[0].shape
    return pl.pallas_call(
        join_kernel,
        grid_spec=pltpu.PrefetchScalarGridSpec(
            num_scalar_prefetch=1,
            grid=(n,),
            in_specs=[pl.BlockSpec((micro, rows, quarter), lambda d, p: (0, 0, 0))] * n,
            out_specs=pl.BlockSpec((micro, rows, quarter), lambda d, p: (0, 0, (p[0] - d) & (n - 1))),
        ),
        out_shape=jax.ShapeDtypeStruct((micro, rows, n * quarter), BF16),
        compiler_params=params(32),
        name="join",
    )(p, *blocks)


def turned(block, distance):
    n = lax.axis_size("pipe")
    return lax.ppermute(block, "pipe", [(i, (i + distance) % n) for i in range(n)])


def gathered(block):
    n = lax.axis_size("pipe")
    return [block] + [turned(block, n - j) for j in range(1, n)]


def on_device(normed, saved_out, expert_grads, routes, router_weight, upstream):
    sections = lax.axis_size("pipe")
    section = lax.axis_index("pipe")
    p = section.astype(jnp.int32).reshape(1)
    normed = normed[0]
    micro, rows, width = normed.shape
    quarter = width // sections
    w = router_weight[0].T
    experts = w.shape[0]

    grads = in_hbm(jnp.transpose(expert_grads[0, :, 0, 0], (0, 2, 1, 3)))
    units = 2 * micro + 1
    cut = units - 2
    lead = lax.all_to_all(pack(grads, 0, cut), "expert", 0, 0, tiled=True)
    tail_send = pack(grads, cut, units)

    v, gates, places = gates_of(normed, w, jnp.transpose(routes[0], (0, 2, 1)))
    gates = jnp.concatenate([gates, gates], axis=-1)
    places = jnp.concatenate([places, places], axis=-1)

    def part_for(array, distance, axis):
        start = ((section + distance) % sections) * quarter
        return lax.dynamic_slice_in_dim(array, start, quarter, axis)

    def spread(array, axis):
        blocks = [part_for(array, 0, axis)]
        for j in range(1, sections):
            blocks.append(turned(part_for(array, sections - j, axis), sections - j))
        return jnp.stack(blocks)

    v_all = jnp.stack(gathered(v))
    w_all = spread(w, 1)
    saved_all = spread(jnp.transpose(saved_out[0], (2, 0, 1, 3)), 3)
    links = coupling(p, saved_all, w_all, v_all)
    links = sum(gathered(links))
    gates, places, links, saved_all, w_all, v_all, tail_send = lax.optimization_barrier(
        (gates, places, links, saved_all, w_all, v_all, tail_send)
    )

    def spread_back(back):
        def block(distance):
            return lax.dynamic_index_in_dim(back, (section + distance) % sections, 0, False)

        blocks = [block(0)] + [turned(block(sections - j), sections - j) for j in range(1, sections)]
        return jnp.stack(blocks)

    lead, tail_send = lax.optimization_barrier((lead, tail_send))
    tail = lax.all_to_all(tail_send, "expert", 0, 0, tiled=True)
    back_lead = spread_back(combine(lead, lead, gates, places, 0, micro - 1, 1))
    dots_lead = partial_dots(p, upstream, back_lead, saved_all, 0, True)
    dots_lead, back_lead, gates = lax.optimization_barrier((dots_lead, back_lead, gates))
    back_tail = combine(tail, lead, gates, places, micro - 1, 1, 0)
    back_tail = lax.all_to_all(back_tail, "pipe", 0, 0, tiled=True)
    dots_tail = partial_dots(p, upstream, back_tail, saved_all, micro - 1, False)

    dots = jnp.concatenate([dots_lead, dots_tail])
    dots = jnp.broadcast_to(dots[None], (sections,) + dots.shape)
    dots = lax.all_to_all(dots, "pipe", 0, 0, tiled=True)
    dense, part = dense_terms(p, dots, links, v_all, normed)

    axes = ("expert", "dp")
    part = lax.all_to_all(part, axes, 0, 0, tiled=True)

    outs_lead = grads_of(p, upstream, back_lead, dense, w_all, 0, True)
    outs_tail = grads_of(p, upstream, back_tail, dense, w_all, micro - 1, False)
    outs = jnp.concatenate([outs_lead, outs_tail], axis=1)
    blocks = [outs[0]] + [turned(outs[d], d) for d in range(1, sections)]

    total = jnp.sum(part.astype(F32), axis=0, keepdims=True).astype(BF16)
    total, blocks[1], blocks[3] = lax.optimization_barrier((total, blocks[1], blocks[3]))
    part = lax.all_to_all(jnp.broadcast_to(total, part.shape), axes, 0, 0, tiled=True)
    cols = width // 128
    router_grad = part.astype(F32).reshape(experts // 8, cols, 8, 128).transpose(0, 2, 1, 3)
    router_grad = router_grad.reshape(experts, width).T
    grad_input = join(p, blocks)
    return (grad_input[None], router_grad[None])


def solution(mesh):
    in_specs = (
        P("pipe", None, ("expert", "dp"), None),
        P("pipe", None, ("expert", "dp"), None, None),
        P("pipe", None, "dp", "expert", None, None, None),
        P("pipe", None, ("expert", "dp"), None),
        P("pipe", None, None),
        P(None, ("expert", "dp"), None),
    )
    out_specs = (P("pipe", None, ("expert", "dp"), None), P("pipe", None, None))
    return jax.shard_map(
        on_device, mesh=mesh, in_specs=in_specs, out_specs=out_specs, check_vma=False
    )
```

```python
import functools

import jax
import jax.numpy as jnp
from jax import lax
from jax.experimental import pallas as pl
from jax.experimental.pallas import tpu as pltpu
from jax.sharding import PartitionSpec as P

F32 = jnp.float32
BF16 = jnp.bfloat16
NT = (((1,), (1,)), ((), ()))
TN = (((0,), (0,)), ((), ()))

TILE = 8


def params(mib):
    return pltpu.CompilerParams(vmem_limit_bytes=mib << 20)


def in_hbm(array):
    return pltpu.with_memory_space_constraint(array, pltpu.MemorySpace.HBM)


def iotas(shape):
    return [lax.broadcasted_iota(jnp.int32, shape, d) for d in range(2)]


def swap_matrix(slots, dests):
    out_row, in_row = iotas((slots * dests, slots * dests))
    return (in_row == (out_row % slots) * dests + out_row // slots).astype(BF16)


def lead_pack_kernel(grads_ref, out_ref):
    _, slots, dests, width = grads_ref.shape
    half = width // 2
    swap = swap_matrix(slots, dests)
    for h in range(2):
        rows = grads_ref[0, :, :, h * half : (h + 1) * half].reshape(slots * dests, half)
        moved = jnp.dot(swap, rows, preferred_element_type=F32)
        out_ref[:, h * slots : (h + 1) * slots, :] = moved.reshape(dests, slots, half).astype(BF16)


def lead_pack(grads, count):
    _, _, dests, width = grads.shape
    half = width // 2
    return pl.pallas_call(
        lead_pack_kernel,
        grid=(count,),
        in_specs=[pl.BlockSpec((1, TILE, dests, width), lambda m: (m, 0, 0, 0))],
        out_specs=pl.BlockSpec((dests, 2 * TILE, half), lambda m: (0, m, 0)),
        out_shape=pltpu.HBM((dests, 2 * TILE * count, half), BF16),
        compiler_params=params(40),
        name="lead_pack",
    )(grads)


def tail_pack_kernel(*refs):
    out_ref = refs[-1]
    kept, dests, quarter = refs[0].shape
    micro = kept - TILE
    swap = swap_matrix(TILE, dests)
    out_row, in_row = iotas((2 * micro * dests, micro * dests))
    within = out_row % (2 * micro)
    source = (within % micro) * dests + out_row // (2 * micro)
    for c in range(2):
        total = jnp.zeros((2 * micro * dests, quarter), F32)
        columns = slice(c * quarter, (c + 1) * quarter)
        for h in range(2):
            ref = refs[2 * h + c]
            moved = jnp.dot(swap, ref[:TILE].reshape(TILE * dests, quarter), preferred_element_type=F32)
            moved = moved.reshape(dests, TILE, quarter).astype(BF16)
            out_ref[:, h * TILE : (h + 1) * TILE, columns] = moved
            pick = ((in_row == source) & (within // micro == h)).astype(BF16)
            rows = ref[TILE:].reshape(micro * dests, quarter)
            total = total + jnp.dot(pick, rows, preferred_element_type=F32)
        out_ref[:, 2 * TILE :, columns] = total.reshape(dests, 2 * micro, quarter).astype(BF16)


def tail_pack(blocks):
    kept, dests, quarter = blocks[0].shape
    return pl.pallas_call(
        tail_pack_kernel,
        out_shape=jax.ShapeDtypeStruct((dests, 2 * TILE + 2 * (kept - TILE), 2 * quarter), BF16),
        compiler_params=params(40),
        name="tail_pack",
    )(*blocks)


def gate_kernel(normed_ref, w_ref, routes_ref, info_ref):
    m = pl.program_id(0)
    logits = lax.dot_general(w_ref[...], normed_ref[0], NT, preferred_element_type=F32)
    experts, rows = logits.shape
    expl = jnp.exp(logits)
    probs = expl / jnp.sum(expl, axis=0, keepdims=True)
    ids = lax.broadcasted_iota(jnp.int32, (experts, rows), 0)
    first, second = iotas((rows, rows))
    earlier = (first < second).astype(BF16)
    named = [ids == routes_ref[0, k : k + 1, :] for k in range(2)]
    both = jnp.where(named[0] | named[1], 1.0, 0.0).astype(BF16)
    before = jnp.dot(both, earlier, preferred_element_type=F32)
    found = []
    gates = []
    places = []
    for k in range(2):
        gate = jnp.sum(jnp.where(named[k], probs, 0.0), axis=0, keepdims=True)
        found.append(gate * (jnp.where(named[k], 1.0, 0.0) - probs))
        gates.append(gate)
        slot = jnp.sum(jnp.where(named[k], before, 0.0), axis=0, keepdims=True).astype(jnp.int32)
        start = routes_ref[0, k : k + 1, :] * TILE
        place = jnp.where(slot < TILE, start + slot, experts * TILE + start + m)
        places.append(place.astype(F32))
    found.append(jnp.concatenate(gates + places + [jnp.zeros((4, rows), F32)], axis=0))
    info = jnp.concatenate(found, axis=0)
    info_ref[0, :, :rows] = info
    info_ref[0, :, rows:] = info


def gate_info(normed, w, routes):
    micro, rows, width = normed.shape
    experts = w.shape[0]
    height = 2 * experts + 8
    return pl.pallas_call(
        gate_kernel,
        grid=(micro,),
        in_specs=[
            pl.BlockSpec((1, rows, width), lambda m: (m, 0, 0)),
            pl.BlockSpec((experts, width), lambda m: (0, 0)),
            pl.BlockSpec((1, 2, rows), lambda m: (m, 0, 0)),
        ],
        out_specs=pl.BlockSpec((1, height, 2 * rows), lambda m: (m, 0, 0)),
        out_shape=jax.ShapeDtypeStruct((micro, height, 2 * rows), F32),
        compiler_params=params(32),
        name="gates",
    )(normed, w, routes)


def pairs(sections):
    found = []
    for s in range(sections - 1):
        for k in range(2):
            for upper in range(s + 1, sections):
                for k2 in range(2):
                    found.append((s, k, upper, k2))
    return {key: row for row, key in enumerate(found)}


def couple_kernel(p_ref, saved_ref, w_ref, info_ref, out_ref):
    p = p_ref[0]
    sections, experts, _ = w_ref.shape
    rows = saved_ref.shape[3]
    table = pairs(sections)
    for s in range(sections - 1):
        j = (s - p) & (sections - 1)
        for k in range(2):
            saved = saved_ref[j, k, 0]
            for upper in range(s + 1, sections):
                j2 = (upper - p) & (sections - 1)
                part = lax.dot_general(w_ref[j2], saved, NT, preferred_element_type=F32)
                for k2 in range(2):
                    row = table[(s, k, upper, k2)]
                    v = info_ref[j2, 0, k2 * experts : (k2 + 1) * experts, :rows]
                    out_ref[0, row : row + 1, :] = jnp.sum(part * v, axis=0, keepdims=True)


def coupling(p, saved, w, info):
    sections, _, micro, rows, quarter = saved.shape
    experts = w.shape[1]
    n = len(pairs(sections))
    return pl.pallas_call(
        couple_kernel,
        grid_spec=pltpu.PrefetchScalarGridSpec(
            num_scalar_prefetch=1,
            grid=(micro,),
            in_specs=[
                pl.BlockSpec((sections, 2, 1, rows, quarter), lambda m, p: (0, 0, m, 0, 0)),
                pl.BlockSpec((sections, experts, quarter), lambda m, p: (0, 0, 0)),
                pl.BlockSpec((sections, 1) + info.shape[2:], lambda m, p: (0, m, 0, 0)),
            ],
            out_specs=pl.BlockSpec((1, n, rows), lambda m, p: (m, 0, 0)),
        ),
        out_shape=jax.ShapeDtypeStruct((micro, n, rows), F32),
        compiler_params=params(32),
        name="coupling",
    )(p, saved, w, info)


def picked(info, experts, rows, value, first, received):
    n = received.shape[0]
    index = lax.broadcasted_iota(jnp.int32, (n, 2 * rows), 0)
    pick = jnp.zeros((n, 2 * rows), F32)
    for k in range(2):
        gate = info[2 * experts + k : 2 * experts + k + 1, :]
        place = info[2 * experts + 2 + k : 2 * experts + 3 + k, :].astype(jnp.int32)
        inside = (place >= first) & (place < first + n)
        row = jnp.where(inside, place - first + value, -1)
        pick = pick + jnp.where(index == row, gate, 0.0)
    high = pick.astype(BF16).astype(F32)
    is_low = lax.broadcasted_iota(jnp.int32, (n, 2 * rows), 1) >= rows
    pick = jnp.where(is_low, pick - high, high).astype(BF16)
    both = lax.dot_general(pick, received, TN, preferred_element_type=F32)
    return both[:rows] + both[rows:]


def lead_kernel(experts, main_ref, info_ref, out_ref):
    half = main_ref.shape[2]
    rows = info_ref.shape[2] // 2
    received = main_ref[...].reshape(experts * TILE, half)
    total = picked(info_ref[0], experts, rows, 0, 0, received).astype(BF16)
    out_ref[0, 0] = total[:, : half // 2]
    out_ref[1, 0] = total[:, half // 2 :]


def lead_combine(received, info):
    experts, packed, half = received.shape
    count = packed // (2 * TILE)
    rows = info.shape[2] // 2
    return pl.pallas_call(
        functools.partial(lead_kernel, experts),
        grid=(2, count),
        in_specs=[
            pl.BlockSpec((experts, TILE, half), lambda h, m: (0, 2 * m + h, 0)),
            pl.BlockSpec((1,) + info.shape[1:], lambda h, m: (m, 0, 0)),
        ],
        out_specs=pl.BlockSpec((2, 1, rows, half // 2), lambda h, m: (h, m, 0, 0)),
        out_shape=jax.ShapeDtypeStruct((4, count, rows, half // 2), BF16),
        compiler_params=params(40),
        name="lead_combine",
    )(received, info)


def tail_kernel(
    p_ref, received_ref, info_ref, up_ref, lead_ref, saved_ref, back_ref, dots_ref, last_ref, sum_ref
):
    m = pl.program_id(0)
    micro = pl.num_programs(0)
    p = p_ref[0]
    experts, _, half = received_ref.shape
    sections, _, rows, quarter = sum_ref.shape[:1] + (1,) + sum_ref.shape[1:]
    n = experts * TILE

    @pl.when(m == 0)
    def _():
        last_ref[...] = received_ref[:, 2 * TILE :, :].reshape(n, half)

    for j in range(sections):
        h, c = divmod(j, 2)
        columns = slice(c * quarter, (c + 1) * quarter)
        info = info_ref[j, 0]
        extra = picked(info, experts, rows, h * (TILE // 2), n, last_ref[:, columns])

        @pl.when(m < micro - 1)
        def _():
            sum_ref[j] = extra + lead_ref[j, 0].astype(F32)

        @pl.when(m == micro - 1)
        def _():
            main = received_ref[:, h * TILE : (h + 1) * TILE, columns].reshape(n, quarter)
            sum_ref[j] = extra + picked(info, experts, rows, 0, 0, main)

        back_ref[j, 0] = sum_ref[j].astype(BF16)

    base = up_ref[0].astype(F32)
    ones = jnp.ones((8, 128), F32)
    found = {}
    for s in reversed(range(sections)):
        j = (s - p) & (sections - 1)
        for k in range(2):
            product = base * saved_ref[j, k, 0].astype(F32)
            lane = product[:, :128]
            for c in range(1, quarter // 128):
                lane = lane + product[:, c * 128 : (c + 1) * 128]
            row = lax.dot_general(
                ones, lane, NT, precision=lax.Precision.HIGHEST, preferred_element_type=F32
            )
            found[2 * s + k] = row[:1]
        if s > 0:
            base = base + sum_ref[j]
    dots = jnp.concatenate([found[i] for i in range(2 * sections)], axis=0)
    for dest in range(sections):
        dots_ref[dest, 0, :, :rows] = dots


def tail_combine(p, received, info, upstream, lead, saved):
    sections, _, micro, rows, quarter = saved.shape
    experts, packed, half = received.shape
    last_lead = lead.shape[1] - 1
    part = (sections, 1, rows, quarter)
    return pl.pallas_call(
        tail_kernel,
        grid_spec=pltpu.PrefetchScalarGridSpec(
            num_scalar_prefetch=1,
            grid=(micro,),
            in_specs=[
                pl.BlockSpec((experts, packed, half), lambda m, p: (0, 0, 0)),
                pl.BlockSpec((sections, 1) + info.shape[2:], lambda m, p: (0, m, 0, 0)),
                pl.BlockSpec((1, rows, quarter), lambda m, p: (m, 0, p[0])),
                pl.BlockSpec(part, lambda m, p: (0, jnp.minimum(m, last_lead), 0, 0)),
                pl.BlockSpec((sections, 2, 1, rows, quarter), lambda m, p: (0, 0, m, 0, 0)),
            ],
            out_specs=[
                pl.BlockSpec(part, lambda m, p: (0, m, 0, 0)),
                pl.BlockSpec((sections, 1, 2 * sections, 128), lambda m, p: (0, m, 0, 0)),
            ],
            scratch_shapes=[
                pltpu.VMEM((experts * TILE, half), BF16),
                pltpu.VMEM((sections, rows, quarter), F32),
            ],
        ),
        out_shape=[
            jax.ShapeDtypeStruct((sections, micro, rows, quarter), BF16),
            jax.ShapeDtypeStruct((sections, micro, 2 * sections, 128), F32),
        ],
        compiler_params=params(48),
        name="tail_combine",
    )(p, received, info, upstream, lead, saved)


def dense_kernel(p_ref, dots_ref, couple_ref, info_ref, normed_ref, dense_ref, part_ref, total_ref):
    m = pl.program_id(0)
    micro = pl.num_programs(0)
    p = p_ref[0]
    sections = dots_ref.shape[0]
    rows = normed_ref.shape[1]
    experts, width = total_ref.shape
    table = pairs(sections)
    given = dots_ref[0, 0, :, :rows]
    for source in range(1, sections):
        given = given + dots_ref[source, 0, :, :rows]
    links = couple_ref[0]
    dots = {}
    own = jnp.zeros((experts, rows), F32)
    for s in reversed(range(sections)):
        j = (s - p) & (sections - 1)
        dense = jnp.zeros((experts, rows), F32)
        for k in range(2):
            value = given[2 * s + k : 2 * s + k + 1, :]
            for upper in range(s + 1, sections):
                for k2 in range(2):
                    row = table[(s, k, upper, k2)]
                    value = value + links[row : row + 1, :] * dots[(upper, k2)]
            dots[(s, k)] = value
            dense = dense + value * info_ref[j, 0, k * experts : (k + 1) * experts, :rows]
        dense_ref[0, s * experts : (s + 1) * experts, :] = dense.astype(BF16)
        own = jnp.where(p == s, dense, own)
    part = jnp.dot(own.astype(BF16), normed_ref[0], preferred_element_type=F32)

    @pl.when(m == 0)
    def _():
        total_ref[...] = part

    @pl.when(m > 0)
    def _():
        total_ref[...] += part

    @pl.when(m == micro - 1)
    def _():
        total = total_ref[...] * (1.0 / micro)
        cols = width // 128
        for r in range(experts // 8):
            for c in range(cols):
                tile = total[r * 8 : (r + 1) * 8, c * 128 : (c + 1) * 128]
                part_ref[r * cols + c] = tile.astype(BF16)


def dense_terms(p, dots, links, info, normed):
    sections, micro = dots.shape[:2]
    _, rows, width = normed.shape
    experts = (info.shape[2] - 8) // 2
    blocks = experts // 8 * (width // 128)
    return pl.pallas_call(
        dense_kernel,
        grid_spec=pltpu.PrefetchScalarGridSpec(
            num_scalar_prefetch=1,
            grid=(micro,),
            in_specs=[
                pl.BlockSpec((sections, 1) + dots.shape[2:], lambda m, p: (0, m, 0, 0)),
                pl.BlockSpec((1,) + links.shape[1:], lambda m, p: (m, 0, 0)),
                pl.BlockSpec((sections, 1) + info.shape[2:], lambda m, p: (0, m, 0, 0)),
                pl.BlockSpec((1, rows, width), lambda m, p: (m, 0, 0)),
            ],
            out_specs=[
                pl.BlockSpec((1, sections * experts, rows), lambda m, p: (m, 0, 0)),
                pl.BlockSpec((blocks, 8, 128), lambda m, p: (0, 0, 0)),
            ],
            scratch_shapes=[pltpu.VMEM((experts, width), F32)],
        ),
        out_shape=[
            jax.ShapeDtypeStruct((micro, sections * experts, rows), BF16),
            jax.ShapeDtypeStruct((blocks, 8, 128), BF16),
        ],
        compiler_params=params(32),
        name="dense",
    )(p, dots, links, info, normed)


def grads_kernel(p_ref, up_ref, back_ref, dense_ref, w_ref, *refs):
    p = p_ref[0]
    total_ref = refs[-1]
    sections = back_ref.shape[0]
    experts = w_ref.shape[1]
    total = up_ref[0].astype(F32)
    for s in reversed(range(sections)):
        j = (s - p) & (sections - 1)
        dense = dense_ref[0, s * experts : (s + 1) * experts, :]
        term = lax.dot_general(dense, w_ref[j], TN, preferred_element_type=F32)
        total = total + back_ref[j, 0].astype(F32) + term
        total_ref[j] = total.astype(BF16)
    for j in range(sections):
        refs[j][0] = total_ref[j]


def grads_of(p, upstream, back, dense, w):
    sections, micro, rows, quarter = back.shape
    experts = w.shape[1]
    return pl.pallas_call(
        grads_kernel,
        grid_spec=pltpu.PrefetchScalarGridSpec(
            num_scalar_prefetch=1,
            grid=(micro,),
            in_specs=[
                pl.BlockSpec((1, rows, quarter), lambda m, p: (m, 0, p[0])),
                pl.BlockSpec((sections, 1, rows, quarter), lambda m, p: (0, m, 0, 0)),
                pl.BlockSpec((1, sections * experts, rows), lambda m, p: (m, 0, 0)),
                pl.BlockSpec((sections, experts, quarter), lambda m, p: (0, 0, 0)),
            ],
            out_specs=[pl.BlockSpec((1, rows, quarter), lambda m, p: (m, 0, 0))] * sections,
            scratch_shapes=[pltpu.VMEM((sections, rows, quarter), BF16)],
        ),
        out_shape=[jax.ShapeDtypeStruct((micro, rows, quarter), BF16)] * sections,
        compiler_params=params(32),
        name="grads",
    )(p, upstream, back, dense, w)


def join_kernel(p_ref, *refs):
    step = pl.program_id(0)
    out_ref = refs[-1]
    for d in range(len(refs) - 1):

        @pl.when(step == d)
        def _():
            out_ref[...] = refs[d][...]


def join(p, blocks):
    n = len(blocks)
    micro, rows, quarter = blocks[0].shape
    return pl.pallas_call(
        join_kernel,
        grid_spec=pltpu.PrefetchScalarGridSpec(
            num_scalar_prefetch=1,
            grid=(n,),
            in_specs=[pl.BlockSpec((micro, rows, quarter), lambda d, p: (0, 0, 0))] * n,
            out_specs=pl.BlockSpec((micro, rows, quarter), lambda d, p: (0, 0, (p[0] - d) & (n - 1))),
        ),
        out_shape=jax.ShapeDtypeStruct((micro, rows, n * quarter), BF16),
        compiler_params=params(32),
        name="join",
    )(p, *blocks)


def turned(block, distance):
    n = lax.axis_size("pipe")
    return lax.ppermute(block, "pipe", [(i, (i + distance) % n) for i in range(n)])


def gathered(block):
    n = lax.axis_size("pipe")
    return [block] + [turned(block, n - j) for j in range(1, n)]


def on_device(normed, saved_out, expert_grads, routes, router_weight, upstream):
    sections = lax.axis_size("pipe")
    section = lax.axis_index("pipe")
    p = section.astype(jnp.int32).reshape(1)
    normed = in_hbm(normed[0])
    upstream = in_hbm(upstream)
    micro, rows, width = normed.shape
    quarter = width // sections
    w = router_weight[0].T
    experts = w.shape[0]

    def spread(array, axis):
        blocks = []
        for j in range(sections):
            start = ((section - j) % sections) * quarter
            block = lax.dynamic_slice_in_dim(array, start, quarter, axis)
            blocks.append(turned(block, sections - j) if j else block)
        return blocks

    grads = jnp.transpose(expert_grads[0, :, 0, 0], (0, 2, 1, 3))
    lead = lax.all_to_all(lead_pack(in_hbm(grads), micro - 1), "expert", 0, 0, tiled=True)
    late = spread(jnp.concatenate([grads[micro - 1, :TILE], grads[:, TILE]]), 2)
    info = gate_info(normed, w, jnp.transpose(routes[0], (0, 2, 1)))
    tail_send = tail_pack(late)
    saved_out, tail_send = lax.optimization_barrier((saved_out, tail_send))

    info_all = jnp.stack(gathered(info))
    w_all = jnp.stack(spread(w, 1))
    saved = spread(jnp.transpose(saved_out[0], (2, 0, 1, 3)), 3)
    lead, tail_send, saved[1], saved[2], w_all, info_all = lax.optimization_barrier(
        (lead, tail_send, saved[1], saved[2], w_all, info_all)
    )
    saved_all = jnp.stack(saved)
    links = sum(gathered(coupling(p, saved_all, w_all, info_all)))

    tail = lax.all_to_all(tail_send, "expert", 0, 0, tiled=True)
    back = lead_combine(lead, info)

    def back_for(distance):
        return lax.dynamic_index_in_dim(back, (section + distance) % sections, 0, False)

    lead = jnp.stack(
        [turned(back_for(sections - j), sections - j) if j else back_for(0) for j in range(sections)]
    )
    lead, info_all, w_all, saved_all, links = lax.optimization_barrier(
        (lead, info_all, w_all, saved_all, links)
    )
    back, dots = tail_combine(p, tail, info_all, upstream, lead, saved_all)
    dots = lax.all_to_all(dots, "pipe", 0, 0, tiled=True)
    dense, part = dense_terms(p, dots, links, info_all, normed)

    axes = ("expert", "dp")
    part = lax.all_to_all(part, axes, 0, 0, tiled=True)
    outs = grads_of(p, upstream, back, dense, w_all)
    blocks = [turned(outs[d], d) if d else outs[0] for d in range(sections)]
    total = jnp.sum(part.astype(F32), axis=0, keepdims=True).astype(BF16)
    part = lax.all_to_all(jnp.broadcast_to(total, part.shape), axes, 0, 0, tiled=True)
    cols = width // 128
    router_grad = part.astype(F32).reshape(experts // 8, cols, 8, 128).transpose(0, 2, 1, 3)
    router_grad = router_grad.reshape(experts, width).T
    grad_input = join(p, blocks)
    return (grad_input[None], router_grad[None])


def solution(mesh):
    in_specs = (
        P("pipe", None, ("expert", "dp"), None),
        P("pipe", None, ("expert", "dp"), None, None),
        P("pipe", None, "dp", "expert", None, None, None),
        P("pipe", None, ("expert", "dp"), None),
        P("pipe", None, None),
        P(None, ("expert", "dp"), None),
    )
    out_specs = (P("pipe", None, ("expert", "dp"), None), P("pipe", None, None))
    return jax.shard_map(
        on_device, mesh=mesh, in_specs=in_specs, out_specs=out_specs, check_vma=False
    )
```

```python
import functools

import jax
import jax.numpy as jnp
from jax import lax
from jax.experimental import pallas as pl
from jax.experimental.pallas import tpu as pltpu
from jax.sharding import PartitionSpec as P

F32 = jnp.float32
BF16 = jnp.bfloat16
NT = (((1,), (1,)), ((), ()))
TN = (((0,), (0,)), ((), ()))

TILE = 8


def params(mib):
    return pltpu.CompilerParams(vmem_limit_bytes=mib << 20)


def in_hbm(array):
    return pltpu.with_memory_space_constraint(array, pltpu.MemorySpace.HBM)


def iotas(shape):
    return [lax.broadcasted_iota(jnp.int32, shape, d) for d in range(2)]


def swap_matrix(slots, dests):
    out_row, in_row = iotas((slots * dests, slots * dests))
    return (in_row == (out_row % slots) * dests + out_row // slots).astype(BF16)


def lead_pack_kernel(grads_ref, out_ref):
    _, slots, dests, width = grads_ref.shape
    half = width // 2
    swap = swap_matrix(slots, dests)
    for h in range(2):
        rows = grads_ref[0, :, :, h * half : (h + 1) * half].reshape(slots * dests, half)
        moved = jnp.dot(swap, rows, preferred_element_type=F32)
        out_ref[:, h * slots : (h + 1) * slots, :] = moved.reshape(dests, slots, half).astype(BF16)


def lead_pack(grads, count):
    _, _, dests, width = grads.shape
    half = width // 2
    return pl.pallas_call(
        lead_pack_kernel,
        grid=(count,),
        in_specs=[pl.BlockSpec((1, TILE, dests, width), lambda m: (m, 0, 0, 0))],
        out_specs=pl.BlockSpec((dests, 2 * TILE, half), lambda m: (0, m, 0)),
        out_shape=pltpu.HBM((dests, 2 * TILE * count, half), BF16),
        compiler_params=params(40),
        name="lead_pack",
    )(grads)


def tail_pack_kernel(*refs):
    out_ref = refs[-1]
    kept, dests, quarter = refs[0].shape
    micro = kept - TILE
    swap = swap_matrix(TILE, dests)
    out_row, in_row = iotas((2 * micro * dests, micro * dests))
    within = out_row % (2 * micro)
    source = (within % micro) * dests + out_row // (2 * micro)
    for c in range(2):
        total = jnp.zeros((2 * micro * dests, quarter), F32)
        columns = slice(c * quarter, (c + 1) * quarter)
        for h in range(2):
            ref = refs[2 * h + c]
            moved = jnp.dot(swap, ref[:TILE].reshape(TILE * dests, quarter), preferred_element_type=F32)
            moved = moved.reshape(dests, TILE, quarter).astype(BF16)
            out_ref[:, h * TILE : (h + 1) * TILE, columns] = moved
            pick = ((in_row == source) & (within // micro == h)).astype(BF16)
            rows = ref[TILE:].reshape(micro * dests, quarter)
            total = total + jnp.dot(pick, rows, preferred_element_type=F32)
        out_ref[:, 2 * TILE :, columns] = total.reshape(dests, 2 * micro, quarter).astype(BF16)


def tail_pack(blocks):
    kept, dests, quarter = blocks[0].shape
    return pl.pallas_call(
        tail_pack_kernel,
        out_shape=jax.ShapeDtypeStruct((dests, 2 * TILE + 2 * (kept - TILE), 2 * quarter), BF16),
        compiler_params=params(40),
        name="tail_pack",
    )(*blocks)


def late_kernel(p_ref, main_ref, last_ref, *out_refs):
    step = pl.program_id(0)
    for j in range(len(out_refs)):

        @pl.when(step == j)
        def _():
            out_refs[j][:TILE] = main_ref[0]
            out_refs[j][TILE:] = last_ref[:, 0]


def late_blocks(p, grads, sections):
    micro, cap, dests, width = grads.shape
    quarter = width // sections
    shape = (TILE + micro, dests, quarter)
    return pl.pallas_call(
        late_kernel,
        grid_spec=pltpu.PrefetchScalarGridSpec(
            num_scalar_prefetch=1,
            grid=(sections,),
            in_specs=[
                pl.BlockSpec(
                    (1, TILE, dests, quarter),
                    lambda j, p: (micro - 1, 0, 0, (p[0] - j) & (sections - 1)),
                ),
                pl.BlockSpec(
                    (micro, 1, dests, quarter),
                    lambda j, p: (0, cap - 1, 0, (p[0] - j) & (sections - 1)),
                ),
            ],
            out_specs=[pl.BlockSpec(shape, lambda j, p: (0, 0, 0))] * sections,
        ),
        out_shape=[jax.ShapeDtypeStruct(shape, BF16)] * sections,
        compiler_params=params(32),
        name="late_blocks",
    )(p, grads, grads)


def gate_kernel(micro, normed_ref, w_ref, routes_ref, info_ref, near_ref):
    logits = lax.dot_general(w_ref[...], normed_ref[...], NT, preferred_element_type=F32)
    experts, tokens = logits.shape
    rows = tokens // micro
    expl = jnp.exp(logits)
    probs = expl / jnp.sum(expl, axis=0, keepdims=True)
    ids = lax.broadcasted_iota(jnp.int32, (experts, tokens), 0)
    first, second = iotas((tokens, tokens))
    lane = lax.broadcasted_iota(jnp.int32, (1, tokens), 1)
    block = jnp.zeros((1, tokens), jnp.int32)
    same = first >= 0
    for m in range(1, micro):
        block = block + (lane >= m * rows).astype(jnp.int32)
        same = same & ((first >= m * rows) == (second >= m * rows))
    earlier = ((first < second) & same).astype(BF16)
    named = [ids == routes_ref[k : k + 1, :] for k in range(2)]
    both = jnp.where(named[0] | named[1], 1.0, 0.0).astype(BF16)
    before = jnp.dot(both, earlier, preferred_element_type=F32)
    found = []
    gates = []
    places = []
    for k in range(2):
        gate = jnp.sum(jnp.where(named[k], probs, 0.0), axis=0, keepdims=True)
        found.append(gate * (jnp.where(named[k], 1.0, 0.0) - probs))
        gates.append(gate)
        slot = jnp.sum(jnp.where(named[k], before, 0.0), axis=0, keepdims=True).astype(jnp.int32)
        expert = routes_ref[k : k + 1, :]
        place = jnp.where(slot < TILE, expert * TILE + slot, experts * TILE + block * experts + expert)
        places.append(place.astype(F32))
    near = jnp.concatenate(gates + places + [jnp.zeros((4, tokens), F32)], axis=0)
    info_ref[...] = jnp.concatenate(found + [near], axis=0)
    for m in range(micro):
        part = near[:, m * rows : (m + 1) * rows]
        near_ref[m, :, :rows] = part
        near_ref[m, :, rows:] = part


def gate_info(normed, w, routes, micro):
    tokens, width = normed.shape
    experts = w.shape[0]
    return pl.pallas_call(
        functools.partial(gate_kernel, micro),
        out_shape=[
            jax.ShapeDtypeStruct((2 * experts + 8, tokens), F32),
            jax.ShapeDtypeStruct((micro, 8, 2 * tokens // micro), F32),
        ],
        compiler_params=params(32),
        name="gates",
    )(normed, w, routes)


def pairs(sections):
    found = []
    for s in range(sections - 1):
        for k in range(2):
            for upper in range(s + 1, sections):
                for k2 in range(2):
                    found.append((s, k, upper, k2))
    return {key: row for row, key in enumerate(found)}


def couple_kernel(p_ref, saved_ref, w_ref, info_ref, out_ref):
    p = p_ref[0]
    sections, experts, quarter = w_ref.shape
    tokens = saved_ref.shape[2]
    table = pairs(sections)
    for s in range(sections - 1):
        j = (s - p) & (sections - 1)
        for k in range(2):
            saved = saved_ref[j, k]
            for upper in range(s + 1, sections):
                j2 = (upper - p) & (sections - 1)
                part = lax.dot_general(w_ref[j2], saved, NT, preferred_element_type=F32)
                for k2 in range(2):
                    row = table[(s, k, upper, k2)]
                    v = info_ref[j2, k2 * experts : (k2 + 1) * experts, :]
                    out_ref[row : row + 1, :] = jnp.sum(part * v, axis=0, keepdims=True)


SCALAR = pl.BlockSpec(memory_space=pltpu.MemorySpace.SMEM)
WHOLE = pl.BlockSpec(memory_space=pltpu.MemorySpace.VMEM)
STAYS = pl.BlockSpec(memory_space=pl.ANY)


def coupling(p, saved, w, info):
    sections, _, tokens, _ = saved.shape
    return pl.pallas_call(
        couple_kernel,
        in_specs=[SCALAR, WHOLE, WHOLE, WHOLE],
        out_specs=WHOLE,
        out_shape=jax.ShapeDtypeStruct((len(pairs(sections)), tokens), F32),
        compiler_params=params(32),
        name="coupling",
    )(p, saved, w, info)


def picked(gates, places, first, received):
    n = received.shape[0]
    lanes = gates[0].shape[1]
    index, lane = iotas((n, lanes))
    pick = jnp.zeros((n, lanes), F32)
    for k in range(2):
        pick = pick + jnp.where(index + first == places[k], gates[k], 0.0)
    high = pick.astype(BF16).astype(F32)
    pick = jnp.where(lane >= lanes // 2, pick - high, high).astype(BF16)
    both = lax.dot_general(pick, received, TN, preferred_element_type=F32)
    return both[: lanes // 2] + both[lanes // 2 :]


def lead_kernel(main_ref, near_ref, out_ref):
    experts, _, half = main_ref.shape
    received = main_ref[...].reshape(experts * TILE, half)
    gates = [near_ref[0, k : k + 1, :] for k in range(2)]
    places = [near_ref[0, 2 + k : 3 + k, :].astype(jnp.int32) for k in range(2)]
    total = picked(gates, places, 0, received).astype(BF16)
    out_ref[0, 0] = total[:, : half // 2]
    out_ref[1, 0] = total[:, half // 2 :]


def lead_combine(received, near):
    experts, packed, half = received.shape
    count = packed // (2 * TILE)
    rows = near.shape[2] // 2
    return pl.pallas_call(
        lead_kernel,
        grid=(2, count),
        in_specs=[
            pl.BlockSpec((experts, TILE, half), lambda h, m: (0, 2 * m + h, 0)),
            pl.BlockSpec((1,) + near.shape[1:], lambda h, m: (m, 0, 0)),
        ],
        out_specs=pl.BlockSpec((2, 1, rows, half // 2), lambda h, m: (h, m, 0, 0)),
        out_shape=jax.ShapeDtypeStruct((4, count, rows, half // 2), BF16),
        compiler_params=params(40),
        name="lead_combine",
    )(received, near)


def tail_kernel(
    p_ref, received_ref, info_ref, up_ref, lead_ref, saved_ref, links_ref,
    back_ref, sent_ref, block_ref, last_ref, sum_ref, sems,
):
    p = p_ref[0]
    sections, rows, quarter = sum_ref.shape
    _, experts, _, half = block_ref.shape
    micro = up_ref.shape[0]
    n = experts * TILE
    copies = [
        pltpu.make_async_copy(
            received_ref.at[:, pl.ds(TILE * unit, TILE), :], block_ref.at[unit], sems.at[unit]
        )
        for unit in range(3)
    ]
    copies[2].start()
    copies[0].start()
    copies[1].start()
    out_row, in_row = iotas((n, n))
    order = (in_row == (out_row % experts) * TILE + out_row // experts).astype(BF16)
    lane = lax.broadcasted_iota(jnp.int32, (rows, 128), 1)
    row, column = iotas((2 * sections, 128))
    eye = (row == column).astype(F32)
    copies[2].wait()
    last = block_ref[2].reshape(n, half)
    last_ref[...] = jnp.dot(order, last, preferred_element_type=F32).astype(BF16)
    for m in range(micro):
        if m == micro - 1:
            copies[0].wait()
            copies[1].wait()
        for j in range(sections):
            h, c = divmod(j, 2)
            columns = slice(c * quarter, (c + 1) * quarter)
            facts = info_ref[j, 2 * experts :, m * rows : (m + 1) * rows]
            facts = jnp.concatenate([facts, facts], axis=1)
            gates = [facts[k : k + 1] for k in range(2)]
            places = [facts[2 + k : 3 + k].astype(jnp.int32) for k in range(2)]
            start = (h * micro + m) * experts
            total = picked(gates, places, n + m * experts, last_ref[start : start + experts, columns])
            if m == micro - 1:
                main = block_ref[h, :, :, columns].reshape(n, quarter)
                total = total + picked(gates, places, 0, main)
            else:
                total = total + lead_ref[j, m].astype(F32)
            sum_ref[j] = total
            back_ref[j, m] = total.astype(BF16)
        base = up_ref[m].astype(F32)
        dots = jnp.zeros((rows, 128), F32)
        for s in reversed(range(sections)):
            j = (s - p) & (sections - 1)
            for k in range(2):
                product = base * saved_ref[j, k, m * rows : (m + 1) * rows, :].astype(F32)
                part = product[:, :128]
                for t in range(1, quarter // 128):
                    part = part + product[:, t * 128 : (t + 1) * 128]
                part = jnp.sum(part, axis=1, keepdims=True)
                dots = jnp.where(lane == 2 * s + k, part, dots)
            if s > 0:
                base = base + sum_ref[j]
        dots = lax.dot_general(
            eye, dots, NT, precision=lax.Precision.HIGHEST, preferred_element_type=F32
        )
        for dest in range(sections):
            sent_ref[dest, : 2 * sections, m * rows : (m + 1) * rows] = dots
    for dest in range(sections):
        sent_ref[dest, 2 * sections :, :] = links_ref[...]


def tail_combine(p, received, info, upstream, lead, saved, links):
    sections, _, tokens, quarter = saved.shape
    micro, rows, _ = upstream.shape
    experts, packed, half = received.shape
    return pl.pallas_call(
        tail_kernel,
        in_specs=[SCALAR, STAYS] + [WHOLE] * 5,
        out_specs=[WHOLE] * 2,
        out_shape=[
            jax.ShapeDtypeStruct((sections, micro, rows, quarter), BF16),
            jax.ShapeDtypeStruct((sections, 2 * sections + links.shape[0], tokens), F32),
        ],
        scratch_shapes=[
            pltpu.VMEM((3, experts, TILE, half), BF16),
            pltpu.VMEM((experts * TILE, half), BF16),
            pltpu.VMEM((sections, rows, quarter), F32),
            pltpu.SemaphoreType.DMA((3,)),
        ],
        compiler_params=params(48),
        name="tail_combine",
    )(p, received, info, upstream, lead, saved, links)


def dense_kernel(micro, p_ref, sent_ref, info_ref, normed_ref, dense_ref, part_ref, rows_ref, sem):
    copy = pltpu.make_async_copy(normed_ref, rows_ref, sem)
    copy.start()
    p = p_ref[0]
    sections = sent_ref.shape[0]
    tokens, width = rows_ref.shape
    experts = (info_ref.shape[1] - 8) // 2
    table = pairs(sections)
    given = sent_ref[0]
    for source in range(1, sections):
        given = given + sent_ref[source]
    dots = {}
    own = jnp.zeros((experts, tokens), F32)
    for s in reversed(range(sections)):
        j = (s - p) & (sections - 1)
        dense = jnp.zeros((experts, tokens), F32)
        for k in range(2):
            value = given[2 * s + k : 2 * s + k + 1, :]
            for upper in range(s + 1, sections):
                for k2 in range(2):
                    row = 2 * sections + table[(s, k, upper, k2)]
                    value = value + given[row : row + 1, :] * dots[(upper, k2)]
            dots[(s, k)] = value
            dense = dense + value * info_ref[j, k * experts : (k + 1) * experts, :]
        dense_ref[s * experts : (s + 1) * experts, :] = dense.astype(BF16)
        own = jnp.where(p == s, dense, own)
    copy.wait()
    total = jnp.dot(own.astype(BF16), rows_ref[...], preferred_element_type=F32) * (1.0 / micro)
    cols = width // 128
    for r in range(experts // 8):
        for c in range(cols):
            tile = total[r * 8 : (r + 1) * 8, c * 128 : (c + 1) * 128]
            part_ref[r * cols + c] = tile.astype(BF16)


def dense_terms(p, sent, info, normed, micro):
    sections, _, tokens = sent.shape
    width = normed.shape[1]
    experts = (info.shape[1] - 8) // 2
    blocks = experts // 8 * (width // 128)
    return pl.pallas_call(
        functools.partial(dense_kernel, micro),
        in_specs=[SCALAR, WHOLE, WHOLE, STAYS],
        out_specs=[WHOLE] * 2,
        out_shape=[
            jax.ShapeDtypeStruct((sections * experts, tokens), BF16),
            jax.ShapeDtypeStruct((blocks, 8, 128), BF16),
        ],
        scratch_shapes=[pltpu.VMEM((tokens, width), BF16), pltpu.SemaphoreType.DMA],
        compiler_params=params(32),
        name="dense",
    )(p, sent, info, normed)


def grads_kernel(p_ref, up_ref, back_ref, dense_ref, w_ref, *refs):
    p = p_ref[0]
    outs, total_ref, turn_ref = refs[:-2], refs[-2], refs[-1]
    sections, micro, rows, quarter = back_ref.shape
    experts = w_ref.shape[1]
    total_ref[...] = up_ref[...].astype(F32)
    for s in reversed(range(sections)):
        j = (s - p) & (sections - 1)
        dense = dense_ref[s * experts : (s + 1) * experts, :]
        term = lax.dot_general(dense, w_ref[j], TN, preferred_element_type=F32)
        for m in range(micro):
            total = total_ref[m] + back_ref[j, m].astype(F32) + term[m * rows : (m + 1) * rows]
            total_ref[m] = total
            turn_ref[j, m] = total.astype(BF16)
    for j in range(sections):
        outs[j][...] = turn_ref[j]


def grads_of(p, upstream, back, dense, w):
    sections, micro, rows, quarter = back.shape
    return pl.pallas_call(
        grads_kernel,
        in_specs=[SCALAR] + [WHOLE] * 4,
        out_specs=[WHOLE] * sections,
        out_shape=[jax.ShapeDtypeStruct((micro, rows, quarter), BF16)] * sections,
        scratch_shapes=[
            pltpu.VMEM((micro, rows, quarter), F32),
            pltpu.VMEM((sections, micro, rows, quarter), BF16),
        ],
        compiler_params=params(40),
        name="grads",
    )(p, upstream, back, dense, w)


def join_kernel(p_ref, *refs):
    step = pl.program_id(0)
    out_ref = refs[-1]
    for d in range(len(refs) - 1):

        @pl.when(step == d)
        def _():
            out_ref[...] = refs[d][...]


def join(p, blocks):
    n = len(blocks)
    micro, rows, quarter = blocks[0].shape
    return pl.pallas_call(
        join_kernel,
        grid_spec=pltpu.PrefetchScalarGridSpec(
            num_scalar_prefetch=1,
            grid=(n,),
            in_specs=[pl.BlockSpec((micro, rows, quarter), lambda d, p: (0, 0, 0))] * n,
            out_specs=pl.BlockSpec((micro, rows, quarter), lambda d, p: (0, 0, (p[0] - d) & (n - 1))),
        ),
        out_shape=jax.ShapeDtypeStruct((micro, rows, n * quarter), BF16),
        compiler_params=params(32),
        name="join",
    )(p, *blocks)


def turned(block, distance):
    n = lax.axis_size("pipe")
    return lax.ppermute(block, "pipe", [(i, (i + distance) % n) for i in range(n)])


def gathered(block):
    n = lax.axis_size("pipe")
    return [block] + [turned(block, n - j) for j in range(1, n)]


def on_device(normed, saved_out, expert_grads, routes, router_weight, upstream):
    sections = lax.axis_size("pipe")
    section = lax.axis_index("pipe")
    p = section.astype(jnp.int32).reshape(1)
    _, micro, rows, width = normed.shape
    tokens = micro * rows
    quarter = width // sections
    normed = normed.reshape(tokens, width)
    w = router_weight[0].T
    experts = w.shape[0]

    def part(array, j, axis):
        return lax.dynamic_slice_in_dim(array, ((section - j) % sections) * quarter, quarter, axis)

    def spread(blocks):
        return [turned(block, sections - j) if j else block for j, block in enumerate(blocks)]

    grads = in_hbm(jnp.transpose(expert_grads[0, :, 0, 0], (0, 2, 1, 3)))
    lead = lax.all_to_all(lead_pack(grads, micro - 1), "expert", 0, 0, tiled=True)
    late = spread(late_blocks(p, grads, sections))
    info, near = gate_info(normed, w, jnp.transpose(routes[0], (2, 0, 1)).reshape(2, tokens), micro)
    info_all = jnp.stack(spread([info] * sections))
    w_all = jnp.stack(spread([part(w, j, 1) for j in range(sections)]))
    tail_send = tail_pack(late)
    saved_out, tail_send, info_all, w_all = lax.optimization_barrier(
        (saved_out, tail_send, info_all, w_all)
    )

    saved = jnp.transpose(saved_out[0], (2, 0, 1, 3))
    early = spread([part(saved[:, : micro - 1], j, 3) for j in range(sections)])
    lead, tail_send, *early = lax.optimization_barrier((lead, tail_send, *early))
    tail = lax.all_to_all(tail_send, "expert", 0, 0, tiled=True)
    rest = spread([part(saved[:, micro - 1 :], j, 3) for j in range(sections)])
    back = lead_combine(lead, near)
    lead = [
        lax.dynamic_index_in_dim(back, (section - j) % sections, 0, False) for j in range(sections)
    ]
    lead = jnp.stack(spread(lead))
    saved = jnp.concatenate([jnp.stack(early), jnp.stack(rest)], axis=2)
    saved = saved.reshape(sections, 2, tokens, quarter)
    links = coupling(p, saved, w_all, info_all)
    up = part(upstream, 0, 2)
    lead, info_all, w_all, saved, links, up = lax.optimization_barrier(
        (lead, info_all, w_all, saved, links, up)
    )
    back, sent = tail_combine(p, tail, info_all, up, lead, saved, links)
    sent = lax.all_to_all(sent, "pipe", 0, 0, tiled=True)
    dense, partial = dense_terms(p, sent, info_all, normed, micro)

    axes = ("expert", "dp")
    partial = lax.all_to_all(partial, axes, 0, 0, tiled=True)
    outs = grads_of(p, up, back, dense, w_all)
    blocks = [turned(out, d) if d else out for d, out in enumerate(outs)]
    total = jnp.sum(partial.astype(F32), axis=0, keepdims=True).astype(BF16)
    total = lax.all_to_all(jnp.broadcast_to(total, partial.shape), axes, 0, 0, tiled=True)
    total = total.astype(F32).reshape(experts // 8, width // 128, 8, 128).transpose(0, 2, 1, 3)
    router_grad = total.reshape(experts, width).T
    return (join(p, blocks)[None], router_grad[None])


def solution(mesh):
    in_specs = (
        P("pipe", None, ("expert", "dp"), None),
        P("pipe", None, ("expert", "dp"), None, None),
        P("pipe", None, "dp", "expert", None, None, None),
        P("pipe", None, ("expert", "dp"), None),
        P("pipe", None, None),
        P(None, ("expert", "dp"), None),
    )
    out_specs = (P("pipe", None, ("expert", "dp"), None), P("pipe", None, None))
    return jax.shard_map(
        on_device, mesh=mesh, in_specs=in_specs, out_specs=out_specs, check_vma=False
    )
```

```python
import functools

import jax
import jax.numpy as jnp
from jax import lax
from jax.experimental import pallas as pl
from jax.experimental.pallas import tpu as pltpu
from jax.sharding import PartitionSpec as P

F32 = jnp.float32
BF16 = jnp.bfloat16
NT = (((1,), (1,)), ((), ()))
TN = (((0,), (0,)), ((), ()))

TILE = 8


def params(mib):
    return pltpu.CompilerParams(vmem_limit_bytes=mib << 20)


def in_hbm(array):
    return pltpu.with_memory_space_constraint(array, pltpu.MemorySpace.HBM)


def iotas(shape):
    return [lax.broadcasted_iota(jnp.int32, shape, d) for d in range(2)]


def swap_matrix(slots, dests):
    out_row, in_row = iotas((slots * dests, slots * dests))
    return (in_row == (out_row % slots) * dests + out_row // slots).astype(BF16)


def lead_pack_kernel(grads_ref, out_ref):
    _, slots, dests, width = grads_ref.shape
    half = width // 2
    swap = swap_matrix(slots, dests)
    for h in range(2):
        rows = grads_ref[0, :, :, h * half : (h + 1) * half].reshape(slots * dests, half)
        moved = jnp.dot(swap, rows, preferred_element_type=F32)
        out_ref[:, h * slots : (h + 1) * slots, :] = moved.reshape(dests, slots, half).astype(BF16)


def lead_pack(grads, count):
    _, _, dests, width = grads.shape
    half = width // 2
    return pl.pallas_call(
        lead_pack_kernel,
        grid=(count,),
        in_specs=[pl.BlockSpec((1, TILE, dests, width), lambda m: (m, 0, 0, 0))],
        out_specs=pl.BlockSpec((dests, 2 * TILE, half), lambda m: (0, m, 0)),
        out_shape=pltpu.HBM((dests, 2 * TILE * count, half), BF16),
        compiler_params=params(40),
        name="lead_pack",
    )(grads)


def tail_pack_kernel(*refs):
    out_ref = refs[-1]
    kept, dests, quarter = refs[0].shape
    micro = kept - TILE
    swap = swap_matrix(TILE, dests)
    out_row, in_row = iotas((2 * micro * dests, micro * dests))
    within = out_row % (2 * micro)
    source = (within % micro) * dests + out_row // (2 * micro)
    for c in range(2):
        total = jnp.zeros((2 * micro * dests, quarter), F32)
        columns = slice(c * quarter, (c + 1) * quarter)
        for h in range(2):
            ref = refs[2 * h + c]
            moved = jnp.dot(swap, ref[:TILE].reshape(TILE * dests, quarter), preferred_element_type=F32)
            moved = moved.reshape(dests, TILE, quarter).astype(BF16)
            out_ref[:, h * TILE : (h + 1) * TILE, columns] = moved
            pick = ((in_row == source) & (within // micro == h)).astype(BF16)
            rows = ref[TILE:].reshape(micro * dests, quarter)
            total = total + jnp.dot(pick, rows, preferred_element_type=F32)
        out_ref[:, 2 * TILE :, columns] = total.reshape(dests, 2 * micro, quarter).astype(BF16)


def tail_pack(blocks):
    kept, dests, quarter = blocks[0].shape
    return pl.pallas_call(
        tail_pack_kernel,
        out_shape=jax.ShapeDtypeStruct((dests, 2 * TILE + 2 * (kept - TILE), 2 * quarter), BF16),
        compiler_params=params(40),
        name="tail_pack",
    )(*blocks)


def late_kernel(p_ref, main_ref, last_ref, *out_refs):
    step = pl.program_id(0)
    for j in range(len(out_refs)):

        @pl.when(step == j)
        def _():
            out_refs[j][:TILE] = main_ref[0]
            out_refs[j][TILE:] = last_ref[:, 0]


def late_blocks(p, grads, sections):
    micro, cap, dests, width = grads.shape
    quarter = width // sections
    shape = (TILE + micro, dests, quarter)
    return pl.pallas_call(
        late_kernel,
        grid_spec=pltpu.PrefetchScalarGridSpec(
            num_scalar_prefetch=1,
            grid=(sections,),
            in_specs=[
                pl.BlockSpec(
                    (1, TILE, dests, quarter),
                    lambda j, p: (micro - 1, 0, 0, (p[0] - j) & (sections - 1)),
                ),
                pl.BlockSpec(
                    (micro, 1, dests, quarter),
                    lambda j, p: (0, cap - 1, 0, (p[0] - j) & (sections - 1)),
                ),
            ],
            out_specs=[pl.BlockSpec(shape, lambda j, p: (0, 0, 0))] * sections,
        ),
        out_shape=[jax.ShapeDtypeStruct(shape, BF16)] * sections,
        compiler_params=params(32),
        name="late_blocks",
    )(p, grads, grads)


def gate_kernel(micro, normed_ref, w_ref, routes_ref, info_ref, near_ref):
    logits = lax.dot_general(w_ref[...], normed_ref[...], NT, preferred_element_type=F32)
    experts, tokens = logits.shape
    rows = tokens // micro
    expl = jnp.exp(logits)
    probs = expl / jnp.sum(expl, axis=0, keepdims=True)
    ids = lax.broadcasted_iota(jnp.int32, (experts, tokens), 0)
    first, second = iotas((tokens, tokens))
    lane = lax.broadcasted_iota(jnp.int32, (1, tokens), 1)
    block = jnp.zeros((1, tokens), jnp.int32)
    same = first >= 0
    for m in range(1, micro):
        block = block + (lane >= m * rows).astype(jnp.int32)
        same = same & ((first >= m * rows) == (second >= m * rows))
    earlier = ((first < second) & same).astype(BF16)
    named = [ids == routes_ref[k : k + 1, :] for k in range(2)]
    both = jnp.where(named[0] | named[1], 1.0, 0.0).astype(BF16)
    before = jnp.dot(both, earlier, preferred_element_type=F32)
    found = []
    gates = []
    places = []
    for k in range(2):
        gate = jnp.sum(jnp.where(named[k], probs, 0.0), axis=0, keepdims=True)
        found.append(gate * (jnp.where(named[k], 1.0, 0.0) - probs))
        gates.append(gate)
        slot = jnp.sum(jnp.where(named[k], before, 0.0), axis=0, keepdims=True).astype(jnp.int32)
        expert = routes_ref[k : k + 1, :]
        place = jnp.where(slot < TILE, expert * TILE + slot, experts * TILE + block * experts + expert)
        places.append(place.astype(F32))
    near = jnp.concatenate(gates + places + [jnp.zeros((4, tokens), F32)], axis=0)
    info_ref[...] = jnp.concatenate(found + [near], axis=0)
    for m in range(micro):
        part = near[:, m * rows : (m + 1) * rows]
        near_ref[m, :, :rows] = part
        near_ref[m, :, rows:] = part


def gate_info(normed, w, routes, micro):
    tokens, width = normed.shape
    experts = w.shape[0]
    return pl.pallas_call(
        functools.partial(gate_kernel, micro),
        out_shape=[
            jax.ShapeDtypeStruct((2 * experts + 8, tokens), F32),
            jax.ShapeDtypeStruct((micro, 8, 2 * tokens // micro), F32),
        ],
        compiler_params=params(32),
        name="gates",
    )(normed, w, routes)


def pairs(sections):
    found = []
    for s in range(sections - 1):
        for k in range(2):
            for upper in range(s + 1, sections):
                for k2 in range(2):
                    found.append((s, k, upper, k2))
    return {key: row for row, key in enumerate(found)}


def couple_kernel(p_ref, early_ref, rest_ref, w_ref, info_ref, out_ref):
    p = p_ref[0]
    sections, experts, quarter = w_ref.shape
    table = pairs(sections)
    start = 0
    for saved_ref in (early_ref, rest_ref):
        tokens = saved_ref.shape[2] * saved_ref.shape[3]
        lanes = slice(start, start + tokens)
        for s in range(sections - 1):
            j = (s - p) & (sections - 1)
            for k in range(2):
                saved = saved_ref[j, k].reshape(tokens, quarter)
                for upper in range(s + 1, sections):
                    j2 = (upper - p) & (sections - 1)
                    part = lax.dot_general(w_ref[j2], saved, NT, preferred_element_type=F32)
                    for k2 in range(2):
                        row = table[(s, k, upper, k2)]
                        v = info_ref[j2, k2 * experts : (k2 + 1) * experts, lanes]
                        out_ref[row : row + 1, lanes] = jnp.sum(part * v, axis=0, keepdims=True)
        start += tokens


SCALAR = pl.BlockSpec(memory_space=pltpu.MemorySpace.SMEM)
WHOLE = pl.BlockSpec(memory_space=pltpu.MemorySpace.VMEM)
STAYS = pl.BlockSpec(memory_space=pl.ANY)


def coupling(p, early, rest, w, info):
    sections = early.shape[0]
    tokens = info.shape[2]
    return pl.pallas_call(
        couple_kernel,
        in_specs=[SCALAR, WHOLE, WHOLE, WHOLE, WHOLE],
        out_specs=WHOLE,
        out_shape=jax.ShapeDtypeStruct((len(pairs(sections)), tokens), F32),
        compiler_params=params(32),
        name="coupling",
    )(p, early, rest, w, info)


def picked(gates, places, first, received):
    n = received.shape[0]
    lanes = gates[0].shape[1]
    index, lane = iotas((n, lanes))
    pick = jnp.zeros((n, lanes), F32)
    for k in range(2):
        pick = pick + jnp.where(index + first == places[k], gates[k], 0.0)
    high = pick.astype(BF16).astype(F32)
    pick = jnp.where(lane >= lanes // 2, pick - high, high).astype(BF16)
    both = lax.dot_general(pick, received, TN, preferred_element_type=F32)
    return both[: lanes // 2] + both[lanes // 2 :]


def lead_kernel(main_ref, near_ref, out_ref):
    experts, _, half = main_ref.shape
    received = main_ref[...].reshape(experts * TILE, half)
    gates = [near_ref[0, k : k + 1, :] for k in range(2)]
    places = [near_ref[0, 2 + k : 3 + k, :].astype(jnp.int32) for k in range(2)]
    total = picked(gates, places, 0, received).astype(BF16)
    out_ref[0, 0] = total[:, : half // 2]
    out_ref[1, 0] = total[:, half // 2 :]


def lead_combine(received, near):
    experts, packed, half = received.shape
    count = packed // (2 * TILE)
    rows = near.shape[2] // 2
    return pl.pallas_call(
        lead_kernel,
        grid=(2, count),
        in_specs=[
            pl.BlockSpec((experts, TILE, half), lambda h, m: (0, 2 * m + h, 0)),
            pl.BlockSpec((1,) + near.shape[1:], lambda h, m: (m, 0, 0)),
        ],
        out_specs=pl.BlockSpec((2, 1, rows, half // 2), lambda h, m: (h, m, 0, 0)),
        out_shape=jax.ShapeDtypeStruct((4, count, rows, half // 2), BF16),
        compiler_params=params(40),
        name="lead_combine",
    )(received, near)


def tail_kernel(
    p_ref, received_hbm, info_hbm, up_hbm, lead_hbm, early_hbm, rest_hbm, links_hbm, back_hbm, sent_ref,
    block_ref, info_ref, up_ref, lead_ref, saved_ref, links_ref, last_ref, sum_ref, back_ref,
    block_sems, info_sem, up_sem, links_sem, lead_sems, saved_sems, back_sems,
):
    p = p_ref[0]
    sections, rows, quarter = sum_ref.shape
    _, experts, _, half = block_ref.shape
    micro = up_ref.shape[0]
    n = experts * TILE
    blocks = [
        pltpu.make_async_copy(
            received_hbm.at[:, pl.ds(TILE * unit, TILE), :], block_ref.at[unit], block_sems.at[unit]
        )
        for unit in range(3)
    ]
    lead = [
        pltpu.make_async_copy(lead_hbm.at[:, m], lead_ref.at[m], lead_sems.at[m]) for m in range(micro - 1)
    ]
    saved = [
        pltpu.make_async_copy(early_hbm.at[:, :, m], saved_ref.at[m], saved_sems.at[m])
        for m in range(micro - 1)
    ]
    saved.append(
        pltpu.make_async_copy(rest_hbm.at[:, :, 0], saved_ref.at[micro - 1], saved_sems.at[micro - 1])
    )
    info = pltpu.make_async_copy(info_hbm, info_ref, info_sem)
    up = pltpu.make_async_copy(up_hbm, up_ref, up_sem)
    links = pltpu.make_async_copy(links_hbm, links_ref, links_sem)
    backs = [
        pltpu.make_async_copy(back_ref.at[m], back_hbm.at[:, m], back_sems.at[m]) for m in range(micro)
    ]
    for copy in [blocks[2], info, lead[0], up, saved[0], lead[1], saved[1], lead[2], saved[2]]:
        copy.start()
    for copy in [blocks[0], blocks[1], saved[3], links]:
        copy.start()
    out_row, in_row = iotas((2 * n, n))
    within = out_row % (2 * experts)
    order = in_row == (within % experts) * TILE + out_row // (2 * experts)
    order = order.astype(BF16)
    lane = lax.broadcasted_iota(jnp.int32, (rows, 128), 1)
    row, column = iotas((2 * sections, 128))
    eye = (row == column).astype(F32)
    blocks[2].wait()
    last = block_ref[2].reshape(n, half)
    last_ref[...] = jnp.dot(order, last, preferred_element_type=F32).astype(BF16)
    info.wait()
    for m in range(micro):
        if m == micro - 1:
            blocks[0].wait()
            blocks[1].wait()
        else:
            lead[m].wait()
        for j in range(sections):
            h, c = divmod(j, 2)
            columns = slice(c * quarter, (c + 1) * quarter)
            facts = info_ref[j, 2 * experts :, m * rows : (m + 1) * rows]
            gates = [facts[k : k + 1] for k in range(2)]
            places = [facts[2 + k : 3 + k].astype(jnp.int32) for k in range(2)]
            start = (h * micro + m) * 2 * experts
            pick = split_pick(gates, places, n + m * experts, experts)
            received = last_ref[start : start + 2 * experts, columns]
            total = lax.dot_general(pick, received, TN, preferred_element_type=F32)
            if m == micro - 1:
                main = block_ref[h, :, :, columns].reshape(n, quarter)
                pick = split_pick(gates, places, 0, n)
                total = total + lax.dot_general(
                    pick, jnp.concatenate([main, main], axis=0), TN, preferred_element_type=F32
                )
            else:
                total = total + lead_ref[m, j].astype(F32)
            sum_ref[j] = total
            back_ref[m, j] = total.astype(BF16)
        backs[m].start()
        if m == 0:
            up.wait()
        saved[m].wait()
        base = up_ref[m].astype(F32)
        dots = jnp.zeros((rows, 128), F32)
        for s in reversed(range(sections)):
            j = (s - p) & (sections - 1)
            for k in range(2):
                product = base * saved_ref[m, j, k].astype(F32)
                part = product[:, :128]
                for t in range(1, quarter // 128):
                    part = part + product[:, t * 128 : (t + 1) * 128]
                part = jnp.sum(part, axis=1, keepdims=True)
                dots = jnp.where(lane == 2 * s + k, part, dots)
            if s > 0:
                base = base + sum_ref[j]
        dots = lax.dot_general(
            eye, dots, NT, precision=lax.Precision.HIGHEST, preferred_element_type=F32
        )
        for dest in range(sections):
            sent_ref[dest, : 2 * sections, m * rows : (m + 1) * rows] = dots
    links.wait()
    for dest in range(sections):
        sent_ref[dest, 2 * sections :, :] = links_ref[...]
    for copy in backs:
        copy.wait()


def split_pick(gates, places, first, n):
    index = lax.broadcasted_iota(jnp.int32, (n, gates[0].shape[1]), 0) + first
    pick = jnp.zeros(index.shape, F32)
    for k in range(2):
        pick = pick + jnp.where(index == places[k], gates[k], 0.0)
    high = pick.astype(BF16).astype(F32)
    return jnp.concatenate([high, pick - high], axis=0).astype(BF16)


def tail_combine(p, received, info, upstream, lead, early, rest, links):
    sections = early.shape[0]
    micro, rows, quarter = upstream.shape
    experts, packed, half = received.shape
    part = (sections, rows, quarter)
    dma = pltpu.SemaphoreType.DMA
    return pl.pallas_call(
        tail_kernel,
        in_specs=[SCALAR] + [STAYS] * 7,
        out_specs=[STAYS, WHOLE],
        out_shape=[
            pltpu.HBM((sections, micro, rows, quarter), BF16),
            jax.ShapeDtypeStruct((sections, 2 * sections + links.shape[0], micro * rows), F32),
        ],
        scratch_shapes=[
            pltpu.VMEM((3, experts, TILE, half), BF16),
            pltpu.VMEM(info.shape, F32),
            pltpu.VMEM(upstream.shape, BF16),
            pltpu.VMEM((micro - 1,) + part, BF16),
            pltpu.VMEM((micro, sections, 2, rows, quarter), BF16),
            pltpu.VMEM(links.shape, F32),
            pltpu.VMEM((2 * experts * TILE, half), BF16),
            pltpu.VMEM(part, F32),
            pltpu.VMEM((micro,) + part, BF16),
            dma((3,)), dma, dma, dma, dma((micro - 1,)), dma((micro,)), dma((micro,)),
        ],
        compiler_params=params(48),
        name="tail_combine",
    )(p, *[in_hbm(array) for array in (received, info, upstream, lead, early, rest, links)])


def dense_kernel(
    micro, p_ref, sent_ref, info_ref, normed_hbm, dense_hbm, part_hbm, rows_ref, dense_ref, part_ref, sems
):
    copy = pltpu.make_async_copy(normed_hbm, rows_ref, sems.at[0])
    copy.start()
    p = p_ref[0]
    sections = sent_ref.shape[0]
    tokens, width = rows_ref.shape
    experts = (info_ref.shape[1] - 8) // 2
    table = pairs(sections)
    given = sent_ref[0]
    for source in range(1, sections):
        given = given + sent_ref[source]
    dots = {}
    own = jnp.zeros((experts, tokens), F32)
    for s in reversed(range(sections)):
        j = (s - p) & (sections - 1)
        dense = jnp.zeros((experts, tokens), F32)
        for k in range(2):
            value = given[2 * s + k : 2 * s + k + 1, :]
            for upper in range(s + 1, sections):
                for k2 in range(2):
                    row = 2 * sections + table[(s, k, upper, k2)]
                    value = value + given[row : row + 1, :] * dots[(upper, k2)]
            dots[(s, k)] = value
            dense = dense + value * info_ref[j, k * experts : (k + 1) * experts, :]
        dense_ref[s * experts : (s + 1) * experts, :] = dense.astype(BF16)
        own = jnp.where(p == s, dense, own)
    out_dense = pltpu.make_async_copy(dense_ref, dense_hbm, sems.at[1])
    out_dense.start()
    copy.wait()
    total = jnp.dot(own.astype(BF16), rows_ref[...], preferred_element_type=F32) * (1.0 / micro)
    cols = width // 128
    for r in range(experts // 8):
        for c in range(cols):
            tile = total[r * 8 : (r + 1) * 8, c * 128 : (c + 1) * 128]
            part_ref[r * cols + c] = tile.astype(BF16)
    out_part = pltpu.make_async_copy(part_ref, part_hbm, sems.at[2])
    out_part.start()
    out_dense.wait()
    out_part.wait()


def dense_terms(p, sent, info, normed, micro):
    sections, _, tokens = sent.shape
    width = normed.shape[1]
    experts = (info.shape[1] - 8) // 2
    dense = (sections * experts, tokens)
    part = (experts // 8 * (width // 128), 8, 128)
    return pl.pallas_call(
        functools.partial(dense_kernel, micro),
        in_specs=[SCALAR, WHOLE, WHOLE, STAYS],
        out_specs=[STAYS] * 2,
        out_shape=[jax.ShapeDtypeStruct(dense, BF16), pltpu.HBM(part, BF16)],
        scratch_shapes=[
            pltpu.VMEM((tokens, width), BF16),
            pltpu.VMEM(dense, BF16),
            pltpu.VMEM(part, BF16),
            pltpu.SemaphoreType.DMA((3,)),
        ],
        compiler_params=params(32),
        name="dense",
    )(p, sent, info, in_hbm(normed))


def grads_kernel(p_ref, up_ref, back_hbm, dense_ref, w_ref, *refs):
    outs = refs[:-5]
    back_ref, total_ref, turn_ref, back_sems, out_sems = refs[-5:]
    p = p_ref[0]
    sections, micro, rows, quarter = turn_ref.shape
    experts = w_ref.shape[1]
    copies = [
        pltpu.make_async_copy(back_hbm.at[:, m], back_ref.at[m], back_sems.at[m]) for m in range(micro)
    ]
    for copy in copies:
        copy.start()
    total_ref[...] = up_ref[...].astype(F32)
    for s in reversed(range(sections)):
        j = (s - p) & (sections - 1)
        dense = dense_ref[s * experts : (s + 1) * experts, :]
        term = lax.dot_general(dense, w_ref[j], TN, preferred_element_type=F32)
        for m in range(micro):
            if s == sections - 1:
                copies[m].wait()
            total = total_ref[m] + back_ref[m, j].astype(F32) + term[m * rows : (m + 1) * rows]
            total_ref[m] = total
            turn_ref[j, m] = total.astype(BF16)
    copies = [pltpu.make_async_copy(turn_ref.at[j], outs[j], out_sems.at[j]) for j in range(sections)]
    for copy in copies:
        copy.start()
    for copy in copies:
        copy.wait()


def grads_of(p, upstream, back, dense, w):
    sections, micro, rows, quarter = back.shape
    part = (micro, rows, quarter)
    return pl.pallas_call(
        grads_kernel,
        in_specs=[SCALAR, WHOLE, STAYS, WHOLE, WHOLE],
        out_specs=[STAYS] * sections,
        out_shape=[pltpu.HBM(part, BF16)] * sections,
        scratch_shapes=[
            pltpu.VMEM((micro, sections, rows, quarter), BF16),
            pltpu.VMEM(part, F32),
            pltpu.VMEM((sections,) + part, BF16),
            pltpu.SemaphoreType.DMA((micro,)),
            pltpu.SemaphoreType.DMA((sections,)),
        ],
        compiler_params=params(40),
        name="grads",
    )(p, upstream, in_hbm(back), dense, w)


def join_kernel(p_ref, *refs):
    step = pl.program_id(0)
    out_ref = refs[-1]
    for d in range(len(refs) - 1):

        @pl.when(step == d)
        def _():
            out_ref[...] = refs[d][...]


def join(p, blocks):
    n = len(blocks)
    micro, rows, quarter = blocks[0].shape
    return pl.pallas_call(
        join_kernel,
        grid_spec=pltpu.PrefetchScalarGridSpec(
            num_scalar_prefetch=1,
            grid=(n,),
            in_specs=[pl.BlockSpec((micro, rows, quarter), lambda d, p: (0, 0, 0))] * n,
            out_specs=pl.BlockSpec((micro, rows, quarter), lambda d, p: (0, 0, (p[0] - d) & (n - 1))),
        ),
        out_shape=jax.ShapeDtypeStruct((micro, rows, n * quarter), BF16),
        compiler_params=params(32),
        name="join",
    )(p, *blocks)


def turned(block, distance):
    n = lax.axis_size("pipe")
    return lax.ppermute(block, "pipe", [(i, (i + distance) % n) for i in range(n)])


def gathered(block):
    n = lax.axis_size("pipe")
    return [block] + [turned(block, n - j) for j in range(1, n)]


def on_device(normed, saved_out, expert_grads, routes, router_weight, upstream):
    sections = lax.axis_size("pipe")
    section = lax.axis_index("pipe")
    p = section.astype(jnp.int32).reshape(1)
    _, micro, rows, width = normed.shape
    tokens = micro * rows
    quarter = width // sections
    normed = normed.reshape(tokens, width)
    w = router_weight[0].T
    experts = w.shape[0]

    def part(array, j, axis):
        return lax.dynamic_slice_in_dim(array, ((section - j) % sections) * quarter, quarter, axis)

    def spread(blocks):
        return [turned(block, sections - j) if j else block for j, block in enumerate(blocks)]

    grads = in_hbm(jnp.transpose(expert_grads[0, :, 0, 0], (0, 2, 1, 3)))
    lead = lax.all_to_all(lead_pack(grads, micro - 1), "expert", 0, 0, tiled=True)
    late = spread(late_blocks(p, grads, sections))
    saved = jnp.transpose(saved_out[0], (2, 0, 1, 3))
    early = [part(saved[:, : micro - 1], j, 3) for j in range(sections)]
    *early, late[1], late[2], late[3] = lax.optimization_barrier((*early, *late[1:]))
    early = spread(early)
    tail_send = tail_pack(late)
    info, near = gate_info(normed, w, jnp.transpose(routes[0], (2, 0, 1)).reshape(2, tokens), micro)
    info_all = jnp.stack(spread([info] * sections))
    w_all = jnp.stack(spread([part(w, j, 1) for j in range(sections)]))

    lead, tail_send, info_all, w_all, *early = lax.optimization_barrier(
        (lead, tail_send, info_all, w_all, *early)
    )
    tail = lax.all_to_all(tail_send, "expert", 0, 0, tiled=True)
    rest = spread([part(saved[:, micro - 1 :], j, 3) for j in range(sections)])
    back = lead_combine(lead, near)
    lead = [
        lax.dynamic_index_in_dim(back, (section - j) % sections, 0, False) for j in range(sections)
    ]
    lead = jnp.stack(spread(lead))
    early = jnp.stack(early)
    rest = jnp.stack(rest)
    links = coupling(p, early, rest, w_all, info_all)
    up = part(upstream, 0, 2)
    lead, info_all, w_all, early, rest, links, up = lax.optimization_barrier(
        (lead, info_all, w_all, early, rest, links, up)
    )
    back, sent = tail_combine(p, tail, info_all, up, lead, early, rest, links)
    sent = lax.all_to_all(sent, "pipe", 0, 0, tiled=True)
    dense, partial = dense_terms(p, sent, info_all, normed, micro)

    axes = ("expert", "dp")
    partial = lax.all_to_all(partial, axes, 0, 0, tiled=True)
    outs = grads_of(p, up, back, dense, w_all)
    blocks = [turned(out, d) if d else out for d, out in enumerate(outs)]
    total = jnp.sum(partial.astype(F32), axis=0, keepdims=True).astype(BF16)
    total = lax.all_to_all(jnp.broadcast_to(total, partial.shape), axes, 0, 0, tiled=True)
    total = total.astype(F32).reshape(experts // 8, width // 128, 8, 128).transpose(0, 2, 1, 3)
    router_grad = total.reshape(experts, width).T
    blocks[0] = in_hbm(blocks[0])
    return (join(p, blocks)[None], router_grad[None])


def solution(mesh):
    in_specs = (
        P("pipe", None, ("expert", "dp"), None),
        P("pipe", None, ("expert", "dp"), None, None),
        P("pipe", None, "dp", "expert", None, None, None),
        P("pipe", None, ("expert", "dp"), None),
        P("pipe", None, None),
        P(None, ("expert", "dp"), None),
    )
    out_specs = (P("pipe", None, ("expert", "dp"), None), P("pipe", None, None))
    return jax.shard_map(
        on_device, mesh=mesh, in_specs=in_specs, out_specs=out_specs, check_vma=False
    )
```

```python
import functools

import jax
import jax.numpy as jnp
from jax import lax
from jax.experimental import pallas as pl
from jax.experimental.pallas import tpu as pltpu
from jax.sharding import PartitionSpec as P

F32 = jnp.float32
BF16 = jnp.bfloat16
NT = (((1,), (1,)), ((), ()))
TN = (((0,), (0,)), ((), ()))

TILE = 8


SCALAR = pl.BlockSpec(memory_space=pltpu.MemorySpace.SMEM)
WHOLE = pl.BlockSpec(memory_space=pltpu.MemorySpace.VMEM)
STAYS = pl.BlockSpec(memory_space=pl.ANY)


def params(mib):
    return pltpu.CompilerParams(vmem_limit_bytes=mib << 20)


def in_hbm(array):
    return pltpu.with_memory_space_constraint(array, pltpu.MemorySpace.HBM)


def iotas(shape):
    return [lax.broadcasted_iota(jnp.int32, shape, d) for d in range(2)]


def swap_matrix(slots, dests):
    out_row, in_row = iotas((slots * dests, slots * dests))
    return (in_row == (out_row % slots) * dests + out_row // slots).astype(BF16)


def lead_pack_kernel(grads_hbm, out_hbm, grads_ref, out_ref, in_sems, out_sems):
    count, slots, dests, width = grads_ref.shape
    half = width // 2
    reads = [
        pltpu.make_async_copy(grads_hbm.at[m, pl.ds(0, slots)], grads_ref.at[m], in_sems.at[m])
        for m in range(count)
    ]
    for copy in reads:
        copy.start()
    swap = swap_matrix(slots, dests)
    writes = []
    for m in range(count):
        reads[m].wait()
        for h in range(2):
            unit = 2 * m + h
            rows = grads_ref[m, :, :, h * half : (h + 1) * half].reshape(slots * dests, half)
            moved = jnp.dot(swap, rows, preferred_element_type=F32)
            out_ref[unit] = moved.reshape(dests, slots, half).astype(BF16)
            copy = pltpu.make_async_copy(
                out_ref.at[unit], out_hbm.at[:, pl.ds(unit * slots, slots), :], out_sems.at[unit]
            )
            copy.start()
            writes.append(copy)
    for copy in writes:
        copy.wait()


def lead_pack(grads, count):
    _, _, dests, width = grads.shape
    half = width // 2
    return pl.pallas_call(
        lead_pack_kernel,
        in_specs=[STAYS],
        out_specs=STAYS,
        out_shape=pltpu.HBM((dests, 2 * TILE * count, half), BF16),
        scratch_shapes=[
            pltpu.VMEM((count, TILE, dests, width), BF16),
            pltpu.VMEM((2 * count, dests, TILE, half), BF16),
            pltpu.SemaphoreType.DMA((count,)),
            pltpu.SemaphoreType.DMA((2 * count,)),
        ],
        compiler_params=params(40),
        name="lead_pack",
    )(grads)


def tail_pack_kernel(*refs):
    out_ref = refs[-1]
    kept, dests, quarter = refs[0].shape
    micro = kept - TILE
    swap = swap_matrix(TILE, dests)
    out_row, in_row = iotas((2 * micro * dests, micro * dests))
    within = out_row % (2 * micro)
    source = (within % micro) * dests + out_row // (2 * micro)
    for c in range(2):
        total = jnp.zeros((2 * micro * dests, quarter), F32)
        columns = slice(c * quarter, (c + 1) * quarter)
        for h in range(2):
            ref = refs[2 * h + c]
            moved = jnp.dot(swap, ref[:TILE].reshape(TILE * dests, quarter), preferred_element_type=F32)
            moved = moved.reshape(dests, TILE, quarter).astype(BF16)
            out_ref[:, h * TILE : (h + 1) * TILE, columns] = moved
            pick = ((in_row == source) & (within // micro == h)).astype(BF16)
            rows = ref[TILE:].reshape(micro * dests, quarter)
            total = total + jnp.dot(pick, rows, preferred_element_type=F32)
        out_ref[:, 2 * TILE :, columns] = total.reshape(dests, 2 * micro, quarter).astype(BF16)


def tail_pack(blocks):
    kept, dests, quarter = blocks[0].shape
    return pl.pallas_call(
        tail_pack_kernel,
        out_shape=jax.ShapeDtypeStruct((dests, 2 * TILE + 2 * (kept - TILE), 2 * quarter), BF16),
        compiler_params=params(40),
        name="tail_pack",
    )(*blocks)


def late_kernel(p_ref, main_ref, last_ref, *out_refs):
    step = pl.program_id(0)
    for j in range(len(out_refs)):

        @pl.when(step == j)
        def _():
            out_refs[j][:TILE] = main_ref[0]
            out_refs[j][TILE:] = last_ref[:, 0]


def late_blocks(p, grads, sections):
    micro, cap, dests, width = grads.shape
    quarter = width // sections
    shape = (TILE + micro, dests, quarter)
    return pl.pallas_call(
        late_kernel,
        grid_spec=pltpu.PrefetchScalarGridSpec(
            num_scalar_prefetch=1,
            grid=(sections,),
            in_specs=[
                pl.BlockSpec(
                    (1, TILE, dests, quarter),
                    lambda j, p: (micro - 1, 0, 0, (p[0] - j) & (sections - 1)),
                ),
                pl.BlockSpec(
                    (micro, 1, dests, quarter),
                    lambda j, p: (0, cap - 1, 0, (p[0] - j) & (sections - 1)),
                ),
            ],
            out_specs=[pl.BlockSpec(shape, lambda j, p: (0, 0, 0))] * sections,
        ),
        out_shape=[jax.ShapeDtypeStruct(shape, BF16)] * sections,
        compiler_params=params(32),
        name="late_blocks",
    )(p, grads, grads)


def gate_kernel(micro, normed_ref, w_ref, routes_ref, info_ref, near_ref):
    logits = lax.dot_general(w_ref[...], normed_ref[...], NT, preferred_element_type=F32)
    experts, tokens = logits.shape
    rows = tokens // micro
    expl = jnp.exp(logits)
    probs = expl / jnp.sum(expl, axis=0, keepdims=True)
    ids = lax.broadcasted_iota(jnp.int32, (experts, tokens), 0)
    first, second = iotas((tokens, tokens))
    lane = lax.broadcasted_iota(jnp.int32, (1, tokens), 1)
    block = jnp.zeros((1, tokens), jnp.int32)
    same = first >= 0
    for m in range(1, micro):
        block = block + (lane >= m * rows).astype(jnp.int32)
        same = same & ((first >= m * rows) == (second >= m * rows))
    earlier = ((first < second) & same).astype(BF16)
    named = [ids == routes_ref[k : k + 1, :] for k in range(2)]
    both = jnp.where(named[0] | named[1], 1.0, 0.0).astype(BF16)
    before = jnp.dot(both, earlier, preferred_element_type=F32)
    found = []
    gates = []
    places = []
    for k in range(2):
        gate = jnp.sum(jnp.where(named[k], probs, 0.0), axis=0, keepdims=True)
        found.append(gate * (jnp.where(named[k], 1.0, 0.0) - probs))
        gates.append(gate)
        slot = jnp.sum(jnp.where(named[k], before, 0.0), axis=0, keepdims=True).astype(jnp.int32)
        expert = routes_ref[k : k + 1, :]
        place = jnp.where(slot < TILE, expert * TILE + slot, experts * TILE + block * experts + expert)
        places.append(place.astype(F32))
    near = jnp.concatenate(gates + places + [jnp.zeros((4, tokens), F32)], axis=0)
    info_ref[...] = jnp.concatenate(found + [near], axis=0)
    for m in range(micro):
        part = near[:, m * rows : (m + 1) * rows]
        near_ref[m, :, :rows] = part
        near_ref[m, :, rows:] = part


def gate_info(normed, w, routes, micro):
    tokens, width = normed.shape
    experts = w.shape[0]
    return pl.pallas_call(
        functools.partial(gate_kernel, micro),
        out_shape=[
            jax.ShapeDtypeStruct((2 * experts + 8, tokens), F32),
            jax.ShapeDtypeStruct((micro, 8, 2 * tokens // micro), F32),
        ],
        compiler_params=params(32),
        name="gates",
    )(normed, w, routes)


def pairs(sections):
    found = []
    for s in range(sections - 1):
        for k in range(2):
            for upper in range(s + 1, sections):
                for k2 in range(2):
                    found.append((s, k, upper, k2))
    return {key: row for row, key in enumerate(found)}


def couple_kernel(p_ref, w_ref, info_ref, *refs):
    sections, experts, quarter = w_ref.shape
    early, rest = refs[:sections], refs[sections : 2 * sections]
    out_ref, early_ref, rest_ref, sems = refs[2 * sections :]
    copies = []
    for j in range(sections):
        copies.append(pltpu.make_async_copy(early[j], early_ref.at[j], sems.at[0, j]))
        copies.append(pltpu.make_async_copy(rest[j], rest_ref.at[j], sems.at[1, j]))
    for copy in copies:
        copy.start()
    for copy in copies:
        copy.wait()
    p = p_ref[0]
    table = pairs(sections)
    start = 0
    for saved_ref in (early_ref, rest_ref):
        tokens = saved_ref.shape[2] * saved_ref.shape[3]
        lanes = slice(start, start + tokens)
        for s in range(sections - 1):
            j = (s - p) & (sections - 1)
            for k in range(2):
                saved = saved_ref[j, k].reshape(tokens, quarter)
                for upper in range(s + 1, sections):
                    j2 = (upper - p) & (sections - 1)
                    part = lax.dot_general(w_ref[j2], saved, NT, preferred_element_type=F32)
                    for k2 in range(2):
                        row = table[(s, k, upper, k2)]
                        v = info_ref[j2, k2 * experts : (k2 + 1) * experts, lanes]
                        out_ref[row : row + 1, lanes] = jnp.sum(part * v, axis=0, keepdims=True)
        start += tokens


def coupling(p, early, rest, w, info):
    sections = len(early)
    tokens = info.shape[2]
    return pl.pallas_call(
        couple_kernel,
        in_specs=[SCALAR, WHOLE, WHOLE] + [STAYS] * (2 * sections),
        out_specs=WHOLE,
        out_shape=jax.ShapeDtypeStruct((len(pairs(sections)), tokens), F32),
        scratch_shapes=[
            pltpu.VMEM((sections,) + early[0].shape, BF16),
            pltpu.VMEM((sections,) + rest[0].shape, BF16),
            pltpu.SemaphoreType.DMA((2, sections)),
        ],
        compiler_params=params(32),
        name="coupling",
    )(p, w, info, *early, *rest)


def picked(gates, places, first, received):
    n = received.shape[0]
    lanes = gates[0].shape[1]
    index, lane = iotas((n, lanes))
    pick = jnp.zeros((n, lanes), F32)
    for k in range(2):
        pick = pick + jnp.where(index + first == places[k], gates[k], 0.0)
    high = pick.astype(BF16).astype(F32)
    pick = jnp.where(lane >= lanes // 2, pick - high, high).astype(BF16)
    both = lax.dot_general(pick, received, TN, preferred_element_type=F32)
    return both[: lanes // 2] + both[lanes // 2 :]


def lead_kernel(main_ref, near_ref, out_ref):
    experts, _, half = main_ref.shape
    received = main_ref[...].reshape(experts * TILE, half)
    gates = [near_ref[0, k : k + 1, :] for k in range(2)]
    places = [near_ref[0, 2 + k : 3 + k, :].astype(jnp.int32) for k in range(2)]
    total = picked(gates, places, 0, received).astype(BF16)
    out_ref[0, 0] = total[:, : half // 2]
    out_ref[1, 0] = total[:, half // 2 :]


def lead_combine(received, near):
    experts, packed, half = received.shape
    count = packed // (2 * TILE)
    rows = near.shape[2] // 2
    return pl.pallas_call(
        lead_kernel,
        grid=(2, count),
        in_specs=[
            pl.BlockSpec((experts, TILE, half), lambda h, m: (0, 2 * m + h, 0)),
            pl.BlockSpec((1,) + near.shape[1:], lambda h, m: (m, 0, 0)),
        ],
        out_specs=pl.BlockSpec((2, 1, rows, half // 2), lambda h, m: (h, m, 0, 0)),
        out_shape=jax.ShapeDtypeStruct((4, count, rows, half // 2), BF16),
        compiler_params=params(40),
        name="lead_combine",
    )(received, near)


def tail_kernel(p_ref, received_hbm, info_hbm, up_hbm, links_hbm, *refs):
    sections = info_hbm.shape[0]
    lead_hbm, early_hbm, rest_hbm = [refs[i * sections : (i + 1) * sections] for i in range(3)]
    back_hbm, sent_ref, block_ref, info_ref, up_ref, lead_ref, saved_ref = refs[3 * sections :][:7]
    links_ref, last_ref, sum_ref, back_ref = refs[3 * sections + 7 :][:4]
    block_sems, info_sem, up_sem, links_sem, lead_sems, saved_sems, back_sems = refs[3 * sections + 11 :]
    p = p_ref[0]
    _, rows, quarter = sum_ref.shape
    _, experts, _, half = block_ref.shape
    micro = up_ref.shape[0]
    n = experts * TILE
    blocks = [
        pltpu.make_async_copy(
            received_hbm.at[:, pl.ds(TILE * unit, TILE), :], block_ref.at[unit], block_sems.at[unit]
        )
        for unit in range(3)
    ]
    lead = [
        [
            pltpu.make_async_copy(lead_hbm[j].at[m], lead_ref.at[m, j], lead_sems.at[m, j])
            for j in range(sections)
        ]
        for m in range(micro - 1)
    ]
    saved = [
        [
            pltpu.make_async_copy(
                early_hbm[j].at[:, m] if m < micro - 1 else rest_hbm[j].at[:, 0],
                saved_ref.at[m, j],
                saved_sems.at[m, j],
            )
            for j in range(sections)
        ]
        for m in range(micro)
    ]
    info = pltpu.make_async_copy(info_hbm, info_ref, info_sem)
    up = pltpu.make_async_copy(up_hbm, up_ref, up_sem)
    links = pltpu.make_async_copy(links_hbm, links_ref, links_sem)
    backs = [
        pltpu.make_async_copy(back_ref.at[m], back_hbm.at[:, m], back_sems.at[m]) for m in range(micro)
    ]
    for copy in [blocks[2], info] + lead[0] + [up] + saved[0] + lead[1] + saved[1] + lead[2] + saved[2]:
        copy.start()
    for copy in blocks[:2] + saved[3] + [links]:
        copy.start()
    out_row, in_row = iotas((2 * n, n))
    within = out_row % (2 * experts)
    order = in_row == (within % experts) * TILE + out_row // (2 * experts)
    order = order.astype(BF16)
    lane = lax.broadcasted_iota(jnp.int32, (rows, 128), 1)
    row, column = iotas((2 * sections, 128))
    eye = (row == column).astype(F32)
    blocks[2].wait()
    last = block_ref[2].reshape(n, half)
    last_ref[...] = jnp.dot(order, last, preferred_element_type=F32).astype(BF16)
    info.wait()
    for m in range(micro):
        if m == micro - 1:
            blocks[0].wait()
            blocks[1].wait()
        for j in range(sections):
            h, c = divmod(j, 2)
            columns = slice(c * quarter, (c + 1) * quarter)
            facts = info_ref[j, 2 * experts :, m * rows : (m + 1) * rows]
            gates = [facts[k : k + 1] for k in range(2)]
            places = [facts[2 + k : 3 + k].astype(jnp.int32) for k in range(2)]
            start = (h * micro + m) * 2 * experts
            pick = split_pick(gates, places, n + m * experts, experts)
            received = last_ref[start : start + 2 * experts, columns]
            total = lax.dot_general(pick, received, TN, preferred_element_type=F32)
            if m == micro - 1:
                main = block_ref[h, :, :, columns].reshape(n, quarter)
                pick = split_pick(gates, places, 0, n)
                total = total + lax.dot_general(
                    pick, jnp.concatenate([main, main], axis=0), TN, preferred_element_type=F32
                )
            else:
                lead[m][j].wait()
                total = total + lead_ref[m, j].astype(F32)
            sum_ref[j] = total
            back_ref[m, j] = total.astype(BF16)
        backs[m].start()
        if m == 0:
            up.wait()
        for copy in saved[m]:
            copy.wait()
        base = up_ref[m].astype(F32)
        dots = jnp.zeros((rows, 128), F32)
        for s in reversed(range(sections)):
            j = (s - p) & (sections - 1)
            for k in range(2):
                product = base * saved_ref[m, j, k].astype(F32)
                part = product[:, :128]
                for t in range(1, quarter // 128):
                    part = part + product[:, t * 128 : (t + 1) * 128]
                part = jnp.sum(part, axis=1, keepdims=True)
                dots = jnp.where(lane == 2 * s + k, part, dots)
            if s > 0:
                base = base + sum_ref[j]
        dots = lax.dot_general(
            eye, dots, NT, precision=lax.Precision.HIGHEST, preferred_element_type=F32
        )
        for dest in range(sections):
            sent_ref[dest, : 2 * sections, m * rows : (m + 1) * rows] = dots
    links.wait()
    for dest in range(sections):
        sent_ref[dest, 2 * sections :, :] = links_ref[...]
    for copy in backs:
        copy.wait()


def split_pick(gates, places, first, n):
    index = lax.broadcasted_iota(jnp.int32, (n, gates[0].shape[1]), 0) + first
    pick = jnp.zeros(index.shape, F32)
    for k in range(2):
        pick = pick + jnp.where(index == places[k], gates[k], 0.0)
    high = pick.astype(BF16).astype(F32)
    return jnp.concatenate([high, pick - high], axis=0).astype(BF16)


def tail_combine(p, received, info, upstream, links, lead, early, rest):
    sections = len(early)
    micro, rows, quarter = upstream.shape
    experts, packed, half = received.shape
    part = (sections, rows, quarter)
    dma = pltpu.SemaphoreType.DMA
    operands = [received, info, upstream, links, *lead, *early, *rest]
    return pl.pallas_call(
        tail_kernel,
        in_specs=[SCALAR] + [STAYS] * len(operands),
        out_specs=[STAYS, WHOLE],
        out_shape=[
            pltpu.HBM((sections, micro, rows, quarter), BF16),
            jax.ShapeDtypeStruct((sections, 2 * sections + links.shape[0], micro * rows), F32),
        ],
        scratch_shapes=[
            pltpu.VMEM((3, experts, TILE, half), BF16),
            pltpu.VMEM(info.shape, F32),
            pltpu.VMEM(upstream.shape, BF16),
            pltpu.VMEM((micro - 1,) + part, BF16),
            pltpu.VMEM((micro, sections, 2, rows, quarter), BF16),
            pltpu.VMEM(links.shape, F32),
            pltpu.VMEM((2 * experts * TILE, half), BF16),
            pltpu.VMEM(part, F32),
            pltpu.VMEM((micro,) + part, BF16),
            dma((3,)), dma, dma, dma, dma((micro - 1, sections)), dma((micro, sections)), dma((micro,)),
        ],
        compiler_params=params(48),
        name="tail_combine",
    )(p, *[in_hbm(array) for array in operands])


def dense_kernel(
    micro, p_ref, sent_ref, info_ref, rows_ref, dense_hbm, part_hbm, dense_ref, part_ref, sems
):
    p = p_ref[0]
    sections = sent_ref.shape[0]
    tokens, width = rows_ref.shape
    experts = (info_ref.shape[1] - 8) // 2
    table = pairs(sections)
    given = sent_ref[0]
    for source in range(1, sections):
        given = given + sent_ref[source]
    dots = {}
    own = jnp.zeros((experts, tokens), F32)
    for s in reversed(range(sections)):
        j = (s - p) & (sections - 1)
        dense = jnp.zeros((experts, tokens), F32)
        for k in range(2):
            value = given[2 * s + k : 2 * s + k + 1, :]
            for upper in range(s + 1, sections):
                for k2 in range(2):
                    row = 2 * sections + table[(s, k, upper, k2)]
                    value = value + given[row : row + 1, :] * dots[(upper, k2)]
            dots[(s, k)] = value
            dense = dense + value * info_ref[j, k * experts : (k + 1) * experts, :]
        dense_ref[s * experts : (s + 1) * experts, :] = dense.astype(BF16)
        own = jnp.where(p == s, dense, own)
    out_dense = pltpu.make_async_copy(dense_ref, dense_hbm, sems.at[0])
    out_dense.start()
    total = jnp.dot(own.astype(BF16), rows_ref[...], preferred_element_type=F32) * (1.0 / micro)
    cols = width // 128
    for r in range(experts // 8):
        for c in range(cols):
            tile = total[r * 8 : (r + 1) * 8, c * 128 : (c + 1) * 128]
            part_ref[r * cols + c] = tile.astype(BF16)
    out_part = pltpu.make_async_copy(part_ref, part_hbm, sems.at[1])
    out_part.start()
    out_dense.wait()
    out_part.wait()


def dense_terms(p, sent, info, normed, micro):
    sections, _, tokens = sent.shape
    width = normed.shape[1]
    experts = (info.shape[1] - 8) // 2
    dense = (sections * experts, tokens)
    part = (experts // 8 * (width // 128), 8, 128)
    return pl.pallas_call(
        functools.partial(dense_kernel, micro),
        in_specs=[SCALAR] + [WHOLE] * 3,
        out_specs=[STAYS] * 2,
        out_shape=[pltpu.HBM(dense, BF16), pltpu.HBM(part, BF16)],
        scratch_shapes=[
            pltpu.VMEM(dense, BF16),
            pltpu.VMEM(part, BF16),
            pltpu.SemaphoreType.DMA((2,)),
        ],
        compiler_params=params(32),
        name="dense",
    )(p, sent, info, normed)


def grads_kernel(p_ref, up_ref, back_hbm, dense_ref, w_ref, *refs):
    outs = refs[:-5]
    back_ref, total_ref, turn_ref, back_sems, out_sems = refs[-5:]
    p = p_ref[0]
    sections, micro, rows, quarter = turn_ref.shape
    experts = w_ref.shape[1]
    copies = [
        pltpu.make_async_copy(back_hbm.at[:, m], back_ref.at[m], back_sems.at[m]) for m in range(micro)
    ]
    for copy in copies:
        copy.start()
    total_ref[...] = up_ref[...].astype(F32)
    for s in reversed(range(sections)):
        j = (s - p) & (sections - 1)
        dense = dense_ref[s * experts : (s + 1) * experts, :]
        term = lax.dot_general(dense, w_ref[j], TN, preferred_element_type=F32)
        for m in range(micro):
            if s == sections - 1:
                copies[m].wait()
            total = total_ref[m] + back_ref[m, j].astype(F32) + term[m * rows : (m + 1) * rows]
            total_ref[m] = total
            turn_ref[j, m] = total.astype(BF16)
    copies = [pltpu.make_async_copy(turn_ref.at[j], outs[j], out_sems.at[j]) for j in range(sections)]
    for copy in copies:
        copy.start()
    for copy in copies:
        copy.wait()


def grads_of(p, upstream, back, dense, w):
    sections, micro, rows, quarter = back.shape
    part = (micro, rows, quarter)
    return pl.pallas_call(
        grads_kernel,
        in_specs=[SCALAR, WHOLE, STAYS, WHOLE, WHOLE],
        out_specs=[STAYS] * sections,
        out_shape=[pltpu.HBM(part, BF16)] * sections,
        scratch_shapes=[
            pltpu.VMEM((micro, sections, rows, quarter), BF16),
            pltpu.VMEM(part, F32),
            pltpu.VMEM((sections,) + part, BF16),
            pltpu.SemaphoreType.DMA((micro,)),
            pltpu.SemaphoreType.DMA((sections,)),
        ],
        compiler_params=params(40),
        name="grads",
    )(p, upstream, in_hbm(back), dense, w)


def join_kernel(p_ref, *refs):
    step = pl.program_id(0)
    out_ref = refs[-1]
    for d in range(len(refs) - 1):

        @pl.when(step == d)
        def _():
            out_ref[...] = refs[d][...]


def join(p, blocks):
    n = len(blocks)
    micro, rows, quarter = blocks[0].shape
    return pl.pallas_call(
        join_kernel,
        grid_spec=pltpu.PrefetchScalarGridSpec(
            num_scalar_prefetch=1,
            grid=(n,),
            in_specs=[pl.BlockSpec((micro, rows, quarter), lambda d, p: (0, 0, 0))] * n,
            out_specs=pl.BlockSpec((micro, rows, quarter), lambda d, p: (0, 0, (p[0] - d) & (n - 1))),
        ),
        out_shape=jax.ShapeDtypeStruct((micro, rows, n * quarter), BF16),
        compiler_params=params(32),
        name="join",
    )(p, *blocks)


def turned(block, distance):
    n = lax.axis_size("pipe")
    return lax.ppermute(block, "pipe", [(i, (i + distance) % n) for i in range(n)])


def gathered(block):
    n = lax.axis_size("pipe")
    return [block] + [turned(block, n - j) for j in range(1, n)]


def on_device(normed, saved_out, expert_grads, routes, router_weight, upstream):
    sections = lax.axis_size("pipe")
    section = lax.axis_index("pipe")
    p = section.astype(jnp.int32).reshape(1)
    _, micro, rows, width = normed.shape
    tokens = micro * rows
    quarter = width // sections
    normed = normed.reshape(tokens, width)
    w = router_weight[0].T
    experts = w.shape[0]

    def part(array, j, axis):
        return lax.dynamic_slice_in_dim(array, ((section - j) % sections) * quarter, quarter, axis)

    def spread(blocks):
        return [turned(block, sections - j) if j else block for j, block in enumerate(blocks)]

    grads = in_hbm(jnp.transpose(expert_grads[0, :, 0, 0], (0, 2, 1, 3)))
    lead = lax.all_to_all(lead_pack(grads, micro - 1), "expert", 0, 0, tiled=True)
    info, near = gate_info(normed, w, jnp.transpose(routes[0], (2, 0, 1)).reshape(2, tokens), micro)
    info_all = spread([info] * sections)
    w_all = spread([part(w, j, 1) for j in range(sections)])
    late = late_blocks(p, grads, sections)
    late, info_all, w_all = lax.optimization_barrier((late, info_all, w_all))
    late = spread(late)
    info_all = jnp.stack(info_all)
    w_all = jnp.stack(w_all)
    saved = jnp.transpose(saved_out[0], (2, 0, 1, 3))
    early = [part(saved[:, : micro - 1], j, 3) for j in range(sections)]
    *early, late[1], late[2], late[3] = lax.optimization_barrier((*early, *late[1:]))
    early = spread(early)
    tail_send = tail_pack(late)
    tail_send, *early = lax.optimization_barrier((tail_send, *early))
    tail = lax.all_to_all(tail_send, "expert", 0, 0, tiled=True)
    rest = spread([part(saved[:, micro - 1 :], j, 3) for j in range(sections)])
    back = lead_combine(lead, near)
    lead = [
        lax.dynamic_index_in_dim(back, (section - j) % sections, 0, False) for j in range(sections)
    ]
    lead = spread(lead)
    links = coupling(p, early, rest, w_all, info_all)
    up = part(upstream, 0, 2)
    lead, info_all, w_all, early, rest, links, up = lax.optimization_barrier(
        (lead, info_all, w_all, early, rest, links, up)
    )
    back, sent = tail_combine(p, tail, info_all, up, links, lead, early, rest)
    sent = lax.all_to_all(sent, "pipe", 0, 0, tiled=True)
    dense, partial = dense_terms(p, sent, info_all, normed, micro)

    axes = ("expert", "dp")
    partial = lax.all_to_all(partial, axes, 0, 0, tiled=True)
    outs = grads_of(p, up, back, dense, w_all)
    blocks = [turned(out, d) if d else out for d, out in enumerate(outs)]
    total = jnp.sum(partial.astype(F32), axis=0, keepdims=True).astype(BF16)
    total = lax.all_to_all(jnp.broadcast_to(total, partial.shape), axes, 0, 0, tiled=True)
    total = total.astype(F32).reshape(experts // 8, width // 128, 8, 128).transpose(0, 2, 1, 3)
    router_grad = total.reshape(experts, width).T
    blocks[0] = in_hbm(blocks[0])
    return (join(p, blocks)[None], router_grad[None])


def solution(mesh):
    in_specs = (
        P("pipe", None, ("expert", "dp"), None),
        P("pipe", None, ("expert", "dp"), None, None),
        P("pipe", None, "dp", "expert", None, None, None),
        P("pipe", None, ("expert", "dp"), None),
        P("pipe", None, None),
        P(None, ("expert", "dp"), None),
    )
    out_specs = (P("pipe", None, ("expert", "dp"), None), P("pipe", None, None))
    return jax.shard_map(
        on_device, mesh=mesh, in_specs=in_specs, out_specs=out_specs, check_vma=False
    )
```

```python
import functools

import jax
import jax.numpy as jnp
from jax import lax
from jax.experimental import pallas as pl
from jax.experimental.pallas import tpu as pltpu
from jax.sharding import PartitionSpec as P

F32 = jnp.float32
BF16 = jnp.bfloat16
NT = (((1,), (1,)), ((), ()))
TN = (((0,), (0,)), ((), ()))

TILE = 8


SCALAR = pl.BlockSpec(memory_space=pltpu.MemorySpace.SMEM)
WHOLE = pl.BlockSpec(memory_space=pltpu.MemorySpace.VMEM)
STAYS = pl.BlockSpec(memory_space=pl.ANY)


def params(mib):
    return pltpu.CompilerParams(vmem_limit_bytes=mib << 20)


def in_hbm(array):
    return pltpu.with_memory_space_constraint(array, pltpu.MemorySpace.HBM)


def iotas(shape):
    return [lax.broadcasted_iota(jnp.int32, shape, d) for d in range(2)]


def swap_matrix(slots, dests):
    out_row, in_row = iotas((slots * dests, slots * dests))
    return (in_row == (out_row % slots) * dests + out_row // slots).astype(BF16)


def lead_pack_kernel(grads_hbm, out_hbm, grads_ref, out_ref, in_sems, out_sems):
    count, slots, dests, width = grads_ref.shape
    half = width // 2
    reads = [
        pltpu.make_async_copy(grads_hbm.at[m, pl.ds(0, slots)], grads_ref.at[m], in_sems.at[m])
        for m in range(count)
    ]
    for copy in reads:
        copy.start()
    swap = swap_matrix(slots, dests)
    writes = []
    for m in range(count):
        reads[m].wait()
        for h in range(2):
            unit = 2 * m + h
            rows = grads_ref[m, :, :, h * half : (h + 1) * half].reshape(slots * dests, half)
            moved = jnp.dot(swap, rows, preferred_element_type=F32)
            out_ref[unit] = moved.reshape(dests, slots, half).astype(BF16)
            copy = pltpu.make_async_copy(
                out_ref.at[unit], out_hbm.at[:, pl.ds(unit * slots, slots), :], out_sems.at[unit]
            )
            copy.start()
            writes.append(copy)
    for copy in writes:
        copy.wait()


def lead_pack(grads, count):
    _, _, dests, width = grads.shape
    half = width // 2
    return pl.pallas_call(
        lead_pack_kernel,
        in_specs=[STAYS],
        out_specs=STAYS,
        out_shape=pltpu.HBM((dests, 2 * TILE * count, half), BF16),
        scratch_shapes=[
            pltpu.VMEM((count, TILE, dests, width), BF16),
            pltpu.VMEM((2 * count, dests, TILE, half), BF16),
            pltpu.SemaphoreType.DMA((count,)),
            pltpu.SemaphoreType.DMA((2 * count,)),
        ],
        compiler_params=params(40),
        name="lead_pack",
    )(grads)


def tail_pack_kernel(*refs):
    out_ref = refs[-1]
    kept, dests, quarter = refs[0].shape
    micro = kept - TILE
    swap = swap_matrix(TILE, dests)
    out_row, in_row = iotas((2 * micro * dests, micro * dests))
    within = out_row % (2 * micro)
    source = (within % micro) * dests + out_row // (2 * micro)
    for c in range(2):
        total = jnp.zeros((2 * micro * dests, quarter), F32)
        columns = slice(c * quarter, (c + 1) * quarter)
        for h in range(2):
            ref = refs[2 * h + c]
            moved = jnp.dot(swap, ref[:TILE].reshape(TILE * dests, quarter), preferred_element_type=F32)
            moved = moved.reshape(dests, TILE, quarter).astype(BF16)
            out_ref[:, h * TILE : (h + 1) * TILE, columns] = moved
            pick = ((in_row == source) & (within // micro == h)).astype(BF16)
            rows = ref[TILE:].reshape(micro * dests, quarter)
            total = total + jnp.dot(pick, rows, preferred_element_type=F32)
        out_ref[:, 2 * TILE :, columns] = total.reshape(dests, 2 * micro, quarter).astype(BF16)


def tail_pack(blocks):
    kept, dests, quarter = blocks[0].shape
    return pl.pallas_call(
        tail_pack_kernel,
        out_shape=jax.ShapeDtypeStruct((dests, 2 * TILE + 2 * (kept - TILE), 2 * quarter), BF16),
        compiler_params=params(40),
        name="tail_pack",
    )(*blocks)


def late_kernel(p_ref, main_ref, last_ref, *out_refs):
    step = pl.program_id(0)
    for j in range(len(out_refs)):

        @pl.when(step == j)
        def _():
            out_refs[j][:TILE] = main_ref[0]
            out_refs[j][TILE:] = last_ref[:, 0]


def late_blocks(p, grads, sections):
    micro, cap, dests, width = grads.shape
    quarter = width // sections
    shape = (TILE + micro, dests, quarter)
    return pl.pallas_call(
        late_kernel,
        grid_spec=pltpu.PrefetchScalarGridSpec(
            num_scalar_prefetch=1,
            grid=(sections,),
            in_specs=[
                pl.BlockSpec(
                    (1, TILE, dests, quarter),
                    lambda j, p: (micro - 1, 0, 0, (p[0] - j) & (sections - 1)),
                ),
                pl.BlockSpec(
                    (micro, 1, dests, quarter),
                    lambda j, p: (0, cap - 1, 0, (p[0] - j) & (sections - 1)),
                ),
            ],
            out_specs=[pl.BlockSpec(shape, lambda j, p: (0, 0, 0))] * sections,
        ),
        out_shape=[jax.ShapeDtypeStruct(shape, BF16)] * sections,
        compiler_params=params(32),
        name="late_blocks",
    )(p, grads, grads)


def gate_kernel(micro, normed_ref, w_ref, routes_ref, info_ref, near_ref):
    logits = lax.dot_general(w_ref[...], normed_ref[...], NT, preferred_element_type=F32)
    experts, tokens = logits.shape
    rows = tokens // micro
    expl = jnp.exp(logits)
    probs = expl / jnp.sum(expl, axis=0, keepdims=True)
    ids = lax.broadcasted_iota(jnp.int32, (experts, tokens), 0)
    first, second = iotas((tokens, tokens))
    lane = lax.broadcasted_iota(jnp.int32, (1, tokens), 1)
    block = jnp.zeros((1, tokens), jnp.int32)
    same = first >= 0
    for m in range(1, micro):
        block = block + (lane >= m * rows).astype(jnp.int32)
        same = same & ((first >= m * rows) == (second >= m * rows))
    earlier = ((first < second) & same).astype(BF16)
    named = [ids == routes_ref[k : k + 1, :] for k in range(2)]
    both = jnp.where(named[0] | named[1], 1.0, 0.0).astype(BF16)
    before = jnp.dot(both, earlier, preferred_element_type=F32)
    found = []
    gates = []
    places = []
    for k in range(2):
        gate = jnp.sum(jnp.where(named[k], probs, 0.0), axis=0, keepdims=True)
        found.append(gate * (jnp.where(named[k], 1.0, 0.0) - probs))
        gates.append(gate)
        slot = jnp.sum(jnp.where(named[k], before, 0.0), axis=0, keepdims=True).astype(jnp.int32)
        expert = routes_ref[k : k + 1, :]
        place = jnp.where(slot < TILE, expert * TILE + slot, experts * TILE + block * experts + expert)
        places.append(place.astype(F32))
    near = jnp.concatenate(gates + places + [jnp.zeros((4, tokens), F32)], axis=0)
    info_ref[...] = jnp.concatenate(found + [near], axis=0)
    for m in range(micro):
        part = near[:, m * rows : (m + 1) * rows]
        near_ref[m, :, :rows] = part
        near_ref[m, :, rows:] = part


def gate_info(normed, w, routes, micro):
    tokens, width = normed.shape
    experts = w.shape[0]
    return pl.pallas_call(
        functools.partial(gate_kernel, micro),
        out_shape=[
            jax.ShapeDtypeStruct((2 * experts + 8, tokens), F32),
            jax.ShapeDtypeStruct((micro, 8, 2 * tokens // micro), F32),
        ],
        compiler_params=params(32),
        name="gates",
    )(normed, w, routes)


def pairs(sections):
    found = []
    for s in range(sections - 1):
        for k in range(2):
            for upper in range(s + 1, sections):
                for k2 in range(2):
                    found.append((s, k, upper, k2))
    return {key: row for row, key in enumerate(found)}


def couple_kernel(p_ref, w_ref, info_ref, *refs):
    sections, experts, quarter = w_ref.shape
    early, rest = refs[:sections], refs[sections : 2 * sections]
    out_ref, early_ref, rest_ref, sems = refs[2 * sections :]
    copies = []
    for j in range(sections):
        copies.append(pltpu.make_async_copy(early[j], early_ref.at[j], sems.at[0, j]))
        copies.append(pltpu.make_async_copy(rest[j], rest_ref.at[j], sems.at[1, j]))
    for copy in copies:
        copy.start()
    for copy in copies:
        copy.wait()
    p = p_ref[0]
    table = pairs(sections)
    start = 0
    for saved_ref in (early_ref, rest_ref):
        tokens = saved_ref.shape[2] * saved_ref.shape[3]
        lanes = slice(start, start + tokens)
        for s in range(sections - 1):
            j = (s - p) & (sections - 1)
            for k in range(2):
                saved = saved_ref[j, k].reshape(tokens, quarter)
                for upper in range(s + 1, sections):
                    j2 = (upper - p) & (sections - 1)
                    part = lax.dot_general(w_ref[j2], saved, NT, preferred_element_type=F32)
                    for k2 in range(2):
                        row = table[(s, k, upper, k2)]
                        v = info_ref[j2, k2 * experts : (k2 + 1) * experts, lanes]
                        out_ref[row : row + 1, lanes] = jnp.sum(part * v, axis=0, keepdims=True)
        start += tokens


def coupling(p, early, rest, w, info):
    sections = len(early)
    tokens = info.shape[2]
    return pl.pallas_call(
        couple_kernel,
        in_specs=[SCALAR, WHOLE, WHOLE] + [STAYS] * (2 * sections),
        out_specs=WHOLE,
        out_shape=jax.ShapeDtypeStruct((len(pairs(sections)), tokens), F32),
        scratch_shapes=[
            pltpu.VMEM((sections,) + early[0].shape, BF16),
            pltpu.VMEM((sections,) + rest[0].shape, BF16),
            pltpu.SemaphoreType.DMA((2, sections)),
        ],
        compiler_params=params(32),
        name="coupling",
    )(p, w, info, *early, *rest)


def picked(gates, places, first, received):
    n = received.shape[0]
    lanes = gates[0].shape[1]
    index, lane = iotas((n, lanes))
    pick = jnp.zeros((n, lanes), F32)
    for k in range(2):
        pick = pick + jnp.where(index + first == places[k], gates[k], 0.0)
    high = pick.astype(BF16).astype(F32)
    pick = jnp.where(lane >= lanes // 2, pick - high, high).astype(BF16)
    both = lax.dot_general(pick, received, TN, preferred_element_type=F32)
    return both[: lanes // 2] + both[lanes // 2 :]


def lead_kernel(p_ref, received_hbm, near_ref, *refs):
    outs = refs[:-4]
    block_ref, out_ref, in_sems, out_sems = refs[-4:]
    units, experts, _, half = block_ref.shape
    reads = [
        pltpu.make_async_copy(
            received_hbm.at[:, pl.ds(TILE * unit, TILE), :], block_ref.at[unit], in_sems.at[unit]
        )
        for unit in range(units)
    ]
    for copy in reads:
        copy.start()
    for unit in range(units):
        m, h = divmod(unit, 2)
        reads[unit].wait()
        received = block_ref[unit].reshape(experts * TILE, half)
        gates = [near_ref[m, k : k + 1, :] for k in range(2)]
        places = [near_ref[m, 2 + k : 3 + k, :].astype(jnp.int32) for k in range(2)]
        total = picked(gates, places, 0, received).astype(BF16)
        out_ref[2 * h, m] = total[:, : half // 2]
        out_ref[2 * h + 1, m] = total[:, half // 2 :]
    sections = len(outs)
    writes = [
        pltpu.make_async_copy(out_ref.at[(p_ref[0] - j) & (sections - 1)], outs[j], out_sems.at[j])
        for j in range(sections)
    ]
    for copy in writes:
        copy.start()
    for copy in writes:
        copy.wait()


def lead_combine(p, received, near, sections):
    experts, packed, half = received.shape
    units = packed // TILE
    part = (units // 2, near.shape[2] // 2, 2 * half // sections)
    return pl.pallas_call(
        lead_kernel,
        in_specs=[SCALAR, STAYS, WHOLE],
        out_specs=[STAYS] * sections,
        out_shape=[pltpu.HBM(part, BF16)] * sections,
        scratch_shapes=[
            pltpu.VMEM((units, experts, TILE, half), BF16),
            pltpu.VMEM((sections,) + part, BF16),
            pltpu.SemaphoreType.DMA((units,)),
            pltpu.SemaphoreType.DMA((sections,)),
        ],
        compiler_params=params(24),
        name="lead_combine",
    )(p, in_hbm(received), near)


def tail_kernel(p_ref, received_hbm, info_hbm, up_hbm, links_hbm, *refs):
    sections = info_hbm.shape[0]
    lead_hbm, early_hbm, rest_hbm = [refs[i * sections : (i + 1) * sections] for i in range(3)]
    back_hbm, sent_ref, block_ref, info_ref, up_ref, early_ref, rest_ref = refs[3 * sections :][:7]
    lead_ref, links_ref, last_ref, sum_ref, back_ref = refs[3 * sections + 7 :][:5]
    block_sems, info_sem, up_sem, links_sem, saved_sems, back_sems = refs[3 * sections + 12 :]
    p = p_ref[0]
    _, rows, quarter = sum_ref.shape
    _, experts, _, half = block_ref.shape
    micro = up_ref.shape[0]
    n = experts * TILE
    blocks = [
        pltpu.make_async_copy(
            received_hbm.at[:, pl.ds(TILE * unit, TILE), :], block_ref.at[unit], block_sems.at[unit]
        )
        for unit in range(3)
    ]
    early = [
        pltpu.make_async_copy(early_hbm[j], early_ref.at[j], saved_sems.at[0, j]) for j in range(sections)
    ]
    rest = [
        pltpu.make_async_copy(rest_hbm[j], rest_ref.at[j], saved_sems.at[1, j]) for j in range(sections)
    ]
    lead = [
        pltpu.make_async_copy(lead_hbm[j], lead_ref.at[j], saved_sems.at[2, j]) for j in range(sections)
    ]
    info = pltpu.make_async_copy(info_hbm, info_ref, info_sem)
    up = pltpu.make_async_copy(up_hbm, up_ref, up_sem)
    links = pltpu.make_async_copy(links_hbm, links_ref, links_sem)
    backs = [
        pltpu.make_async_copy(back_ref.at[m], back_hbm.at[:, m], back_sems.at[m]) for m in range(micro)
    ]
    for copy in [blocks[2], info] + lead + [up] + early + blocks[:2] + rest + [links]:
        copy.start()
    out_row, in_row = iotas((2 * n, n))
    within = out_row % (2 * experts)
    order = in_row == (within % experts) * TILE + out_row // (2 * experts)
    order = order.astype(BF16)
    lane = lax.broadcasted_iota(jnp.int32, (rows, 128), 1)
    row, column = iotas((2 * sections, 128))
    eye = (row == column).astype(F32)
    blocks[2].wait()
    last = block_ref[2].reshape(n, half)
    last_ref[...] = jnp.dot(order, last, preferred_element_type=F32).astype(BF16)
    info.wait()
    for m in range(micro):
        if m == micro - 1:
            blocks[0].wait()
            blocks[1].wait()
        for j in range(sections):
            h, c = divmod(j, 2)
            columns = slice(c * quarter, (c + 1) * quarter)
            facts = info_ref[j, 2 * experts :, m * rows : (m + 1) * rows]
            gates = [facts[k : k + 1] for k in range(2)]
            places = [facts[2 + k : 3 + k].astype(jnp.int32) for k in range(2)]
            start = (h * micro + m) * 2 * experts
            pick = split_pick(gates, places, n + m * experts, experts)
            received = last_ref[start : start + 2 * experts, columns]
            total = lax.dot_general(pick, received, TN, preferred_element_type=F32)
            if m == micro - 1:
                main = block_ref[h, :, :, columns].reshape(n, quarter)
                pick = split_pick(gates, places, 0, n)
                total = total + lax.dot_general(
                    pick, jnp.concatenate([main, main], axis=0), TN, preferred_element_type=F32
                )
            else:
                if m == 0:
                    lead[j].wait()
                total = total + lead_ref[j, m].astype(F32)
            sum_ref[j] = total
            back_ref[m, j] = total.astype(BF16)
        backs[m].start()
        if m == 0:
            up.wait()
            for copy in early:
                copy.wait()
        if m == micro - 1:
            for copy in rest:
                copy.wait()
        base = up_ref[m].astype(F32)
        dots = jnp.zeros((rows, 128), F32)
        for s in reversed(range(sections)):
            j = (s - p) & (sections - 1)
            for k in range(2):
                saved = early_ref[j, k, m] if m < micro - 1 else rest_ref[j, k, 0]
                product = base * saved.astype(F32)
                part = product[:, :128]
                for t in range(1, quarter // 128):
                    part = part + product[:, t * 128 : (t + 1) * 128]
                part = jnp.sum(part, axis=1, keepdims=True)
                dots = jnp.where(lane == 2 * s + k, part, dots)
            if s > 0:
                base = base + sum_ref[j]
        dots = lax.dot_general(
            eye, dots, NT, precision=lax.Precision.HIGHEST, preferred_element_type=F32
        )
        for dest in range(sections):
            sent_ref[dest, : 2 * sections, m * rows : (m + 1) * rows] = dots
    links.wait()
    for dest in range(sections):
        sent_ref[dest, 2 * sections :, :] = links_ref[...]
    for copy in backs:
        copy.wait()


def split_pick(gates, places, first, n):
    index = lax.broadcasted_iota(jnp.int32, (n, gates[0].shape[1]), 0) + first
    pick = jnp.zeros(index.shape, F32)
    for k in range(2):
        pick = pick + jnp.where(index == places[k], gates[k], 0.0)
    high = pick.astype(BF16).astype(F32)
    return jnp.concatenate([high, pick - high], axis=0).astype(BF16)


def tail_combine(p, received, info, upstream, links, lead, early, rest):
    sections = len(early)
    micro, rows, quarter = upstream.shape
    experts, packed, half = received.shape
    part = (sections, rows, quarter)
    dma = pltpu.SemaphoreType.DMA
    fetched = [in_hbm(array) for array in (received, info, upstream, links, *lead, *early, *rest)]
    return pl.pallas_call(
        tail_kernel,
        in_specs=[SCALAR] + [STAYS] * len(fetched),
        out_specs=[STAYS, WHOLE],
        out_shape=[
            pltpu.HBM((sections, micro, rows, quarter), BF16),
            jax.ShapeDtypeStruct((sections, 2 * sections + links.shape[0], micro * rows), F32),
        ],
        scratch_shapes=[
            pltpu.VMEM((3, experts, TILE, half), BF16),
            pltpu.VMEM(info.shape, F32),
            pltpu.VMEM(upstream.shape, BF16),
            pltpu.VMEM((sections,) + early[0].shape, BF16),
            pltpu.VMEM((sections,) + rest[0].shape, BF16),
            pltpu.VMEM((sections,) + lead[0].shape, BF16),
            pltpu.VMEM(links.shape, F32),
            pltpu.VMEM((2 * experts * TILE, half), BF16),
            pltpu.VMEM(part, F32),
            pltpu.VMEM((micro,) + part, BF16),
            dma((3,)), dma, dma, dma, dma((3, sections)), dma((micro,)),
        ],
        compiler_params=params(24),
        name="tail_combine",
    )(p, *fetched)


def dense_kernel(
    micro, p_ref, sent_ref, info_ref, rows_ref, dense_hbm, part_hbm, dense_ref, part_ref, sems
):
    p = p_ref[0]
    sections = sent_ref.shape[0]
    tokens, width = rows_ref.shape
    experts = (info_ref.shape[1] - 8) // 2
    table = pairs(sections)
    given = sent_ref[0]
    for source in range(1, sections):
        given = given + sent_ref[source]
    dots = {}
    own = jnp.zeros((experts, tokens), F32)
    for s in reversed(range(sections)):
        j = (s - p) & (sections - 1)
        dense = jnp.zeros((experts, tokens), F32)
        for k in range(2):
            value = given[2 * s + k : 2 * s + k + 1, :]
            for upper in range(s + 1, sections):
                for k2 in range(2):
                    row = 2 * sections + table[(s, k, upper, k2)]
                    value = value + given[row : row + 1, :] * dots[(upper, k2)]
            dots[(s, k)] = value
            dense = dense + value * info_ref[j, k * experts : (k + 1) * experts, :]
        dense_ref[s * experts : (s + 1) * experts, :] = dense.astype(BF16)
        own = jnp.where(p == s, dense, own)
    out_dense = pltpu.make_async_copy(dense_ref, dense_hbm, sems.at[0])
    out_dense.start()
    total = jnp.dot(own.astype(BF16), rows_ref[...], preferred_element_type=F32) * (1.0 / micro)
    cols = width // 128
    for r in range(experts // 8):
        for c in range(cols):
            tile = total[r * 8 : (r + 1) * 8, c * 128 : (c + 1) * 128]
            part_ref[r * cols + c] = tile.astype(BF16)
    out_part = pltpu.make_async_copy(part_ref, part_hbm, sems.at[1])
    out_part.start()
    out_dense.wait()
    out_part.wait()


def dense_terms(p, sent, info, normed, micro):
    sections, _, tokens = sent.shape
    width = normed.shape[1]
    experts = (info.shape[1] - 8) // 2
    dense = (sections * experts, tokens)
    part = (experts // 8 * (width // 128), 8, 128)
    return pl.pallas_call(
        functools.partial(dense_kernel, micro),
        in_specs=[SCALAR] + [WHOLE] * 3,
        out_specs=[STAYS] * 2,
        out_shape=[pltpu.HBM(dense, BF16), pltpu.HBM(part, BF16)],
        scratch_shapes=[
            pltpu.VMEM(dense, BF16),
            pltpu.VMEM(part, BF16),
            pltpu.SemaphoreType.DMA((2,)),
        ],
        compiler_params=params(32),
        name="dense",
    )(p, sent, info, normed)


def grads_kernel(p_ref, up_ref, back_hbm, dense_ref, w_ref, *refs):
    outs = refs[:-5]
    back_ref, total_ref, turn_ref, back_sems, out_sems = refs[-5:]
    p = p_ref[0]
    sections, micro, rows, quarter = turn_ref.shape
    experts = w_ref.shape[1]
    copies = [
        pltpu.make_async_copy(back_hbm.at[:, m], back_ref.at[m], back_sems.at[m]) for m in range(micro)
    ]
    for copy in copies:
        copy.start()
    total_ref[...] = up_ref[...].astype(F32)
    for s in reversed(range(sections)):
        j = (s - p) & (sections - 1)
        dense = dense_ref[s * experts : (s + 1) * experts, :]
        term = lax.dot_general(dense, w_ref[j], TN, preferred_element_type=F32)
        for m in range(micro):
            if s == sections - 1:
                copies[m].wait()
            total = total_ref[m] + back_ref[m, j].astype(F32) + term[m * rows : (m + 1) * rows]
            total_ref[m] = total
            turn_ref[j, m] = total.astype(BF16)
    copies = [pltpu.make_async_copy(turn_ref.at[j], outs[j], out_sems.at[j]) for j in range(sections)]
    for copy in copies:
        copy.start()
    for copy in copies:
        copy.wait()


def grads_of(p, upstream, back, dense, w):
    sections, micro, rows, quarter = back.shape
    part = (micro, rows, quarter)
    return pl.pallas_call(
        grads_kernel,
        in_specs=[SCALAR, WHOLE, STAYS, WHOLE, WHOLE],
        out_specs=[STAYS] * sections,
        out_shape=[pltpu.HBM(part, BF16)] * sections,
        scratch_shapes=[
            pltpu.VMEM((micro, sections, rows, quarter), BF16),
            pltpu.VMEM(part, F32),
            pltpu.VMEM((sections,) + part, BF16),
            pltpu.SemaphoreType.DMA((micro,)),
            pltpu.SemaphoreType.DMA((sections,)),
        ],
        compiler_params=params(40),
        name="grads",
    )(p, upstream, in_hbm(back), dense, w)


def total_kernel(parts_ref, out_hbm, out_ref, sem):
    total = parts_ref[0].astype(F32)
    for source in range(1, parts_ref.shape[0]):
        total = total + parts_ref[source].astype(F32)
    total = total.astype(BF16)
    for dest in range(out_ref.shape[0]):
        out_ref[dest] = total
    copy = pltpu.make_async_copy(out_ref, out_hbm, sem)
    copy.start()
    copy.wait()


def total_for_all(parts):
    return pl.pallas_call(
        total_kernel,
        in_specs=[WHOLE],
        out_specs=STAYS,
        out_shape=pltpu.HBM(parts.shape, BF16),
        scratch_shapes=[pltpu.VMEM(parts.shape, BF16), pltpu.SemaphoreType.DMA],
        compiler_params=params(8),
        name="router_total",
    )(parts)


def join_kernel(p_ref, *refs):
    step = pl.program_id(0)
    out_ref = refs[-1]
    for d in range(len(refs) - 1):

        @pl.when(step == d)
        def _():
            out_ref[...] = refs[d][...]


def join(p, blocks):
    n = len(blocks)
    micro, rows, quarter = blocks[0].shape
    return pl.pallas_call(
        join_kernel,
        grid_spec=pltpu.PrefetchScalarGridSpec(
            num_scalar_prefetch=1,
            grid=(n,),
            in_specs=[pl.BlockSpec((micro, rows, quarter), lambda d, p: (0, 0, 0))] * n,
            out_specs=pl.BlockSpec((micro, rows, quarter), lambda d, p: (0, 0, (p[0] - d) & (n - 1))),
        ),
        out_shape=jax.ShapeDtypeStruct((micro, rows, n * quarter), BF16),
        compiler_params=params(32),
        name="join",
    )(p, *blocks)


def turned(block, distance):
    n = lax.axis_size("pipe")
    return lax.ppermute(block, "pipe", [(i, (i + distance) % n) for i in range(n)])


def gathered(block):
    n = lax.axis_size("pipe")
    return [block] + [turned(block, n - j) for j in range(1, n)]


def on_device(normed, saved_out, expert_grads, routes, router_weight, upstream):
    sections = lax.axis_size("pipe")
    section = lax.axis_index("pipe")
    p = section.astype(jnp.int32).reshape(1)
    _, micro, rows, width = normed.shape
    tokens = micro * rows
    quarter = width // sections
    normed = normed.reshape(tokens, width)
    w = router_weight[0].T
    experts = w.shape[0]

    def part(array, j, axis):
        return lax.dynamic_slice_in_dim(array, ((section - j) % sections) * quarter, quarter, axis)

    def spread(blocks):
        return [turned(block, sections - j) if j else block for j, block in enumerate(blocks)]

    grads = in_hbm(jnp.transpose(expert_grads[0, :, 0, 0], (0, 2, 1, 3)))
    lead = lax.all_to_all(lead_pack(grads, micro - 1), "expert", 0, 0, tiled=True)
    info, near = gate_info(normed, w, jnp.transpose(routes[0], (2, 0, 1)).reshape(2, tokens), micro)
    info_all = spread([info] * sections)
    w_all = spread([part(w, j, 1) for j in range(sections)])
    late = late_blocks(p, grads, sections)
    late, info_all, w_all = lax.optimization_barrier((late, info_all, w_all))
    late = spread(late)
    info_all = jnp.stack(info_all)
    w_all = jnp.stack(w_all)
    saved = jnp.transpose(saved_out[0], (2, 0, 1, 3))
    early = [part(saved[:, : micro - 1], j, 3) for j in range(sections)]
    *early, late[1], late[2], late[3] = lax.optimization_barrier((*early, *late[1:]))
    early = spread(early)
    tail_send = tail_pack(late)
    tail_send, *early = lax.optimization_barrier((tail_send, *early))
    tail = lax.all_to_all(tail_send, "expert", 0, 0, tiled=True)
    rest = spread([part(saved[:, micro - 1 :], j, 3) for j in range(sections)])
    lead = spread(lead_combine(p, lead, near, sections))
    links = coupling(p, early, rest, w_all, info_all)
    up = part(upstream, 0, 2)
    lead, info_all, w_all, early, rest, links, up = lax.optimization_barrier(
        (lead, info_all, w_all, early, rest, links, up)
    )
    back, sent = tail_combine(p, tail, info_all, up, links, lead, early, rest)
    sent = lax.all_to_all(sent, "pipe", 0, 0, tiled=True)
    dense, partial = dense_terms(p, sent, info_all, normed, micro)

    axes = ("expert", "dp")
    partial = lax.all_to_all(partial, axes, 0, 0, tiled=True)
    outs = grads_of(p, up, back, dense, w_all)
    blocks = [turned(out, d) if d else out for d, out in enumerate(outs)]
    total = lax.all_to_all(total_for_all(partial), axes, 0, 0, tiled=True)
    total = total.astype(F32).reshape(experts // 8, width // 128, 8, 128).transpose(0, 2, 1, 3)
    router_grad = total.reshape(experts, width).T
    blocks[0] = in_hbm(blocks[0])
    return (join(p, blocks)[None], router_grad[None])


def solution(mesh):
    in_specs = (
        P("pipe", None, ("expert", "dp"), None),
        P("pipe", None, ("expert", "dp"), None, None),
        P("pipe", None, "dp", "expert", None, None, None),
        P("pipe", None, ("expert", "dp"), None),
        P("pipe", None, None),
        P(None, ("expert", "dp"), None),
    )
    out_specs = (P("pipe", None, ("expert", "dp"), None), P("pipe", None, None))
    return jax.shard_map(
        on_device, mesh=mesh, in_specs=in_specs, out_specs=out_specs, check_vma=False
    )
```

```python
import functools

import jax
import jax.numpy as jnp
from jax import lax
from jax.experimental import pallas as pl
from jax.experimental.pallas import tpu as pltpu
from jax.sharding import PartitionSpec as P

F32 = jnp.float32
BF16 = jnp.bfloat16
NT = (((1,), (1,)), ((), ()))
TN = (((0,), (0,)), ((), ()))

TILE = 8


SCALAR = pl.BlockSpec(memory_space=pltpu.MemorySpace.SMEM)
WHOLE = pl.BlockSpec(memory_space=pltpu.MemorySpace.VMEM)
STAYS = pl.BlockSpec(memory_space=pl.ANY)


def params(mib):
    return pltpu.CompilerParams(vmem_limit_bytes=mib << 20)


def in_hbm(array):
    return pltpu.with_memory_space_constraint(array, pltpu.MemorySpace.HBM)


def iotas(shape):
    return [lax.broadcasted_iota(jnp.int32, shape, d) for d in range(2)]


def swap_matrix(slots, dests):
    out_row, in_row = iotas((slots * dests, slots * dests))
    return (in_row == (out_row % slots) * dests + out_row // slots).astype(BF16)


def lead_pack_kernel(grads_hbm, out_hbm, grads_ref, out_ref, in_sems, out_sems):
    count, slots, dests, width = grads_ref.shape
    half = width // 2
    reads = [
        pltpu.make_async_copy(grads_hbm.at[m, pl.ds(0, slots)], grads_ref.at[m], in_sems.at[m])
        for m in range(count)
    ]
    for copy in reads:
        copy.start()
    swap = swap_matrix(slots, dests)
    writes = []
    for m in range(count):
        reads[m].wait()
        for h in range(2):
            unit = 2 * m + h
            rows = grads_ref[m, :, :, h * half : (h + 1) * half].reshape(slots * dests, half)
            moved = jnp.dot(swap, rows, preferred_element_type=F32)
            out_ref[unit] = moved.reshape(dests, slots, half).astype(BF16)
            copy = pltpu.make_async_copy(
                out_ref.at[unit], out_hbm.at[:, pl.ds(unit * slots, slots), :], out_sems.at[unit]
            )
            copy.start()
            writes.append(copy)
    for copy in writes:
        copy.wait()


def lead_pack(grads, count):
    _, _, dests, width = grads.shape
    half = width // 2
    return pl.pallas_call(
        lead_pack_kernel,
        in_specs=[STAYS],
        out_specs=STAYS,
        out_shape=pltpu.HBM((dests, 2 * TILE * count, half), BF16),
        scratch_shapes=[
            pltpu.VMEM((count, TILE, dests, width), BF16),
            pltpu.VMEM((2 * count, dests, TILE, half), BF16),
            pltpu.SemaphoreType.DMA((count,)),
            pltpu.SemaphoreType.DMA((2 * count,)),
        ],
        compiler_params=params(40),
        name="lead_pack",
    )(grads)


def tail_pack_kernel(*refs):
    out_ref = refs[-1]
    kept, dests, quarter = refs[0].shape
    micro = kept - TILE
    swap = swap_matrix(TILE, dests)
    out_row, in_row = iotas((2 * micro * dests, micro * dests))
    within = out_row % (2 * micro)
    source = (within % micro) * dests + out_row // (2 * micro)
    for c in range(2):
        total = jnp.zeros((2 * micro * dests, quarter), F32)
        columns = slice(c * quarter, (c + 1) * quarter)
        for h in range(2):
            ref = refs[2 * h + c]
            moved = jnp.dot(swap, ref[:TILE].reshape(TILE * dests, quarter), preferred_element_type=F32)
            moved = moved.reshape(dests, TILE, quarter).astype(BF16)
            out_ref[:, h * TILE : (h + 1) * TILE, columns] = moved
            pick = ((in_row == source) & (within // micro == h)).astype(BF16)
            rows = ref[TILE:].reshape(micro * dests, quarter)
            total = total + jnp.dot(pick, rows, preferred_element_type=F32)
        out_ref[:, 2 * TILE :, columns] = total.reshape(dests, 2 * micro, quarter).astype(BF16)


def tail_pack(blocks):
    kept, dests, quarter = blocks[0].shape
    return pl.pallas_call(
        tail_pack_kernel,
        out_shape=jax.ShapeDtypeStruct((dests, 2 * TILE + 2 * (kept - TILE), 2 * quarter), BF16),
        compiler_params=params(40),
        name="tail_pack",
    )(*blocks)


def late_kernel(p_ref, main_ref, last_ref, *out_refs):
    step = pl.program_id(0)
    for j in range(len(out_refs)):

        @pl.when(step == j)
        def _():
            out_refs[j][:TILE] = main_ref[0]
            out_refs[j][TILE:] = last_ref[:, 0]


def late_blocks(p, grads, sections):
    micro, cap, dests, width = grads.shape
    quarter = width // sections
    shape = (TILE + micro, dests, quarter)
    return pl.pallas_call(
        late_kernel,
        grid_spec=pltpu.PrefetchScalarGridSpec(
            num_scalar_prefetch=1,
            grid=(sections,),
            in_specs=[
                pl.BlockSpec(
                    (1, TILE, dests, quarter),
                    lambda j, p: (micro - 1, 0, 0, (p[0] - j) & (sections - 1)),
                ),
                pl.BlockSpec(
                    (micro, 1, dests, quarter),
                    lambda j, p: (0, cap - 1, 0, (p[0] - j) & (sections - 1)),
                ),
            ],
            out_specs=[pl.BlockSpec(shape, lambda j, p: (0, 0, 0))] * sections,
        ),
        out_shape=[jax.ShapeDtypeStruct(shape, BF16)] * sections,
        compiler_params=params(32),
        name="late_blocks",
    )(p, grads, grads)


def gate_kernel(micro, normed_ref, w_ref, routes_ref, info_ref, near_ref):
    logits = lax.dot_general(w_ref[...], normed_ref[...], NT, preferred_element_type=F32)
    experts, tokens = logits.shape
    rows = tokens // micro
    expl = jnp.exp(logits)
    probs = expl / jnp.sum(expl, axis=0, keepdims=True)
    ids = lax.broadcasted_iota(jnp.int32, (experts, tokens), 0)
    first, second = iotas((tokens, tokens))
    lane = lax.broadcasted_iota(jnp.int32, (1, tokens), 1)
    block = jnp.zeros((1, tokens), jnp.int32)
    same = first >= 0
    for m in range(1, micro):
        block = block + (lane >= m * rows).astype(jnp.int32)
        same = same & ((first >= m * rows) == (second >= m * rows))
    earlier = ((first < second) & same).astype(BF16)
    named = [ids == routes_ref[k : k + 1, :] for k in range(2)]
    both = jnp.where(named[0] | named[1], 1.0, 0.0).astype(BF16)
    before = jnp.dot(both, earlier, preferred_element_type=F32)
    found = []
    gates = []
    places = []
    for k in range(2):
        gate = jnp.sum(jnp.where(named[k], probs, 0.0), axis=0, keepdims=True)
        found.append(gate * (jnp.where(named[k], 1.0, 0.0) - probs))
        gates.append(gate)
        slot = jnp.sum(jnp.where(named[k], before, 0.0), axis=0, keepdims=True).astype(jnp.int32)
        expert = routes_ref[k : k + 1, :]
        place = jnp.where(slot < TILE, expert * TILE + slot, experts * TILE + block * experts + expert)
        places.append(place.astype(F32))
    near = jnp.concatenate(gates + places + [jnp.zeros((4, tokens), F32)], axis=0)
    info_ref[...] = jnp.concatenate(found + [near], axis=0)
    for m in range(micro):
        part = near[:, m * rows : (m + 1) * rows]
        near_ref[m, :, :rows] = part
        near_ref[m, :, rows:] = part


def gate_info(normed, w, routes, micro):
    tokens, width = normed.shape
    experts = w.shape[0]
    return pl.pallas_call(
        functools.partial(gate_kernel, micro),
        out_shape=[
            jax.ShapeDtypeStruct((2 * experts + 8, tokens), F32),
            jax.ShapeDtypeStruct((micro, 8, 2 * tokens // micro), F32),
        ],
        compiler_params=params(32),
        name="gates",
    )(normed, w, routes)


def pairs(sections):
    found = []
    for s in range(sections - 1):
        for k in range(2):
            for upper in range(s + 1, sections):
                for k2 in range(2):
                    found.append((s, k, upper, k2))
    return {key: row for row, key in enumerate(found)}


def couple_kernel(p_ref, w_ref, info_ref, *refs):
    sections, experts, quarter = w_ref.shape
    early, rest = refs[:sections], refs[sections : 2 * sections]
    out_ref, early_ref, rest_ref, sems = refs[2 * sections :]
    copies = []
    for j in range(sections):
        copies.append(pltpu.make_async_copy(early[j], early_ref.at[j], sems.at[0, j]))
        copies.append(pltpu.make_async_copy(rest[j], rest_ref.at[j], sems.at[1, j]))
    for copy in copies:
        copy.start()
    for copy in copies:
        copy.wait()
    p = p_ref[0]
    table = pairs(sections)
    start = 0
    for saved_ref in (early_ref, rest_ref):
        tokens = saved_ref.shape[2] * saved_ref.shape[3]
        lanes = slice(start, start + tokens)
        for s in range(sections - 1):
            j = (s - p) & (sections - 1)
            for k in range(2):
                saved = saved_ref[j, k].reshape(tokens, quarter)
                for upper in range(s + 1, sections):
                    j2 = (upper - p) & (sections - 1)
                    part = lax.dot_general(w_ref[j2], saved, NT, preferred_element_type=F32)
                    for k2 in range(2):
                        row = table[(s, k, upper, k2)]
                        v = info_ref[j2, k2 * experts : (k2 + 1) * experts, lanes]
                        out_ref[row : row + 1, lanes] = jnp.sum(part * v, axis=0, keepdims=True)
        start += tokens


def coupling(p, early, rest, w, info):
    sections = len(early)
    tokens = info.shape[2]
    return pl.pallas_call(
        couple_kernel,
        in_specs=[SCALAR, WHOLE, WHOLE] + [STAYS] * (2 * sections),
        out_specs=WHOLE,
        out_shape=jax.ShapeDtypeStruct((len(pairs(sections)), tokens), F32),
        scratch_shapes=[
            pltpu.VMEM((sections,) + early[0].shape, BF16),
            pltpu.VMEM((sections,) + rest[0].shape, BF16),
            pltpu.SemaphoreType.DMA((2, sections)),
        ],
        compiler_params=params(32),
        name="coupling",
    )(p, w, info, *early, *rest)


def picked(gates, places, first, received):
    n = received.shape[0]
    lanes = gates[0].shape[1]
    index, lane = iotas((n, lanes))
    pick = jnp.zeros((n, lanes), F32)
    for k in range(2):
        pick = pick + jnp.where(index + first == places[k], gates[k], 0.0)
    high = pick.astype(BF16).astype(F32)
    pick = jnp.where(lane >= lanes // 2, pick - high, high).astype(BF16)
    both = lax.dot_general(pick, received, TN, preferred_element_type=F32)
    return both[: lanes // 2] + both[lanes // 2 :]


def lead_kernel(p_ref, received_hbm, near_ref, *refs):
    outs = refs[:-4]
    block_ref, out_ref, in_sems, out_sems = refs[-4:]
    units, experts, _, half = block_ref.shape
    reads = [
        pltpu.make_async_copy(
            received_hbm.at[:, pl.ds(TILE * unit, TILE), :], block_ref.at[unit], in_sems.at[unit]
        )
        for unit in range(units)
    ]
    for copy in reads:
        copy.start()
    for unit in range(units):
        m, h = divmod(unit, 2)
        reads[unit].wait()
        received = block_ref[unit].reshape(experts * TILE, half)
        gates = [near_ref[m, k : k + 1, :] for k in range(2)]
        places = [near_ref[m, 2 + k : 3 + k, :].astype(jnp.int32) for k in range(2)]
        total = picked(gates, places, 0, received).astype(BF16)
        out_ref[2 * h, m] = total[:, : half // 2]
        out_ref[2 * h + 1, m] = total[:, half // 2 :]
    sections = len(outs)
    writes = [
        pltpu.make_async_copy(out_ref.at[(p_ref[0] - j) & (sections - 1)], outs[j], out_sems.at[j])
        for j in range(sections)
    ]
    for copy in writes:
        copy.start()
    for copy in writes:
        copy.wait()


def lead_combine(p, received, near, sections):
    experts, packed, half = received.shape
    units = packed // TILE
    part = (units // 2, near.shape[2] // 2, 2 * half // sections)
    return pl.pallas_call(
        lead_kernel,
        in_specs=[SCALAR, STAYS, WHOLE],
        out_specs=[STAYS] * sections,
        out_shape=[pltpu.HBM(part, BF16)] * sections,
        scratch_shapes=[
            pltpu.VMEM((units, experts, TILE, half), BF16),
            pltpu.VMEM((sections,) + part, BF16),
            pltpu.SemaphoreType.DMA((units,)),
            pltpu.SemaphoreType.DMA((sections,)),
        ],
        compiler_params=params(24),
        name="lead_combine",
    )(p, in_hbm(received), near)


def tail_kernel(p_ref, received_hbm, info_hbm, up_hbm, links_hbm, *refs):
    sections = info_hbm.shape[0]
    lead_hbm, early_hbm, rest_hbm = [refs[i * sections : (i + 1) * sections] for i in range(3)]
    back_hbm, sent_ref, block_ref, info_ref, up_ref, early_ref, rest_ref = refs[3 * sections :][:7]
    lead_ref, links_ref, last_ref, sum_ref, back_ref = refs[3 * sections + 7 :][:5]
    block_sems, info_sem, up_sem, links_sem, saved_sems, back_sems = refs[3 * sections + 12 :]
    p = p_ref[0]
    _, _, rows, quarter = sum_ref.shape
    _, experts, _, half = block_ref.shape
    micro = up_ref.shape[0]
    n = experts * TILE
    blocks = [
        pltpu.make_async_copy(
            received_hbm.at[:, pl.ds(TILE * unit, TILE), :], block_ref.at[unit], block_sems.at[unit]
        )
        for unit in range(3)
    ]
    early = [
        pltpu.make_async_copy(early_hbm[j], early_ref.at[j], saved_sems.at[0, j]) for j in range(sections)
    ]
    rest = [
        pltpu.make_async_copy(rest_hbm[j], rest_ref.at[j], saved_sems.at[1, j]) for j in range(sections)
    ]
    lead = [
        pltpu.make_async_copy(lead_hbm[j], lead_ref.at[j], saved_sems.at[2, j]) for j in range(sections)
    ]
    info = pltpu.make_async_copy(info_hbm, info_ref, info_sem)
    up = pltpu.make_async_copy(up_hbm, up_ref, up_sem)
    links = pltpu.make_async_copy(links_hbm, links_ref, links_sem)
    backs = [
        pltpu.make_async_copy(back_ref.at[m], back_hbm.at[:, m], back_sems.at[m]) for m in range(micro)
    ]
    for copy in [blocks[2], info] + lead + [up] + early + blocks[:2] + rest + [links]:
        copy.start()
    kept = micro * experts
    out_row, in_row = iotas((4 * kept, n))
    order = (out_row % experts) * TILE + out_row // (2 * kept) * micro + out_row % kept // experts
    order = (in_row == order).astype(BF16)
    lane = lax.broadcasted_iota(jnp.int32, (rows, 128), 1)
    row, column = iotas((2 * sections, 128))
    eye = (row == column).astype(F32)
    blocks[2].wait()
    last = block_ref[2].reshape(n, half)
    last_ref[...] = jnp.dot(order, last, preferred_element_type=F32).astype(BF16)
    info.wait()
    for j in range(sections):
        h, c = divmod(j, 2)
        columns = slice(c * quarter, (c + 1) * quarter)
        facts = info_ref[j, 2 * experts :, :]
        gates = [facts[k : k + 1] for k in range(2)]
        places = [facts[2 + k : 3 + k].astype(jnp.int32) for k in range(2)]
        pick = split_pick(gates, places, n, kept)
        received = last_ref[2 * h * kept : 2 * (h + 1) * kept, columns]
        total = lax.dot_general(pick, received, TN, preferred_element_type=F32)
        sum_ref[j] = total.reshape(micro, rows, quarter)
    for m in range(micro):
        if m == micro - 1:
            blocks[0].wait()
            blocks[1].wait()
        for j in range(sections):
            h, c = divmod(j, 2)
            columns = slice(c * quarter, (c + 1) * quarter)
            if m == micro - 1:
                facts = info_ref[j, 2 * experts :, m * rows : (m + 1) * rows]
                gates = [facts[k : k + 1] for k in range(2)]
                places = [facts[2 + k : 3 + k].astype(jnp.int32) for k in range(2)]
                main = block_ref[h, :, :, columns].reshape(n, quarter)
                pick = split_pick(gates, places, 0, n)
                extra = lax.dot_general(
                    pick, jnp.concatenate([main, main], axis=0), TN, preferred_element_type=F32
                )
            else:
                if m == 0:
                    lead[j].wait()
                extra = lead_ref[j, m].astype(F32)
            total = sum_ref[j, m] + extra
            sum_ref[j, m] = total
            back_ref[m, j] = total.astype(BF16)
        backs[m].start()
        if m == 0:
            up.wait()
            for copy in early:
                copy.wait()
        if m == micro - 1:
            for copy in rest:
                copy.wait()
        base = up_ref[m].astype(F32)
        dots = jnp.zeros((rows, 128), F32)
        for s in reversed(range(sections)):
            j = (s - p) & (sections - 1)
            for k in range(2):
                saved = early_ref[j, k, m] if m < micro - 1 else rest_ref[j, k, 0]
                product = base * saved.astype(F32)
                part = product[:, :128]
                for t in range(1, quarter // 128):
                    part = part + product[:, t * 128 : (t + 1) * 128]
                part = jnp.sum(part, axis=1, keepdims=True)
                dots = jnp.where(lane == 2 * s + k, part, dots)
            if s > 0:
                base = base + sum_ref[j, m]
        dots = lax.dot_general(
            eye, dots, NT, precision=lax.Precision.HIGHEST, preferred_element_type=F32
        )
        for dest in range(sections):
            sent_ref[dest, : 2 * sections, m * rows : (m + 1) * rows] = dots
    links.wait()
    for dest in range(sections):
        sent_ref[dest, 2 * sections :, :] = links_ref[...]
    for copy in backs:
        copy.wait()


def split_pick(gates, places, first, n):
    index = lax.broadcasted_iota(jnp.int32, (n, gates[0].shape[1]), 0) + first
    pick = jnp.zeros(index.shape, F32)
    for k in range(2):
        pick = pick + jnp.where(index == places[k], gates[k], 0.0)
    high = pick.astype(BF16).astype(F32)
    return jnp.concatenate([high, pick - high], axis=0).astype(BF16)


def tail_combine(p, received, info, upstream, links, lead, early, rest):
    sections = len(early)
    micro, rows, quarter = upstream.shape
    experts, packed, half = received.shape
    part = (sections, rows, quarter)
    dma = pltpu.SemaphoreType.DMA
    fetched = [in_hbm(array) for array in (received, info, upstream, links, *lead, *early, *rest)]
    return pl.pallas_call(
        tail_kernel,
        in_specs=[SCALAR] + [STAYS] * len(fetched),
        out_specs=[STAYS, WHOLE],
        out_shape=[
            pltpu.HBM((sections, micro, rows, quarter), BF16),
            jax.ShapeDtypeStruct((sections, 2 * sections + links.shape[0], micro * rows), F32),
        ],
        scratch_shapes=[
            pltpu.VMEM((3, experts, TILE, half), BF16),
            pltpu.VMEM(info.shape, F32),
            pltpu.VMEM(upstream.shape, BF16),
            pltpu.VMEM((sections,) + early[0].shape, BF16),
            pltpu.VMEM((sections,) + rest[0].shape, BF16),
            pltpu.VMEM((sections,) + lead[0].shape, BF16),
            pltpu.VMEM(links.shape, F32),
            pltpu.VMEM((4 * micro * experts, half), BF16),
            pltpu.VMEM((sections, micro, rows, quarter), F32),
            pltpu.VMEM((micro,) + part, BF16),
            dma((3,)), dma, dma, dma, dma((3, sections)), dma((micro,)),
        ],
        compiler_params=params(32),
        name="tail_combine",
    )(p, *fetched)


def dense_kernel(
    micro, p_ref, sent_ref, info_hbm, rows_ref, dense_hbm, part_hbm, info_ref, dense_ref, part_ref, sems
):
    copy = pltpu.make_async_copy(
        info_hbm.at[:, pl.ds(0, info_ref.shape[1])], info_ref, sems.at[2]
    )
    copy.start()
    p = p_ref[0]
    sections = sent_ref.shape[0]
    tokens, width = rows_ref.shape
    experts = info_ref.shape[1] // 2
    table = pairs(sections)
    given = sent_ref[0]
    for source in range(1, sections):
        given = given + sent_ref[source]
    copy.wait()
    dots = {}
    own = jnp.zeros((experts, tokens), F32)
    for s in reversed(range(sections)):
        j = (s - p) & (sections - 1)
        dense = jnp.zeros((experts, tokens), F32)
        for k in range(2):
            value = given[2 * s + k : 2 * s + k + 1, :]
            for upper in range(s + 1, sections):
                for k2 in range(2):
                    row = 2 * sections + table[(s, k, upper, k2)]
                    value = value + given[row : row + 1, :] * dots[(upper, k2)]
            dots[(s, k)] = value
            dense = dense + value * info_ref[j, k * experts : (k + 1) * experts, :]
        dense_ref[s * experts : (s + 1) * experts, :] = dense.astype(BF16)
        own = jnp.where(p == s, dense, own)
    out_dense = pltpu.make_async_copy(dense_ref, dense_hbm, sems.at[0])
    out_dense.start()
    total = jnp.dot(own.astype(BF16), rows_ref[...], preferred_element_type=F32) * (1.0 / micro)
    cols = width // 128
    for r in range(experts // 8):
        for c in range(cols):
            tile = total[r * 8 : (r + 1) * 8, c * 128 : (c + 1) * 128]
            part_ref[r * cols + c] = tile.astype(BF16)
    out_part = pltpu.make_async_copy(part_ref, part_hbm, sems.at[1])
    out_part.start()
    out_dense.wait()
    out_part.wait()


def dense_terms(p, sent, info, normed, micro):
    sections, _, tokens = sent.shape
    width = normed.shape[1]
    experts = (info.shape[1] - 8) // 2
    dense = (sections * experts, tokens)
    part = (experts // 8 * (width // 128), 8, 128)
    return pl.pallas_call(
        functools.partial(dense_kernel, micro),
        in_specs=[SCALAR, WHOLE, STAYS, WHOLE],
        out_specs=[STAYS] * 2,
        out_shape=[pltpu.HBM(dense, BF16), pltpu.HBM(part, BF16)],
        scratch_shapes=[
            pltpu.VMEM((sections, 2 * experts, tokens), F32),
            pltpu.VMEM(dense, BF16),
            pltpu.VMEM(part, BF16),
            pltpu.SemaphoreType.DMA((3,)),
        ],
        compiler_params=params(32),
        name="dense",
    )(p, sent, in_hbm(info), normed)


def grads_kernel(p_ref, up_hbm, back_hbm, dense_hbm, w_hbm, *refs):
    outs = refs[:-8]
    up_ref, dense_ref, w_ref, back_ref, total_ref, turn_ref, in_sems, out_sems = refs[-8:]
    p = p_ref[0]
    sections, micro, rows, quarter = turn_ref.shape
    experts = w_ref.shape[1]
    small = [
        pltpu.make_async_copy(source, target, in_sems.at[micro + i])
        for i, (source, target) in enumerate(
            ((up_hbm, up_ref), (dense_hbm, dense_ref), (w_hbm, w_ref))
        )
    ]
    copies = [
        pltpu.make_async_copy(back_hbm.at[:, m], back_ref.at[m], in_sems.at[m]) for m in range(micro)
    ]
    for copy in small + copies:
        copy.start()
    for copy in small:
        copy.wait()
    total_ref[...] = up_ref[...].astype(F32)
    for s in reversed(range(sections)):
        j = (s - p) & (sections - 1)
        dense = dense_ref[s * experts : (s + 1) * experts, :]
        term = lax.dot_general(dense, w_ref[j], TN, preferred_element_type=F32)
        for m in range(micro):
            if s == sections - 1:
                copies[m].wait()
            total = total_ref[m] + back_ref[m, j].astype(F32) + term[m * rows : (m + 1) * rows]
            total_ref[m] = total
            turn_ref[j, m] = total.astype(BF16)
    copies = [pltpu.make_async_copy(turn_ref.at[j], outs[j], out_sems.at[j]) for j in range(sections)]
    for copy in copies:
        copy.start()
    for copy in copies:
        copy.wait()


def grads_of(p, upstream, back, dense, w):
    sections, micro, rows, quarter = back.shape
    part = (micro, rows, quarter)
    return pl.pallas_call(
        grads_kernel,
        in_specs=[SCALAR] + [STAYS] * 4,
        out_specs=[STAYS] * sections,
        out_shape=[pltpu.HBM(part, BF16)] * sections,
        scratch_shapes=[
            pltpu.VMEM(part, BF16),
            pltpu.VMEM(dense.shape, BF16),
            pltpu.VMEM(w.shape, BF16),
            pltpu.VMEM((micro, sections, rows, quarter), BF16),
            pltpu.VMEM(part, F32),
            pltpu.VMEM((sections,) + part, BF16),
            pltpu.SemaphoreType.DMA((micro + 3,)),
            pltpu.SemaphoreType.DMA((sections,)),
        ],
        compiler_params=params(40),
        name="grads",
    )(p, *[in_hbm(array) for array in (upstream, back, dense, w)])


def total_kernel(parts_ref, out_hbm, out_ref, sem):
    total = parts_ref[0].astype(F32)
    for source in range(1, parts_ref.shape[0]):
        total = total + parts_ref[source].astype(F32)
    total = total.astype(BF16)
    for dest in range(out_ref.shape[0]):
        out_ref[dest] = total
    copy = pltpu.make_async_copy(out_ref, out_hbm, sem)
    copy.start()
    copy.wait()


def total_for_all(parts):
    return pl.pallas_call(
        total_kernel,
        in_specs=[WHOLE],
        out_specs=STAYS,
        out_shape=pltpu.HBM(parts.shape, BF16),
        scratch_shapes=[pltpu.VMEM(parts.shape, BF16), pltpu.SemaphoreType.DMA],
        compiler_params=params(8),
        name="router_total",
    )(parts)


def join_kernel(p_ref, *refs):
    step = pl.program_id(0)
    out_ref = refs[-1]
    for d in range(len(refs) - 1):

        @pl.when(step == d)
        def _():
            out_ref[...] = refs[d][...]


def join(p, blocks):
    n = len(blocks)
    micro, rows, quarter = blocks[0].shape
    return pl.pallas_call(
        join_kernel,
        grid_spec=pltpu.PrefetchScalarGridSpec(
            num_scalar_prefetch=1,
            grid=(n,),
            in_specs=[pl.BlockSpec((micro, rows, quarter), lambda d, p: (0, 0, 0))] * n,
            out_specs=pl.BlockSpec((micro, rows, quarter), lambda d, p: (0, 0, (p[0] - d) & (n - 1))),
        ),
        out_shape=jax.ShapeDtypeStruct((micro, rows, n * quarter), BF16),
        compiler_params=params(32),
        name="join",
    )(p, *blocks)


def turned(block, distance):
    n = lax.axis_size("pipe")
    return lax.ppermute(block, "pipe", [(i, (i + distance) % n) for i in range(n)])


def gathered(block):
    n = lax.axis_size("pipe")
    return [block] + [turned(block, n - j) for j in range(1, n)]


def on_device(normed, saved_out, expert_grads, routes, router_weight, upstream):
    sections = lax.axis_size("pipe")
    section = lax.axis_index("pipe")
    p = section.astype(jnp.int32).reshape(1)
    _, micro, rows, width = normed.shape
    tokens = micro * rows
    quarter = width // sections
    normed = normed.reshape(tokens, width)
    w = router_weight[0].T
    experts = w.shape[0]

    def part(array, j, axis):
        return lax.dynamic_slice_in_dim(array, ((section - j) % sections) * quarter, quarter, axis)

    def spread(blocks):
        return [turned(block, sections - j) if j else block for j, block in enumerate(blocks)]

    grads = in_hbm(jnp.transpose(expert_grads[0, :, 0, 0], (0, 2, 1, 3)))
    lead = lax.all_to_all(lead_pack(grads, micro - 1), "expert", 0, 0, tiled=True)
    info, near = gate_info(normed, w, jnp.transpose(routes[0], (2, 0, 1)).reshape(2, tokens), micro)
    info_all = spread([info] * sections)
    w_all = spread([part(w, j, 1) for j in range(sections)])
    late = late_blocks(p, grads, sections)
    late, info_all, w_all = lax.optimization_barrier((late, info_all, w_all))
    late = spread(late)
    info_all = jnp.stack(info_all)
    w_all = jnp.stack(w_all)
    saved = jnp.transpose(saved_out[0], (2, 0, 1, 3))
    early = [part(saved[:, : micro - 1], j, 3) for j in range(sections)]
    *early, late[1], late[2], late[3] = lax.optimization_barrier((*early, *late[1:]))
    early = spread(early)
    tail_send = tail_pack(late)
    tail_send, *early = lax.optimization_barrier((tail_send, *early))
    tail = lax.all_to_all(tail_send, "expert", 0, 0, tiled=True)
    rest = spread([part(saved[:, micro - 1 :], j, 3) for j in range(sections)])
    lead = spread(lead_combine(p, lead, near, sections))
    links = coupling(p, early, rest, w_all, info_all)
    up = part(upstream, 0, 2)
    lead, info_all, w_all, early, rest, links, up = lax.optimization_barrier(
        (lead, info_all, w_all, early, rest, links, up)
    )
    back, sent = tail_combine(p, tail, info_all, up, links, lead, early, rest)
    sent = lax.all_to_all(sent, "pipe", 0, 0, tiled=True)
    dense, partial = dense_terms(p, sent, info_all, normed, micro)

    axes = ("expert", "dp")
    partial = lax.all_to_all(partial, axes, 0, 0, tiled=True)
    outs = grads_of(p, up, back, dense, w_all)
    blocks = [turned(out, d) if d else out for d, out in enumerate(outs)]
    total = lax.all_to_all(total_for_all(partial), axes, 0, 0, tiled=True)
    total = total.astype(F32).reshape(experts // 8, width // 128, 8, 128).transpose(0, 2, 1, 3)
    router_grad = total.reshape(experts, width).T
    blocks[0] = in_hbm(blocks[0])
    return (join(p, blocks)[None], router_grad[None])


def solution(mesh):
    in_specs = (
        P("pipe", None, ("expert", "dp"), None),
        P("pipe", None, ("expert", "dp"), None, None),
        P("pipe", None, "dp", "expert", None, None, None),
        P("pipe", None, ("expert", "dp"), None),
        P("pipe", None, None),
        P(None, ("expert", "dp"), None),
    )
    out_specs = (P("pipe", None, ("expert", "dp"), None), P("pipe", None, None))
    return jax.shard_map(
        on_device, mesh=mesh, in_specs=in_specs, out_specs=out_specs, check_vma=False
    )
```

```python
import functools

import jax
import jax.numpy as jnp
from jax import lax
from jax.experimental import pallas as pl
from jax.experimental.pallas import tpu as pltpu
from jax.sharding import PartitionSpec as P

F32 = jnp.float32
BF16 = jnp.bfloat16
NT = (((1,), (1,)), ((), ()))
TN = (((0,), (0,)), ((), ()))

TILE = 8


SCALAR = pl.BlockSpec(memory_space=pltpu.MemorySpace.SMEM)
WHOLE = pl.BlockSpec(memory_space=pltpu.MemorySpace.VMEM)
STAYS = pl.BlockSpec(memory_space=pl.ANY)


def params(mib):
    return pltpu.CompilerParams(vmem_limit_bytes=mib << 20)


def in_hbm(array):
    return pltpu.with_memory_space_constraint(array, pltpu.MemorySpace.HBM)


def iotas(shape):
    return [lax.broadcasted_iota(jnp.int32, shape, d) for d in range(2)]


def swap_matrix(slots, dests):
    out_row, in_row = iotas((slots * dests, slots * dests))
    return (in_row == (out_row % slots) * dests + out_row // slots).astype(BF16)


def lead_pack_kernel(grads_hbm, out_hbm, grads_ref, out_ref, in_sems, out_sems):
    count, slots, dests, width = grads_ref.shape
    half = width // 2
    reads = [
        pltpu.make_async_copy(grads_hbm.at[m, pl.ds(0, slots)], grads_ref.at[m], in_sems.at[m])
        for m in range(count)
    ]
    for copy in reads:
        copy.start()
    swap = swap_matrix(slots, dests)
    writes = []
    for m in range(count):
        reads[m].wait()
        for h in range(2):
            unit = 2 * m + h
            rows = grads_ref[m, :, :, h * half : (h + 1) * half].reshape(slots * dests, half)
            moved = jnp.dot(swap, rows, preferred_element_type=F32)
            out_ref[unit] = moved.reshape(dests, slots, half).astype(BF16)
            copy = pltpu.make_async_copy(
                out_ref.at[unit], out_hbm.at[:, pl.ds(unit * slots, slots), :], out_sems.at[unit]
            )
            copy.start()
            writes.append(copy)
    for copy in writes:
        copy.wait()


def lead_pack(grads, count):
    _, _, dests, width = grads.shape
    half = width // 2
    return pl.pallas_call(
        lead_pack_kernel,
        in_specs=[STAYS],
        out_specs=STAYS,
        out_shape=pltpu.HBM((dests, 2 * TILE * count, half), BF16),
        scratch_shapes=[
            pltpu.VMEM((count, TILE, dests, width), BF16),
            pltpu.VMEM((2 * count, dests, TILE, half), BF16),
            pltpu.SemaphoreType.DMA((count,)),
            pltpu.SemaphoreType.DMA((2 * count,)),
        ],
        compiler_params=params(40),
        name="lead_pack",
    )(grads)


def tail_pack_kernel(*refs):
    out_ref = refs[-1]
    kept, dests, quarter = refs[0].shape
    micro = kept - TILE
    swap = swap_matrix(TILE, dests)
    out_row, in_row = iotas((2 * micro * dests, micro * dests))
    within = out_row % (2 * micro)
    source = (within % micro) * dests + out_row // (2 * micro)
    for c in range(2):
        total = jnp.zeros((2 * micro * dests, quarter), F32)
        columns = slice(c * quarter, (c + 1) * quarter)
        for h in range(2):
            ref = refs[2 * h + c]
            moved = jnp.dot(swap, ref[:TILE].reshape(TILE * dests, quarter), preferred_element_type=F32)
            moved = moved.reshape(dests, TILE, quarter).astype(BF16)
            out_ref[:, h * TILE : (h + 1) * TILE, columns] = moved
            pick = ((in_row == source) & (within // micro == h)).astype(BF16)
            rows = ref[TILE:].reshape(micro * dests, quarter)
            total = total + jnp.dot(pick, rows, preferred_element_type=F32)
        out_ref[:, 2 * TILE :, columns] = total.reshape(dests, 2 * micro, quarter).astype(BF16)


def tail_pack(blocks):
    kept, dests, quarter = blocks[0].shape
    return pl.pallas_call(
        tail_pack_kernel,
        out_shape=jax.ShapeDtypeStruct((dests, 2 * TILE + 2 * (kept - TILE), 2 * quarter), BF16),
        compiler_params=params(40),
        name="tail_pack",
    )(*blocks)


def late_kernel(p_ref, main_ref, last_ref, *out_refs):
    step = pl.program_id(0)
    for j in range(len(out_refs)):

        @pl.when(step == j)
        def _():
            out_refs[j][:TILE] = main_ref[0]
            out_refs[j][TILE:] = last_ref[:, 0]


def late_blocks(p, grads, sections):
    micro, cap, dests, width = grads.shape
    quarter = width // sections
    shape = (TILE + micro, dests, quarter)
    return pl.pallas_call(
        late_kernel,
        grid_spec=pltpu.PrefetchScalarGridSpec(
            num_scalar_prefetch=1,
            grid=(sections,),
            in_specs=[
                pl.BlockSpec(
                    (1, TILE, dests, quarter),
                    lambda j, p: (micro - 1, 0, 0, (p[0] - j) & (sections - 1)),
                ),
                pl.BlockSpec(
                    (micro, 1, dests, quarter),
                    lambda j, p: (0, cap - 1, 0, (p[0] - j) & (sections - 1)),
                ),
            ],
            out_specs=[pl.BlockSpec(shape, lambda j, p: (0, 0, 0))] * sections,
        ),
        out_shape=[jax.ShapeDtypeStruct(shape, BF16)] * sections,
        compiler_params=params(32),
        name="late_blocks",
    )(p, grads, grads)


def gate_kernel(micro, normed_ref, w_ref, routes_ref, info_ref, near_ref):
    logits = lax.dot_general(w_ref[...], normed_ref[...], NT, preferred_element_type=F32)
    experts, tokens = logits.shape
    rows = tokens // micro
    expl = jnp.exp(logits)
    probs = expl / jnp.sum(expl, axis=0, keepdims=True)
    ids = lax.broadcasted_iota(jnp.int32, (experts, tokens), 0)
    first, second = iotas((tokens, tokens))
    lane = lax.broadcasted_iota(jnp.int32, (1, tokens), 1)
    block = jnp.zeros((1, tokens), jnp.int32)
    same = first >= 0
    for m in range(1, micro):
        block = block + (lane >= m * rows).astype(jnp.int32)
        same = same & ((first >= m * rows) == (second >= m * rows))
    earlier = ((first < second) & same).astype(BF16)
    named = [ids == routes_ref[k : k + 1, :] for k in range(2)]
    both = jnp.where(named[0] | named[1], 1.0, 0.0).astype(BF16)
    before = jnp.dot(both, earlier, preferred_element_type=F32)
    found = []
    gates = []
    places = []
    for k in range(2):
        gate = jnp.sum(jnp.where(named[k], probs, 0.0), axis=0, keepdims=True)
        found.append(gate * (jnp.where(named[k], 1.0, 0.0) - probs))
        gates.append(gate)
        slot = jnp.sum(jnp.where(named[k], before, 0.0), axis=0, keepdims=True).astype(jnp.int32)
        expert = routes_ref[k : k + 1, :]
        place = jnp.where(slot < TILE, expert * TILE + slot, experts * TILE + block * experts + expert)
        places.append(place.astype(F32))
    near = jnp.concatenate(gates + places + [jnp.zeros((4, tokens), F32)], axis=0)
    info_ref[...] = jnp.concatenate(found + [near], axis=0)
    for m in range(micro):
        part = near[:, m * rows : (m + 1) * rows]
        near_ref[m, :, :rows] = part
        near_ref[m, :, rows:] = part


def gate_info(normed, w, routes, micro):
    tokens, width = normed.shape
    experts = w.shape[0]
    return pl.pallas_call(
        functools.partial(gate_kernel, micro),
        out_shape=[
            jax.ShapeDtypeStruct((2 * experts + 8, tokens), F32),
            jax.ShapeDtypeStruct((micro, 8, 2 * tokens // micro), F32),
        ],
        compiler_params=params(32),
        name="gates",
    )(normed, w, routes)


def pairs(sections):
    found = []
    for s in range(sections - 1):
        for k in range(2):
            for upper in range(s + 1, sections):
                for k2 in range(2):
                    found.append((s, k, upper, k2))
    return {key: row for row, key in enumerate(found)}


def couple_kernel(p_ref, w_ref, info_ref, *refs):
    sections, experts, quarter = w_ref.shape
    early, rest = refs[:sections], refs[sections : 2 * sections]
    out_ref, early_ref, rest_ref, sems = refs[2 * sections :]
    copies = []
    for j in range(sections):
        copies.append(pltpu.make_async_copy(early[j], early_ref.at[j], sems.at[0, j]))
        copies.append(pltpu.make_async_copy(rest[j], rest_ref.at[j], sems.at[1, j]))
    for copy in copies:
        copy.start()
    for copy in copies:
        copy.wait()
    p = p_ref[0]
    table = pairs(sections)
    start = 0
    for saved_ref in (early_ref, rest_ref):
        tokens = saved_ref.shape[2] * saved_ref.shape[3]
        lanes = slice(start, start + tokens)
        for s in range(sections - 1):
            j = (s - p) & (sections - 1)
            for k in range(2):
                saved = saved_ref[j, k].reshape(tokens, quarter)
                for upper in range(s + 1, sections):
                    j2 = (upper - p) & (sections - 1)
                    part = lax.dot_general(w_ref[j2], saved, NT, preferred_element_type=F32)
                    for k2 in range(2):
                        row = table[(s, k, upper, k2)]
                        v = info_ref[j2, k2 * experts : (k2 + 1) * experts, lanes]
                        out_ref[row : row + 1, lanes] = jnp.sum(part * v, axis=0, keepdims=True)
        start += tokens


def coupling(p, early, rest, w, info):
    sections = len(early)
    tokens = info.shape[2]
    return pl.pallas_call(
        couple_kernel,
        in_specs=[SCALAR, WHOLE, WHOLE] + [STAYS] * (2 * sections),
        out_specs=WHOLE,
        out_shape=jax.ShapeDtypeStruct((len(pairs(sections)), tokens), F32),
        scratch_shapes=[
            pltpu.VMEM((sections,) + early[0].shape, BF16),
            pltpu.VMEM((sections,) + rest[0].shape, BF16),
            pltpu.SemaphoreType.DMA((2, sections)),
        ],
        compiler_params=params(32),
        name="coupling",
    )(p, w, info, *early, *rest)


def picked(gates, places, first, received):
    n = received.shape[0]
    lanes = gates[0].shape[1]
    index, lane = iotas((n, lanes))
    pick = jnp.zeros((n, lanes), F32)
    for k in range(2):
        pick = pick + jnp.where(index + first == places[k], gates[k], 0.0)
    high = pick.astype(BF16).astype(F32)
    pick = jnp.where(lane >= lanes // 2, pick - high, high).astype(BF16)
    both = lax.dot_general(pick, received, TN, preferred_element_type=F32)
    return both[: lanes // 2] + both[lanes // 2 :]


def lead_kernel(p_ref, received_hbm, near_ref, *refs):
    outs = refs[:-4]
    block_ref, out_ref, in_sems, out_sems = refs[-4:]
    units, experts, _, half = block_ref.shape
    reads = [
        pltpu.make_async_copy(
            received_hbm.at[:, pl.ds(TILE * unit, TILE), :], block_ref.at[unit], in_sems.at[unit]
        )
        for unit in range(units)
    ]
    for copy in reads:
        copy.start()
    for unit in range(units):
        m, h = divmod(unit, 2)
        reads[unit].wait()
        received = block_ref[unit].reshape(experts * TILE, half)
        gates = [near_ref[m, k : k + 1, :] for k in range(2)]
        places = [near_ref[m, 2 + k : 3 + k, :].astype(jnp.int32) for k in range(2)]
        total = picked(gates, places, 0, received).astype(BF16)
        out_ref[2 * h, m] = total[:, : half // 2]
        out_ref[2 * h + 1, m] = total[:, half // 2 :]
    sections = len(outs)
    writes = [
        pltpu.make_async_copy(out_ref.at[(p_ref[0] - j) & (sections - 1)], outs[j], out_sems.at[j])
        for j in range(sections)
    ]
    for copy in writes:
        copy.start()
    for copy in writes:
        copy.wait()


def lead_combine(p, received, near, sections):
    experts, packed, half = received.shape
    units = packed // TILE
    part = (units // 2, near.shape[2] // 2, 2 * half // sections)
    return pl.pallas_call(
        lead_kernel,
        in_specs=[SCALAR, STAYS, WHOLE],
        out_specs=[STAYS] * sections,
        out_shape=[pltpu.HBM(part, BF16)] * sections,
        scratch_shapes=[
            pltpu.VMEM((units, experts, TILE, half), BF16),
            pltpu.VMEM((sections,) + part, BF16),
            pltpu.SemaphoreType.DMA((units,)),
            pltpu.SemaphoreType.DMA((sections,)),
        ],
        compiler_params=params(24),
        name="lead_combine",
    )(p, in_hbm(received), near)


def tail_kernel(p_ref, received_hbm, info_hbm, up_hbm, links_hbm, *refs):
    sections = info_hbm.shape[0]
    lead_hbm, early_hbm, rest_hbm = [refs[i * sections : (i + 1) * sections] for i in range(3)]
    back_hbm, sent_ref, v_ref, block_ref, info_ref, up_ref, early_ref, rest_ref = refs[3 * sections :][:8]
    lead_ref, links_ref, last_ref, sum_ref, back_ref = refs[3 * sections + 8 :][:5]
    block_sems, info_sem, up_sem, links_sem, saved_sems, back_sems = refs[3 * sections + 13 :]
    p = p_ref[0]
    _, _, rows, quarter = sum_ref.shape
    _, experts, _, half = block_ref.shape
    micro = up_ref.shape[0]
    n = experts * TILE
    blocks = [
        pltpu.make_async_copy(
            received_hbm.at[:, pl.ds(TILE * unit, TILE), :], block_ref.at[unit], block_sems.at[unit]
        )
        for unit in range(3)
    ]
    early = [
        pltpu.make_async_copy(early_hbm[j], early_ref.at[j], saved_sems.at[0, j]) for j in range(sections)
    ]
    rest = [
        pltpu.make_async_copy(rest_hbm[j], rest_ref.at[j], saved_sems.at[1, j]) for j in range(sections)
    ]
    lead = [
        pltpu.make_async_copy(lead_hbm[j], lead_ref.at[j], saved_sems.at[2, j]) for j in range(sections)
    ]
    info = pltpu.make_async_copy(info_hbm, info_ref, info_sem)
    up = pltpu.make_async_copy(up_hbm, up_ref, up_sem)
    links = pltpu.make_async_copy(links_hbm, links_ref, links_sem)
    backs = [
        pltpu.make_async_copy(back_ref.at[m], back_hbm.at[:, m], back_sems.at[m]) for m in range(micro)
    ]
    for copy in [blocks[2], info] + lead + [up] + early + blocks[:2] + rest + [links]:
        copy.start()
    kept = micro * experts
    out_row, in_row = iotas((4 * kept, n))
    order = (out_row % experts) * TILE + out_row // (2 * kept) * micro + out_row % kept // experts
    order = (in_row == order).astype(BF16)
    lane = lax.broadcasted_iota(jnp.int32, (rows, 128), 1)
    row, column = iotas((2 * sections, 128))
    eye = (row == column).astype(F32)
    blocks[2].wait()
    last = block_ref[2].reshape(n, half)
    last_ref[...] = jnp.dot(order, last, preferred_element_type=F32).astype(BF16)
    info.wait()
    v_ref[...] = info_ref[:, : 2 * experts]
    for j in range(sections):
        h, c = divmod(j, 2)
        columns = slice(c * quarter, (c + 1) * quarter)
        facts = info_ref[j, 2 * experts :, :]
        gates = [facts[k : k + 1] for k in range(2)]
        places = [facts[2 + k : 3 + k].astype(jnp.int32) for k in range(2)]
        pick = split_pick(gates, places, n, kept)
        received = last_ref[2 * h * kept : 2 * (h + 1) * kept, columns]
        total = lax.dot_general(pick, received, TN, preferred_element_type=F32)
        sum_ref[j] = total.reshape(micro, rows, quarter)
    for m in range(micro):
        if m == micro - 1:
            blocks[0].wait()
            blocks[1].wait()
        for j in range(sections):
            h, c = divmod(j, 2)
            columns = slice(c * quarter, (c + 1) * quarter)
            if m == micro - 1:
                facts = info_ref[j, 2 * experts :, m * rows : (m + 1) * rows]
                gates = [facts[k : k + 1] for k in range(2)]
                places = [facts[2 + k : 3 + k].astype(jnp.int32) for k in range(2)]
                main = block_ref[h, :, :, columns].reshape(n, quarter)
                pick = split_pick(gates, places, 0, n)
                extra = lax.dot_general(
                    pick, jnp.concatenate([main, main], axis=0), TN, preferred_element_type=F32
                )
            else:
                if m == 0:
                    lead[j].wait()
                extra = lead_ref[j, m].astype(F32)
            total = sum_ref[j, m] + extra
            sum_ref[j, m] = total
            back_ref[m, j] = total.astype(BF16)
        backs[m].start()
        if m == 0:
            up.wait()
            for copy in early:
                copy.wait()
        if m == micro - 1:
            for copy in rest:
                copy.wait()
        base = up_ref[m].astype(F32)
        dots = jnp.zeros((rows, 128), F32)
        for s in reversed(range(sections)):
            j = (s - p) & (sections - 1)
            for k in range(2):
                saved = early_ref[j, k, m] if m < micro - 1 else rest_ref[j, k, 0]
                product = base * saved.astype(F32)
                part = product[:, :128]
                for t in range(1, quarter // 128):
                    part = part + product[:, t * 128 : (t + 1) * 128]
                part = jnp.sum(part, axis=1, keepdims=True)
                dots = jnp.where(lane == 2 * s + k, part, dots)
            if s > 0:
                base = base + sum_ref[j, m]
        dots = lax.dot_general(
            eye, dots, NT, precision=lax.Precision.HIGHEST, preferred_element_type=F32
        )
        for dest in range(sections):
            sent_ref[dest, : 2 * sections, m * rows : (m + 1) * rows] = dots
    links.wait()
    for dest in range(sections):
        sent_ref[dest, 2 * sections :, :] = links_ref[...]
    for copy in backs:
        copy.wait()


def split_pick(gates, places, first, n):
    index = lax.broadcasted_iota(jnp.int32, (n, gates[0].shape[1]), 0) + first
    pick = jnp.zeros(index.shape, F32)
    for k in range(2):
        pick = pick + jnp.where(index == places[k], gates[k], 0.0)
    high = pick.astype(BF16).astype(F32)
    return jnp.concatenate([high, pick - high], axis=0).astype(BF16)


def tail_combine(p, received, info, upstream, links, lead, early, rest):
    sections = len(early)
    micro, rows, quarter = upstream.shape
    experts, packed, half = received.shape
    part = (sections, rows, quarter)
    dma = pltpu.SemaphoreType.DMA
    fetched = [in_hbm(array) for array in (received, info, upstream, links, *lead, *early, *rest)]
    return pl.pallas_call(
        tail_kernel,
        in_specs=[SCALAR] + [STAYS] * len(fetched),
        out_specs=[STAYS, WHOLE, WHOLE],
        out_shape=[
            pltpu.HBM((sections, micro, rows, quarter), BF16),
            jax.ShapeDtypeStruct((sections, 2 * sections + links.shape[0], micro * rows), F32),
            jax.ShapeDtypeStruct((sections, 2 * experts, micro * rows), F32),
        ],
        scratch_shapes=[
            pltpu.VMEM((3, experts, TILE, half), BF16),
            pltpu.VMEM(info.shape, F32),
            pltpu.VMEM(upstream.shape, BF16),
            pltpu.VMEM((sections,) + early[0].shape, BF16),
            pltpu.VMEM((sections,) + rest[0].shape, BF16),
            pltpu.VMEM((sections,) + lead[0].shape, BF16),
            pltpu.VMEM(links.shape, F32),
            pltpu.VMEM((4 * micro * experts, half), BF16),
            pltpu.VMEM((sections, micro, rows, quarter), F32),
            pltpu.VMEM((micro,) + part, BF16),
            dma((3,)), dma, dma, dma, dma((3, sections)), dma((micro,)),
        ],
        compiler_params=params(32),
        name="tail_combine",
    )(p, *fetched)


def dense_kernel(
    micro, p_ref, sent_ref, v_ref, rows_ref, dense_hbm, part_hbm, dense_ref, part_ref, sems
):
    p = p_ref[0]
    sections = sent_ref.shape[0]
    tokens, width = rows_ref.shape
    experts = v_ref.shape[1] // 2
    table = pairs(sections)
    given = sent_ref[0]
    for source in range(1, sections):
        given = given + sent_ref[source]
    dots = {}
    own = jnp.zeros((experts, tokens), F32)
    for s in reversed(range(sections)):
        j = (s - p) & (sections - 1)
        dense = jnp.zeros((experts, tokens), F32)
        for k in range(2):
            value = given[2 * s + k : 2 * s + k + 1, :]
            for upper in range(s + 1, sections):
                for k2 in range(2):
                    row = 2 * sections + table[(s, k, upper, k2)]
                    value = value + given[row : row + 1, :] * dots[(upper, k2)]
            dots[(s, k)] = value
            dense = dense + value * v_ref[j, k * experts : (k + 1) * experts, :]
        dense_ref[s * experts : (s + 1) * experts, :] = dense.astype(BF16)
        own = jnp.where(p == s, dense, own)
    out_dense = pltpu.make_async_copy(dense_ref, dense_hbm, sems.at[0])
    out_dense.start()
    total = jnp.dot(own.astype(BF16), rows_ref[...], preferred_element_type=F32) * (1.0 / micro)
    cols = width // 128
    for r in range(experts // 8):
        for c in range(cols):
            tile = total[r * 8 : (r + 1) * 8, c * 128 : (c + 1) * 128]
            part_ref[r * cols + c] = tile.astype(BF16)
    out_part = pltpu.make_async_copy(part_ref, part_hbm, sems.at[1])
    out_part.start()
    out_dense.wait()
    out_part.wait()


def dense_terms(p, sent, v, normed, micro):
    sections, _, tokens = sent.shape
    width = normed.shape[1]
    experts = v.shape[1] // 2
    dense = (sections * experts, tokens)
    part = (experts // 8 * (width // 128), 8, 128)
    return pl.pallas_call(
        functools.partial(dense_kernel, micro),
        in_specs=[SCALAR, WHOLE, WHOLE, WHOLE],
        out_specs=[STAYS] * 2,
        out_shape=[pltpu.HBM(dense, BF16), pltpu.HBM(part, BF16)],
        scratch_shapes=[
            pltpu.VMEM(dense, BF16),
            pltpu.VMEM(part, BF16),
            pltpu.SemaphoreType.DMA((2,)),
        ],
        compiler_params=params(32),
        name="dense",
    )(p, sent, v, normed)


def grads_kernel(p_ref, up_hbm, back_hbm, dense_hbm, w_hbm, *refs):
    outs = refs[:-8]
    up_ref, dense_ref, w_ref, back_ref, total_ref, turn_ref, in_sems, out_sems = refs[-8:]
    p = p_ref[0]
    sections, micro, rows, quarter = turn_ref.shape
    experts = w_ref.shape[1]
    small = [
        pltpu.make_async_copy(source, target, in_sems.at[micro + i])
        for i, (source, target) in enumerate(
            ((up_hbm, up_ref), (dense_hbm, dense_ref), (w_hbm, w_ref))
        )
    ]
    copies = [
        pltpu.make_async_copy(back_hbm.at[:, m], back_ref.at[m], in_sems.at[m]) for m in range(micro)
    ]
    for copy in small + copies:
        copy.start()
    for copy in small:
        copy.wait()
    total_ref[...] = up_ref[...].astype(F32)
    for s in reversed(range(sections)):
        j = (s - p) & (sections - 1)
        dense = dense_ref[s * experts : (s + 1) * experts, :]
        term = lax.dot_general(dense, w_ref[j], TN, preferred_element_type=F32)
        for m in range(micro):
            if s == sections - 1:
                copies[m].wait()
            total = total_ref[m] + back_ref[m, j].astype(F32) + term[m * rows : (m + 1) * rows]
            total_ref[m] = total
            turn_ref[j, m] = total.astype(BF16)
    copies = [pltpu.make_async_copy(turn_ref.at[j], outs[j], out_sems.at[j]) for j in range(sections)]
    for copy in copies:
        copy.start()
    for copy in copies:
        copy.wait()


def grads_of(p, upstream, back, dense, w):
    sections, micro, rows, quarter = back.shape
    part = (micro, rows, quarter)
    return pl.pallas_call(
        grads_kernel,
        in_specs=[SCALAR] + [STAYS] * 4,
        out_specs=[STAYS] * sections,
        out_shape=[pltpu.HBM(part, BF16)] * sections,
        scratch_shapes=[
            pltpu.VMEM(part, BF16),
            pltpu.VMEM(dense.shape, BF16),
            pltpu.VMEM(w.shape, BF16),
            pltpu.VMEM((micro, sections, rows, quarter), BF16),
            pltpu.VMEM(part, F32),
            pltpu.VMEM((sections,) + part, BF16),
            pltpu.SemaphoreType.DMA((micro + 3,)),
            pltpu.SemaphoreType.DMA((sections,)),
        ],
        compiler_params=params(40),
        name="grads",
    )(p, *[in_hbm(array) for array in (upstream, back, dense, w)])


def total_kernel(parts_ref, out_hbm, out_ref, sem):
    total = parts_ref[0].astype(F32)
    for source in range(1, parts_ref.shape[0]):
        total = total + parts_ref[source].astype(F32)
    total = total.astype(BF16)
    for dest in range(out_ref.shape[0]):
        out_ref[dest] = total
    copy = pltpu.make_async_copy(out_ref, out_hbm, sem)
    copy.start()
    copy.wait()


def total_for_all(parts):
    return pl.pallas_call(
        total_kernel,
        in_specs=[WHOLE],
        out_specs=STAYS,
        out_shape=pltpu.HBM(parts.shape, BF16),
        scratch_shapes=[pltpu.VMEM(parts.shape, BF16), pltpu.SemaphoreType.DMA],
        compiler_params=params(8),
        name="router_total",
    )(parts)


def join_kernel(p_ref, *refs):
    step = pl.program_id(0)
    out_ref = refs[-1]
    for d in range(len(refs) - 1):

        @pl.when(step == d)
        def _():
            out_ref[...] = refs[d][...]


def join(p, blocks):
    n = len(blocks)
    micro, rows, quarter = blocks[0].shape
    return pl.pallas_call(
        join_kernel,
        grid_spec=pltpu.PrefetchScalarGridSpec(
            num_scalar_prefetch=1,
            grid=(n,),
            in_specs=[pl.BlockSpec((micro, rows, quarter), lambda d, p: (0, 0, 0))] * n,
            out_specs=pl.BlockSpec((micro, rows, quarter), lambda d, p: (0, 0, (p[0] - d) & (n - 1))),
        ),
        out_shape=jax.ShapeDtypeStruct((micro, rows, n * quarter), BF16),
        compiler_params=params(32),
        name="join",
    )(p, *blocks)


def turned(block, distance):
    n = lax.axis_size("pipe")
    return lax.ppermute(block, "pipe", [(i, (i + distance) % n) for i in range(n)])


def gathered(block):
    n = lax.axis_size("pipe")
    return [block] + [turned(block, n - j) for j in range(1, n)]


def on_device(normed, saved_out, expert_grads, routes, router_weight, upstream):
    sections = lax.axis_size("pipe")
    section = lax.axis_index("pipe")
    p = section.astype(jnp.int32).reshape(1)
    _, micro, rows, width = normed.shape
    tokens = micro * rows
    quarter = width // sections
    normed = normed.reshape(tokens, width)
    w = router_weight[0].T
    experts = w.shape[0]

    def part(array, j, axis):
        return lax.dynamic_slice_in_dim(array, ((section - j) % sections) * quarter, quarter, axis)

    def spread(blocks):
        return [turned(block, sections - j) if j else block for j, block in enumerate(blocks)]

    grads = in_hbm(jnp.transpose(expert_grads[0, :, 0, 0], (0, 2, 1, 3)))
    lead = lax.all_to_all(lead_pack(grads, micro - 1), "expert", 0, 0, tiled=True)
    info, near = gate_info(normed, w, jnp.transpose(routes[0], (2, 0, 1)).reshape(2, tokens), micro)
    info_all = spread([info] * sections)
    w_all = spread([part(w, j, 1) for j in range(sections)])
    late = late_blocks(p, grads, sections)
    late, info_all, w_all = lax.optimization_barrier((late, info_all, w_all))
    late = spread(late)
    info_all = jnp.stack(info_all)
    w_all = jnp.stack(w_all)
    saved = jnp.transpose(saved_out[0], (2, 0, 1, 3))
    early = [part(saved[:, : micro - 1], j, 3) for j in range(sections)]
    *early, late[1], late[2], late[3] = lax.optimization_barrier((*early, *late[1:]))
    early = spread(early)
    tail_send = tail_pack(late)
    tail_send, *early = lax.optimization_barrier((tail_send, *early))
    tail = lax.all_to_all(tail_send, "expert", 0, 0, tiled=True)
    rest = spread([part(saved[:, micro - 1 :], j, 3) for j in range(sections)])
    lead = spread(lead_combine(p, lead, near, sections))
    links = coupling(p, early, rest, w_all, info_all)
    up = part(upstream, 0, 2)
    lead, info_all, w_all, early, rest, links, up = lax.optimization_barrier(
        (lead, info_all, w_all, early, rest, links, up)
    )
    back, sent, v = tail_combine(p, tail, info_all, up, links, lead, early, rest)
    sent = lax.all_to_all(sent, "pipe", 0, 0, tiled=True)
    dense, partial = dense_terms(p, sent, v, normed, micro)

    axes = ("expert", "dp")
    partial = lax.all_to_all(partial, axes, 0, 0, tiled=True)
    outs = grads_of(p, up, back, dense, w_all)
    blocks = [turned(out, d) if d else out for d, out in enumerate(outs)]
    total = lax.all_to_all(total_for_all(partial), axes, 0, 0, tiled=True)
    total = total.astype(F32).reshape(experts // 8, width // 128, 8, 128).transpose(0, 2, 1, 3)
    router_grad = total.reshape(experts, width).T
    blocks[0] = in_hbm(blocks[0])
    return (join(p, blocks)[None], router_grad[None])


def solution(mesh):
    in_specs = (
        P("pipe", None, ("expert", "dp"), None),
        P("pipe", None, ("expert", "dp"), None, None),
        P("pipe", None, "dp", "expert", None, None, None),
        P("pipe", None, ("expert", "dp"), None),
        P("pipe", None, None),
        P(None, ("expert", "dp"), None),
    )
    out_specs = (P("pipe", None, ("expert", "dp"), None), P("pipe", None, None))
    return jax.shard_map(
        on_device, mesh=mesh, in_specs=in_specs, out_specs=out_specs, check_vma=False
    )
```

```python
import functools

import jax
import jax.numpy as jnp
from jax import lax
from jax.experimental import pallas as pl
from jax.experimental.pallas import tpu as pltpu
from jax.sharding import PartitionSpec as P

F32 = jnp.float32
BF16 = jnp.bfloat16
NT = (((1,), (1,)), ((), ()))
TN = (((0,), (0,)), ((), ()))

TILE = 8


SCALAR = pl.BlockSpec(memory_space=pltpu.MemorySpace.SMEM)
WHOLE = pl.BlockSpec(memory_space=pltpu.MemorySpace.VMEM)
STAYS = pl.BlockSpec(memory_space=pl.ANY)


def params(mib):
    return pltpu.CompilerParams(vmem_limit_bytes=mib << 20)


def in_hbm(array):
    return pltpu.with_memory_space_constraint(array, pltpu.MemorySpace.HBM)


def iotas(shape):
    return [lax.broadcasted_iota(jnp.int32, shape, d) for d in range(2)]


def swap_matrix(slots, dests):
    out_row, in_row = iotas((slots * dests, slots * dests))
    return (in_row == (out_row % slots) * dests + out_row // slots).astype(BF16)


def lead_pack_kernel(grads_hbm, out_hbm, grads_ref, out_ref, in_sems, out_sems):
    count, slots, dests, width = grads_ref.shape
    half = width // 2
    reads = [
        pltpu.make_async_copy(grads_hbm.at[m, pl.ds(0, slots)], grads_ref.at[m], in_sems.at[m])
        for m in range(count)
    ]
    for copy in reads:
        copy.start()
    swap = swap_matrix(slots, dests)
    writes = []
    for m in range(count):
        reads[m].wait()
        for h in range(2):
            unit = 2 * m + h
            rows = grads_ref[m, :, :, h * half : (h + 1) * half].reshape(slots * dests, half)
            moved = jnp.dot(swap, rows, preferred_element_type=F32)
            out_ref[unit] = moved.reshape(dests, slots, half).astype(BF16)
            copy = pltpu.make_async_copy(
                out_ref.at[unit], out_hbm.at[:, pl.ds(unit * slots, slots), :], out_sems.at[unit]
            )
            copy.start()
            writes.append(copy)
    for copy in writes:
        copy.wait()


def lead_pack(grads, count):
    _, _, dests, width = grads.shape
    half = width // 2
    return pl.pallas_call(
        lead_pack_kernel,
        in_specs=[STAYS],
        out_specs=STAYS,
        out_shape=pltpu.HBM((dests, 2 * TILE * count, half), BF16),
        scratch_shapes=[
            pltpu.VMEM((count, TILE, dests, width), BF16),
            pltpu.VMEM((2 * count, dests, TILE, half), BF16),
            pltpu.SemaphoreType.DMA((count,)),
            pltpu.SemaphoreType.DMA((2 * count,)),
        ],
        compiler_params=params(40),
        name="lead_pack",
    )(grads)


def tail_pack_kernel(*refs):
    out_ref = refs[-1]
    kept, dests, quarter = refs[0].shape
    micro = kept - TILE
    swap = swap_matrix(TILE, dests)
    out_row, in_row = iotas((2 * micro * dests, micro * dests))
    within = out_row % (2 * micro)
    source = (within % micro) * dests + out_row // (2 * micro)
    for c in range(2):
        total = jnp.zeros((2 * micro * dests, quarter), F32)
        columns = slice(c * quarter, (c + 1) * quarter)
        for h in range(2):
            ref = refs[2 * h + c]
            moved = jnp.dot(swap, ref[:TILE].reshape(TILE * dests, quarter), preferred_element_type=F32)
            moved = moved.reshape(dests, TILE, quarter).astype(BF16)
            out_ref[:, h * TILE : (h + 1) * TILE, columns] = moved
            pick = ((in_row == source) & (within // micro == h)).astype(BF16)
            rows = ref[TILE:].reshape(micro * dests, quarter)
            total = total + jnp.dot(pick, rows, preferred_element_type=F32)
        out_ref[:, 2 * TILE :, columns] = total.reshape(dests, 2 * micro, quarter).astype(BF16)


def tail_pack(blocks):
    kept, dests, quarter = blocks[0].shape
    return pl.pallas_call(
        tail_pack_kernel,
        out_shape=jax.ShapeDtypeStruct((dests, 2 * TILE + 2 * (kept - TILE), 2 * quarter), BF16),
        compiler_params=params(40),
        name="tail_pack",
    )(*blocks)


def late_kernel(p_ref, main_ref, last_ref, *out_refs):
    step = pl.program_id(0)
    for j in range(len(out_refs)):

        @pl.when(step == j)
        def _():
            out_refs[j][:TILE] = main_ref[0]
            out_refs[j][TILE:] = last_ref[:, 0]


def late_blocks(p, grads, sections):
    micro, cap, dests, width = grads.shape
    quarter = width // sections
    shape = (TILE + micro, dests, quarter)
    return pl.pallas_call(
        late_kernel,
        grid_spec=pltpu.PrefetchScalarGridSpec(
            num_scalar_prefetch=1,
            grid=(sections,),
            in_specs=[
                pl.BlockSpec(
                    (1, TILE, dests, quarter),
                    lambda j, p: (micro - 1, 0, 0, (p[0] - j) & (sections - 1)),
                ),
                pl.BlockSpec(
                    (micro, 1, dests, quarter),
                    lambda j, p: (0, cap - 1, 0, (p[0] - j) & (sections - 1)),
                ),
            ],
            out_specs=[pl.BlockSpec(shape, lambda j, p: (0, 0, 0))] * sections,
        ),
        out_shape=[jax.ShapeDtypeStruct(shape, BF16)] * sections,
        compiler_params=params(32),
        name="late_blocks",
    )(p, grads, grads)


def gate_kernel(micro, normed_ref, w_ref, routes_ref, info_ref, near_ref):
    logits = lax.dot_general(w_ref[...], normed_ref[...], NT, preferred_element_type=F32)
    experts, tokens = logits.shape
    rows = tokens // micro
    expl = jnp.exp(logits)
    probs = expl / jnp.sum(expl, axis=0, keepdims=True)
    ids = lax.broadcasted_iota(jnp.int32, (experts, tokens), 0)
    first, second = iotas((tokens, tokens))
    lane = lax.broadcasted_iota(jnp.int32, (1, tokens), 1)
    block = jnp.zeros((1, tokens), jnp.int32)
    same = first >= 0
    for m in range(1, micro):
        block = block + (lane >= m * rows).astype(jnp.int32)
        same = same & ((first >= m * rows) == (second >= m * rows))
    earlier = ((first < second) & same).astype(BF16)
    named = [ids == routes_ref[k : k + 1, :] for k in range(2)]
    both = jnp.where(named[0] | named[1], 1.0, 0.0).astype(BF16)
    before = jnp.dot(both, earlier, preferred_element_type=F32)
    found = []
    gates = []
    places = []
    for k in range(2):
        gate = jnp.sum(jnp.where(named[k], probs, 0.0), axis=0, keepdims=True)
        found.append(gate * (jnp.where(named[k], 1.0, 0.0) - probs))
        gates.append(gate)
        slot = jnp.sum(jnp.where(named[k], before, 0.0), axis=0, keepdims=True).astype(jnp.int32)
        expert = routes_ref[k : k + 1, :]
        place = jnp.where(slot < TILE, expert * TILE + slot, experts * TILE + block * experts + expert)
        places.append(place.astype(F32))
    near = jnp.concatenate(gates + places + [jnp.zeros((4, tokens), F32)], axis=0)
    info_ref[...] = jnp.concatenate(found + [near], axis=0)
    for m in range(micro):
        part = near[:, m * rows : (m + 1) * rows]
        near_ref[m, :, :rows] = part
        near_ref[m, :, rows:] = part


def gate_info(normed, w, routes, micro):
    tokens, width = normed.shape
    experts = w.shape[0]
    return pl.pallas_call(
        functools.partial(gate_kernel, micro),
        out_shape=[
            jax.ShapeDtypeStruct((2 * experts + 8, tokens), F32),
            jax.ShapeDtypeStruct((micro, 8, 2 * tokens // micro), F32),
        ],
        compiler_params=params(32),
        name="gates",
    )(normed, w, routes)


def pairs(sections):
    found = []
    for s in range(sections - 1):
        for k in range(2):
            for upper in range(s + 1, sections):
                for k2 in range(2):
                    found.append((s, k, upper, k2))
    return {key: row for row, key in enumerate(found)}


def couple_kernel(p_ref, w_ref, info_ref, *refs):
    sections, experts, quarter = w_ref.shape
    early, rest = refs[:sections], refs[sections : 2 * sections]
    out_ref, early_ref, rest_ref, sems = refs[2 * sections :]
    copies = []
    for j in range(sections):
        copies.append(pltpu.make_async_copy(early[j], early_ref.at[j], sems.at[0, j]))
        copies.append(pltpu.make_async_copy(rest[j], rest_ref.at[j], sems.at[1, j]))
    for copy in copies:
        copy.start()
    for copy in copies:
        copy.wait()
    p = p_ref[0]
    table = pairs(sections)
    start = 0
    for saved_ref in (early_ref, rest_ref):
        tokens = saved_ref.shape[2] * saved_ref.shape[3]
        lanes = slice(start, start + tokens)
        for s in range(sections - 1):
            j = (s - p) & (sections - 1)
            for k in range(2):
                saved = saved_ref[j, k].reshape(tokens, quarter)
                for upper in range(s + 1, sections):
                    j2 = (upper - p) & (sections - 1)
                    part = lax.dot_general(w_ref[j2], saved, NT, preferred_element_type=F32)
                    for k2 in range(2):
                        row = table[(s, k, upper, k2)]
                        v = info_ref[j2, k2 * experts : (k2 + 1) * experts, lanes]
                        out_ref[row : row + 1, lanes] = jnp.sum(part * v, axis=0, keepdims=True)
        start += tokens


def coupling(p, early, rest, w, info):
    sections = len(early)
    tokens = info.shape[2]
    return pl.pallas_call(
        couple_kernel,
        in_specs=[SCALAR, WHOLE, WHOLE] + [STAYS] * (2 * sections),
        out_specs=WHOLE,
        out_shape=jax.ShapeDtypeStruct((len(pairs(sections)), tokens), F32),
        scratch_shapes=[
            pltpu.VMEM((sections,) + early[0].shape, BF16),
            pltpu.VMEM((sections,) + rest[0].shape, BF16),
            pltpu.SemaphoreType.DMA((2, sections)),
        ],
        compiler_params=params(32),
        name="coupling",
    )(p, w, info, *early, *rest)


def picked(gates, places, first, received):
    n = received.shape[0]
    lanes = gates[0].shape[1]
    index, lane = iotas((n, lanes))
    pick = jnp.zeros((n, lanes), F32)
    for k in range(2):
        pick = pick + jnp.where(index + first == places[k], gates[k], 0.0)
    high = pick.astype(BF16).astype(F32)
    pick = jnp.where(lane >= lanes // 2, pick - high, high).astype(BF16)
    both = lax.dot_general(pick, received, TN, preferred_element_type=F32)
    return both[: lanes // 2] + both[lanes // 2 :]


def lead_kernel(p_ref, received_hbm, near_ref, *refs):
    outs = refs[:-4]
    block_ref, out_ref, in_sems, out_sems = refs[-4:]
    units, experts, _, half = block_ref.shape
    reads = [
        pltpu.make_async_copy(
            received_hbm.at[:, pl.ds(TILE * unit, TILE), :], block_ref.at[unit], in_sems.at[unit]
        )
        for unit in range(units)
    ]
    for copy in reads:
        copy.start()
    for unit in range(units):
        m, h = divmod(unit, 2)
        reads[unit].wait()
        received = block_ref[unit].reshape(experts * TILE, half)
        gates = [near_ref[m, k : k + 1, :] for k in range(2)]
        places = [near_ref[m, 2 + k : 3 + k, :].astype(jnp.int32) for k in range(2)]
        total = picked(gates, places, 0, received).astype(BF16)
        out_ref[2 * h, m] = total[:, : half // 2]
        out_ref[2 * h + 1, m] = total[:, half // 2 :]
    sections = len(outs)
    writes = [
        pltpu.make_async_copy(out_ref.at[(p_ref[0] - j) & (sections - 1)], outs[j], out_sems.at[j])
        for j in range(sections)
    ]
    for copy in writes:
        copy.start()
    for copy in writes:
        copy.wait()


def lead_combine(p, received, near, sections):
    experts, packed, half = received.shape
    units = packed // TILE
    part = (units // 2, near.shape[2] // 2, 2 * half // sections)
    return pl.pallas_call(
        lead_kernel,
        in_specs=[SCALAR, STAYS, WHOLE],
        out_specs=[STAYS] * sections,
        out_shape=[pltpu.HBM(part, BF16)] * sections,
        scratch_shapes=[
            pltpu.VMEM((units, experts, TILE, half), BF16),
            pltpu.VMEM((sections,) + part, BF16),
            pltpu.SemaphoreType.DMA((units,)),
            pltpu.SemaphoreType.DMA((sections,)),
        ],
        compiler_params=params(24),
        name="lead_combine",
    )(p, in_hbm(received), near)


def tail_kernel(p_ref, received_hbm, info_hbm, up_hbm, links_hbm, *refs):
    sections = info_hbm.shape[0]
    lead_hbm, early_hbm, rest_hbm = [refs[i * sections : (i + 1) * sections] for i in range(3)]
    back_hbm, sent_ref, v_ref, block_ref, info_ref, up_ref, early_ref, rest_ref = refs[3 * sections :][:8]
    lead_ref, links_ref, last_ref, sum_ref, back_ref = refs[3 * sections + 8 :][:5]
    block_sems, info_sem, up_sem, links_sem, saved_sems, back_sems = refs[3 * sections + 13 :]
    p = p_ref[0]
    _, _, rows, quarter = sum_ref.shape
    _, experts, _, half = block_ref.shape
    micro = up_ref.shape[0]
    n = experts * TILE
    blocks = [
        pltpu.make_async_copy(
            received_hbm.at[:, pl.ds(TILE * unit, TILE), :], block_ref.at[unit], block_sems.at[unit]
        )
        for unit in range(3)
    ]
    early = [
        pltpu.make_async_copy(early_hbm[j], early_ref.at[j], saved_sems.at[0, j]) for j in range(sections)
    ]
    rest = [
        pltpu.make_async_copy(rest_hbm[j], rest_ref.at[j], saved_sems.at[1, j]) for j in range(sections)
    ]
    lead = [
        pltpu.make_async_copy(lead_hbm[j], lead_ref.at[j], saved_sems.at[2, j]) for j in range(sections)
    ]
    info = pltpu.make_async_copy(info_hbm, info_ref, info_sem)
    up = pltpu.make_async_copy(up_hbm, up_ref, up_sem)
    links = pltpu.make_async_copy(links_hbm, links_ref, links_sem)
    backs = [
        pltpu.make_async_copy(back_ref.at[m], back_hbm.at[:, m], back_sems.at[m]) for m in range(micro)
    ]
    for copy in [blocks[2], info] + lead + [up] + early + blocks[:2] + rest + [links]:
        copy.start()
    kept = micro * experts
    out_row, in_row = iotas((4 * kept, n))
    order = (out_row % experts) * TILE + out_row // (2 * kept) * micro + out_row % kept // experts
    order = (in_row == order).astype(BF16)
    lane = lax.broadcasted_iota(jnp.int32, (rows, 128), 1)
    row, column = iotas((2 * sections, 128))
    eye = (row == column).astype(F32)
    blocks[2].wait()
    last = block_ref[2].reshape(n, half)
    last_ref[...] = jnp.dot(order, last, preferred_element_type=F32).astype(BF16)
    info.wait()
    v_ref[...] = info_ref[:, : 2 * experts]
    for j in range(sections):
        h, c = divmod(j, 2)
        columns = slice(c * quarter, (c + 1) * quarter)
        facts = info_ref[j, 2 * experts :, :]
        gates = [facts[k : k + 1] for k in range(2)]
        places = [facts[2 + k : 3 + k].astype(jnp.int32) for k in range(2)]
        pick = split_pick(gates, places, n, kept)
        received = last_ref[2 * h * kept : 2 * (h + 1) * kept, columns]
        total = lax.dot_general(pick, received, TN, preferred_element_type=F32)
        sum_ref[j] = total.reshape(micro, rows, quarter)
    for m in range(micro):
        if m == micro - 1:
            blocks[0].wait()
            blocks[1].wait()
        for j in range(sections):
            h, c = divmod(j, 2)
            columns = slice(c * quarter, (c + 1) * quarter)
            if m == micro - 1:
                facts = info_ref[j, 2 * experts :, m * rows : (m + 1) * rows]
                gates = [facts[k : k + 1] for k in range(2)]
                places = [facts[2 + k : 3 + k].astype(jnp.int32) for k in range(2)]
                main = block_ref[h, :, :, columns].reshape(n, quarter)
                pick = split_pick(gates, places, 0, n)
                extra = lax.dot_general(
                    pick, jnp.concatenate([main, main], axis=0), TN, preferred_element_type=F32
                )
            else:
                if m == 0:
                    lead[j].wait()
                extra = lead_ref[j, m].astype(F32)
            total = sum_ref[j, m] + extra
            sum_ref[j, m] = total
            back_ref[m, j] = total.astype(BF16)
        backs[m].start()
        if m == 0:
            up.wait()
            for copy in early:
                copy.wait()
        if m == micro - 1:
            for copy in rest:
                copy.wait()
        base = up_ref[m].astype(F32)
        dots = jnp.zeros((rows, 128), F32)
        for s in reversed(range(sections)):
            j = (s - p) & (sections - 1)
            for k in range(2):
                saved = early_ref[j, k, m] if m < micro - 1 else rest_ref[j, k, 0]
                product = base * saved.astype(F32)
                part = product[:, :128]
                for t in range(1, quarter // 128):
                    part = part + product[:, t * 128 : (t + 1) * 128]
                part = jnp.sum(part, axis=1, keepdims=True)
                dots = jnp.where(lane == 2 * s + k, part, dots)
            if s > 0:
                base = base + sum_ref[j, m]
        dots = lax.dot_general(
            eye, dots, NT, precision=lax.Precision.HIGHEST, preferred_element_type=F32
        )
        for dest in range(sections):
            sent_ref[dest, : 2 * sections, m * rows : (m + 1) * rows] = dots
    links.wait()
    for dest in range(sections):
        sent_ref[dest, 2 * sections :, :] = links_ref[...]
    for copy in backs:
        copy.wait()


def split_pick(gates, places, first, n):
    index = lax.broadcasted_iota(jnp.int32, (n, gates[0].shape[1]), 0) + first
    pick = jnp.zeros(index.shape, F32)
    for k in range(2):
        pick = pick + jnp.where(index == places[k], gates[k], 0.0)
    high = pick.astype(BF16).astype(F32)
    return jnp.concatenate([high, pick - high], axis=0).astype(BF16)


def tail_combine(p, received, info, upstream, links, lead, early, rest):
    sections = len(early)
    micro, rows, quarter = upstream.shape
    experts, packed, half = received.shape
    part = (sections, rows, quarter)
    dma = pltpu.SemaphoreType.DMA
    fetched = [in_hbm(array) for array in (received, info, upstream, links, *lead, *early, *rest)]
    return pl.pallas_call(
        tail_kernel,
        in_specs=[SCALAR] + [STAYS] * len(fetched),
        out_specs=[STAYS, WHOLE, WHOLE],
        out_shape=[
            pltpu.HBM((sections, micro, rows, quarter), BF16),
            jax.ShapeDtypeStruct((sections, 2 * sections + links.shape[0], micro * rows), F32),
            jax.ShapeDtypeStruct((sections, 2 * experts, micro * rows), F32),
        ],
        scratch_shapes=[
            pltpu.VMEM((3, experts, TILE, half), BF16),
            pltpu.VMEM(info.shape, F32),
            pltpu.VMEM(upstream.shape, BF16),
            pltpu.VMEM((sections,) + early[0].shape, BF16),
            pltpu.VMEM((sections,) + rest[0].shape, BF16),
            pltpu.VMEM((sections,) + lead[0].shape, BF16),
            pltpu.VMEM(links.shape, F32),
            pltpu.VMEM((4 * micro * experts, half), BF16),
            pltpu.VMEM((sections, micro, rows, quarter), F32),
            pltpu.VMEM((micro,) + part, BF16),
            dma((3,)), dma, dma, dma, dma((3, sections)), dma((micro,)),
        ],
        compiler_params=params(32),
        name="tail_combine",
    )(p, *fetched)


def dense_kernel(
    micro, p_ref, sent_ref, v_ref, rows_ref, dense_hbm, part_hbm, dense_ref, part_ref, sems
):
    p = p_ref[0]
    sections = sent_ref.shape[0]
    tokens, width = rows_ref.shape
    experts = v_ref.shape[1] // 2
    table = pairs(sections)
    given = sent_ref[0]
    for source in range(1, sections):
        given = given + sent_ref[source]
    dots = {}
    own = jnp.zeros((experts, tokens), F32)
    for s in reversed(range(sections)):
        j = (s - p) & (sections - 1)
        dense = jnp.zeros((experts, tokens), F32)
        for k in range(2):
            value = given[2 * s + k : 2 * s + k + 1, :]
            for upper in range(s + 1, sections):
                for k2 in range(2):
                    row = 2 * sections + table[(s, k, upper, k2)]
                    value = value + given[row : row + 1, :] * dots[(upper, k2)]
            dots[(s, k)] = value
            dense = dense + value * v_ref[j, k * experts : (k + 1) * experts, :]
        dense_ref[s * experts : (s + 1) * experts, :] = dense.astype(BF16)
        own = jnp.where(p == s, dense, own)
    out_dense = pltpu.make_async_copy(dense_ref, dense_hbm, sems.at[0])
    out_dense.start()
    total = jnp.dot(own.astype(BF16), rows_ref[...], preferred_element_type=F32) * (1.0 / micro)
    cols = width // 128
    for r in range(experts // 8):
        for c in range(cols):
            tile = total[r * 8 : (r + 1) * 8, c * 128 : (c + 1) * 128]
            part_ref[r * cols + c] = tile.astype(BF16)
    out_part = pltpu.make_async_copy(part_ref, part_hbm, sems.at[1])
    out_part.start()
    out_dense.wait()
    out_part.wait()


def dense_terms(p, sent, v, normed, micro):
    sections, _, tokens = sent.shape
    width = normed.shape[1]
    experts = v.shape[1] // 2
    dense = (sections * experts, tokens)
    part = (experts // 8 * (width // 128), 8, 128)
    return pl.pallas_call(
        functools.partial(dense_kernel, micro),
        in_specs=[SCALAR, WHOLE, WHOLE, WHOLE],
        out_specs=[STAYS] * 2,
        out_shape=[pltpu.HBM(dense, BF16), pltpu.HBM(part, BF16)],
        scratch_shapes=[
            pltpu.VMEM(dense, BF16),
            pltpu.VMEM(part, BF16),
            pltpu.SemaphoreType.DMA((2,)),
        ],
        compiler_params=params(32),
        name="dense",
    )(p, sent, v, normed)


def grads_kernel(p_ref, up_hbm, back_hbm, dense_hbm, w_hbm, *refs):
    outs = refs[:-8]
    up_ref, dense_ref, w_ref, back_ref, total_ref, turn_ref, in_sems, out_sems = refs[-8:]
    p = p_ref[0]
    sections, micro, rows, quarter = turn_ref.shape
    experts = w_ref.shape[1]
    small = [
        pltpu.make_async_copy(source, target, in_sems.at[micro + i])
        for i, (source, target) in enumerate(
            ((up_hbm, up_ref), (dense_hbm, dense_ref), (w_hbm, w_ref))
        )
    ]
    copies = [
        pltpu.make_async_copy(back_hbm.at[:, m], back_ref.at[m], in_sems.at[m]) for m in range(micro)
    ]
    for copy in small + copies:
        copy.start()
    for copy in small:
        copy.wait()
    total_ref[...] = up_ref[...].astype(F32)
    for s in reversed(range(sections)):
        j = (s - p) & (sections - 1)
        dense = dense_ref[s * experts : (s + 1) * experts, :]
        term = lax.dot_general(dense, w_ref[j], TN, preferred_element_type=F32)
        for m in range(micro):
            if s == sections - 1:
                copies[m].wait()
            total = total_ref[m] + back_ref[m, j].astype(F32) + term[m * rows : (m + 1) * rows]
            total_ref[m] = total
            turn_ref[j, m] = total.astype(BF16)
    copies = [pltpu.make_async_copy(turn_ref.at[j], outs[j], out_sems.at[j]) for j in range(sections)]
    for copy in copies:
        copy.start()
    for copy in copies:
        copy.wait()


def grads_of(p, upstream, back, dense, w):
    sections, micro, rows, quarter = back.shape
    part = (micro, rows, quarter)
    return pl.pallas_call(
        grads_kernel,
        in_specs=[SCALAR] + [STAYS] * 4,
        out_specs=[STAYS] * sections,
        out_shape=[pltpu.HBM(part, BF16)] * sections,
        scratch_shapes=[
            pltpu.VMEM(part, BF16),
            pltpu.VMEM(dense.shape, BF16),
            pltpu.VMEM(w.shape, BF16),
            pltpu.VMEM((micro, sections, rows, quarter), BF16),
            pltpu.VMEM(part, F32),
            pltpu.VMEM((sections,) + part, BF16),
            pltpu.SemaphoreType.DMA((micro + 3,)),
            pltpu.SemaphoreType.DMA((sections,)),
        ],
        compiler_params=params(40),
        name="grads",
    )(p, *[in_hbm(array) for array in (upstream, back, dense, w)])


def total_kernel(parts_ref, out_hbm, out_ref, sem):
    total = parts_ref[0].astype(F32)
    for source in range(1, parts_ref.shape[0]):
        total = total + parts_ref[source].astype(F32)
    total = total.astype(BF16)
    for dest in range(out_ref.shape[0]):
        out_ref[dest] = total
    copy = pltpu.make_async_copy(out_ref, out_hbm, sem)
    copy.start()
    copy.wait()


def total_for_all(parts):
    return pl.pallas_call(
        total_kernel,
        in_specs=[WHOLE],
        out_specs=STAYS,
        out_shape=pltpu.HBM(parts.shape, BF16),
        scratch_shapes=[pltpu.VMEM(parts.shape, BF16), pltpu.SemaphoreType.DMA],
        compiler_params=params(8),
        name="router_total",
    )(parts)


def join_kernel(p_ref, *refs):
    step = pl.program_id(0)
    out_ref = refs[-1]
    for d in range(len(refs) - 1):

        @pl.when(step == d)
        def _():
            out_ref[...] = refs[d][...]


def join(p, blocks):
    n = len(blocks)
    micro, rows, quarter = blocks[0].shape
    return pl.pallas_call(
        join_kernel,
        grid_spec=pltpu.PrefetchScalarGridSpec(
            num_scalar_prefetch=1,
            grid=(n,),
            in_specs=[pl.BlockSpec((micro, rows, quarter), lambda d, p: (0, 0, 0))] * n,
            out_specs=pl.BlockSpec((micro, rows, quarter), lambda d, p: (0, 0, (p[0] - d) & (n - 1))),
        ),
        out_shape=jax.ShapeDtypeStruct((micro, rows, n * quarter), BF16),
        compiler_params=params(32),
        name="join",
    )(p, *blocks)


def turned(block, distance):
    n = lax.axis_size("pipe")
    return lax.ppermute(block, "pipe", [(i, (i + distance) % n) for i in range(n)])


def gathered(block):
    n = lax.axis_size("pipe")
    return [block] + [turned(block, n - j) for j in range(1, n)]


def on_device(normed, saved_out, expert_grads, routes, router_weight, upstream):
    sections = lax.axis_size("pipe")
    section = lax.axis_index("pipe")
    p = section.astype(jnp.int32).reshape(1)
    _, micro, rows, width = normed.shape
    tokens = micro * rows
    quarter = width // sections
    normed = normed.reshape(tokens, width)
    w = router_weight[0].T
    experts = w.shape[0]

    def part(array, j, axis):
        return lax.dynamic_slice_in_dim(array, ((section - j) % sections) * quarter, quarter, axis)

    def spread(blocks):
        return [turned(block, sections - j) if j else block for j, block in enumerate(blocks)]

    grads = in_hbm(jnp.transpose(expert_grads[0, :, 0, 0], (0, 2, 1, 3)))
    lead = lax.all_to_all(lead_pack(grads, micro - 1), "expert", 0, 0, tiled=True)
    info, near = gate_info(normed, w, jnp.transpose(routes[0], (2, 0, 1)).reshape(2, tokens), micro)
    info_all = spread([info] * sections)
    w_all = spread([part(w, j, 1) for j in range(sections)])
    late = late_blocks(p, grads, sections)
    late, info_all, w_all = lax.optimization_barrier((late, info_all, w_all))
    late = spread(late)
    info_all = jnp.stack(info_all)
    w_all = jnp.stack(w_all)
    saved = jnp.transpose(saved_out[0], (2, 0, 1, 3))
    early = [part(saved[:, : micro - 1], j, 3) for j in range(sections)]
    *early, late[1], late[2], late[3] = lax.optimization_barrier((*early, *late[1:]))
    early = spread(early)
    tail_send = tail_pack(late)
    tail_send, *early = lax.optimization_barrier((tail_send, *early))
    tail = lax.all_to_all(tail_send, "expert", 0, 0, tiled=True)
    rest = spread([part(saved[:, micro - 1 :], j, 3) for j in range(sections)])
    lead = spread(lead_combine(p, lead, near, sections))
    links = coupling(p, early, rest, w_all, info_all)
    up = part(upstream, 0, 2)
    lead, info_all, w_all, early, rest, links, up = lax.optimization_barrier(
        (lead, info_all, w_all, early, rest, links, up)
    )
    back, sent, v = tail_combine(p, tail, info_all, up, links, lead, early, rest)
    sent = lax.all_to_all(sent, "pipe", 0, 0, tiled=True)
    dense, partial = dense_terms(p, sent, v, normed, micro)

    axes = ("dp", "expert")
    partial = lax.all_to_all(partial, axes, 0, 0, tiled=True)
    outs = grads_of(p, up, back, dense, w_all)
    blocks = [turned(out, d) if d else out for d, out in enumerate(outs)]
    total = lax.all_to_all(total_for_all(partial), axes, 0, 0, tiled=True)
    total = total.astype(F32).reshape(experts // 8, width // 128, 8, 128).transpose(0, 2, 1, 3)
    router_grad = total.reshape(experts, width).T
    blocks[0] = in_hbm(blocks[0])
    return (join(p, blocks)[None], router_grad[None])


def solution(mesh):
    in_specs = (
        P("pipe", None, ("expert", "dp"), None),
        P("pipe", None, ("expert", "dp"), None, None),
        P("pipe", None, "dp", "expert", None, None, None),
        P("pipe", None, ("expert", "dp"), None),
        P("pipe", None, None),
        P(None, ("expert", "dp"), None),
    )
    out_specs = (P("pipe", None, ("expert", "dp"), None), P("pipe", None, None))
    return jax.shard_map(
        on_device, mesh=mesh, in_specs=in_specs, out_specs=out_specs, check_vma=False
    )
```
